1024 devices in a mesh: gx: 32 (over y, x, core), gy: 8 (over z_lo), gz: 4 (over z_hi).
Axes of the slice: x: 4, y: 4, z: 32 (z_hi: 4, z_lo: 8; z = z_hi * 8 + z_lo), core: 2. Of those that a mesh axis runs over, the one named last changes fastest.
Arguments:
- initial: float32 [256, 64, 512], P('gx', 'gy', 'gz'), may hold values from -6 to 6
- source: float32 [256, 64, 512], P('gx', 'gy', 'gz'), may hold values from -6 to 6
- metric: float32 [3, 256, 64, 512], P(None, 'gx', 'gy', 'gz'), may hold values from 0.005 to 0.05
- eigenvectors: float32 [3, 10, 10, 32, 8, 64], P(None, None, None, 'gx', 'gy', 'gz'), may hold values from -2 to 2
- eigenvalues: float32 [3, 10, 32, 8, 64], P(None, None, 'gx', 'gy', 'gz'), may hold values from 1 to 8
Outputs:
- solution: float32 [256, 64, 512], P('gx', 'gy', 'gz')
The draws below stay inside these ranges and needn't reach their ends.
All inputs are finite; a program needn't handle non-finite values.
Results may differ from the reference program's by a relative error of at most 0.0001.
Values sent between devices are 32-bit elements; how exact they have to be, the bound alone decides.
A program may use at most 32 MiB of HBM per device.

```python
import math
import jax
import jax.numpy as jnp
import numpy as np
from jax import lax

STEPS = 1
MX = 32
MY = 8
MZ = 64
NX = 256
NY = 64
NZ = 512


def levels(stream_key, dims, pieces, smallest, high):
    loudness, own = 1.0, jax.random.fold_in(stream_key, 6)
    for axis_at, parts in pieces:
        steps = jnp.exp(jax.random.uniform(jax.random.fold_in(own, axis_at), (parts,), jnp.float32, smallest / len(pieces), high / len(pieces)))
        loudness = loudness * jnp.repeat(steps, dims[axis_at] // parts).reshape([-1 if axis == axis_at else 1 for axis in range(len(dims))])
    return loudness


def scatter_about(rng, shape, width, bound, shards=(), held_as=jnp.bfloat16):
    values = jax.random.normal(rng, shape, jnp.float32) * width
    if len(shards) > 0:
        values = levels(rng, shape, shards, -0.22, 0.18) * values
    return jnp.clip(values, min=-bound, max=bound).astype(held_as)


def setup_inputs(seed: int = 0) -> dict:
    seeds = jax.random.split(jax.random.key(seed), 6)
    return {
        "initial": scatter_about(seeds[0], (NX, NY, NZ), 1.0, 6.0, ((0, 32), (1, 8), (2, 4)), jnp.float32),
        "source": scatter_about(seeds[1], (NX, NY, NZ), 1.0, 6.0, ((0, 32), (1, 8), (2, 4)), jnp.float32),
        "metric": jnp.clip(jnp.exp(math.log(0.05) - 2.3025851 * jax.random.uniform(seeds[2], (3, NX, NY, NZ), jnp.float32) ** levels(seeds[2], (3, NX, NY, NZ), ((1, 32), (2, 8), (3, 4)), -0.2, 0.2)), 0.005, 0.05),
        "eigenvectors": scatter_about(seeds[3], (3, 10, 10, MX, MY, MZ), 10 ** -0.5, 2.0, ((3, 32), (4, 8), (5, 4)), jnp.float32),
        "eigenvalues": jnp.clip(jnp.exp(math.log(8.0) - 2.0794415 * jax.random.uniform(seeds[4], (3, 10, MX, MY, MZ), jnp.float32) ** levels(seeds[4], (3, 10, MX, MY, MZ), ((2, 32), (3, 8), (4, 4)), -0.2, 0.2)), 1.0, 8.0),
    }


gll_points = np.array([-1.0, -0.8717401485096066, -0.5917001814331423, -0.2092992179024789, 0.2092992179024789, 0.5917001814331423, 0.8717401485096066, 1.0])


def derivative_table():
    number = gll_points.shape[0]
    products = np.array([np.prod([gll_points[row_index] - gll_points[other] for other in range(number) if other != row_index]) for row_index in range(number)])
    matrix_out = np.zeros((number, number))
    for row_index in range(number):
        for col_index in range(number):
            if row_index != col_index:
                matrix_out[row_index, col_index] = products[row_index] / products[col_index] / (gll_points[row_index] - gll_points[col_index])
        matrix_out[row_index, row_index] = -np.sum(matrix_out[row_index])
    return matrix_out


def apply_along(values, matrix, direction):
    block_size = matrix.shape[1]
    old_shape = values.shape
    pieces_shape = old_shape[:direction] + (old_shape[direction] // block_size, block_size) + old_shape[direction + 1:]
    result = jnp.tensordot(values.reshape(pieces_shape), matrix, axes=((direction + 1,), (1,)), precision=lax.Precision.HIGHEST)
    result = jnp.moveaxis(result, -1, direction + 1)
    return result.reshape(old_shape[:direction] + (old_shape[direction] // block_size * matrix.shape[0],) + old_shape[direction + 1:])


def apply_operator(values, metric):
    deriv_table = jnp.asarray(derivative_table(), jnp.float32)
    summed = jnp.zeros_like(values)
    for direction in range(3):
        gradient = apply_along(values, deriv_table, direction)
        summed = summed + apply_along(metric[direction] * gradient, deriv_table.T, direction)
    return summed


def assemble(padded, offset):
    result = padded
    for direction in range(3):
        length = result.shape[direction]
        view_shape = [1, 1, 1]
        view_shape[direction] = length
        node_index = ((jnp.arange(length) - offset) % 8).reshape(view_shape)
        edge_zero = jnp.zeros_like(lax.slice_in_dim(result, 0, 1, axis=direction))
        upward = jnp.concatenate([lax.slice_in_dim(result, 1, length, axis=direction), edge_zero], axis=direction)
        downward = jnp.concatenate([edge_zero, lax.slice_in_dim(result, 0, length - 1, axis=direction)], axis=direction)
        result = result + jnp.where(node_index == 7, upward, 0.0) + jnp.where(node_index == 0, downward, 0.0)
    return result


def extend_axis(padded, direction):
    shifted = jnp.moveaxis(padded, direction, 0)
    blocks = (shifted.shape[0] - 4) // 8
    trailing = shifted.shape[1:]
    middle = shifted[2:-2].reshape((blocks, 8) + trailing)
    lowest = shifted[0:8 * blocks:8][:, None]
    beyond = shifted[11::8][:, None]
    joined = jnp.concatenate([lowest, middle, beyond], axis=1).reshape((blocks * 10,) + trailing)
    return jnp.moveaxis(joined, 0, direction)


def widen(padded):
    return extend_axis(extend_axis(extend_axis(padded, 0), 1), 2)


def fast_solve(extended, eigenvectors, eigenvalues):
    count_x, count_y, count_z = eigenvectors.shape[3:]
    precise = lax.Precision.HIGHEST
    spectral = extended.reshape(count_x, 10, count_y, 10, count_z, 10)
    spectral = jnp.einsum('apxyz,xaybzc->xpybzc', eigenvectors[0], spectral, precision=precise)
    spectral = jnp.einsum('bqxyz,xpybzc->xpyqzc', eigenvectors[1], spectral, precision=precise)
    spectral = jnp.einsum('csxyz,xpyqzc->xpyqzs', eigenvectors[2], spectral, precision=precise)
    rate_x = jnp.transpose(eigenvalues[0], (1, 0, 2, 3))[:, :, :, None, :, None]
    rate_y = jnp.transpose(eigenvalues[1], (1, 2, 0, 3))[:, None, :, :, :, None]
    rate_z = jnp.transpose(eigenvalues[2], (1, 2, 3, 0))[:, None, :, None, :, :]
    spectral = spectral / (rate_x + rate_y + rate_z)
    spectral = jnp.einsum('csxyz,xpyqzs->xpyqzc', eigenvectors[2], spectral, precision=precise)
    spectral = jnp.einsum('bqxyz,xpyqzc->xpybzc', eigenvectors[1], spectral, precision=precise)
    spectral = jnp.einsum('apxyz,xpybzc->xaybzc', eigenvectors[0], spectral, precision=precise)
    return spectral.reshape(count_x * 10, count_y * 10, count_z * 10)


def return_axis(padded, direction):
    shifted = jnp.moveaxis(padded, direction, 0)
    blocks = (shifted.shape[0] - 4) // 10
    trailing = shifted.shape[1:]
    owned = shifted[2:-2].reshape((blocks, 10) + trailing)[:, 1:9]
    before = shifted[0:10 * blocks].reshape((blocks, 10) + trailing)[:, 0:2]
    following = shifted[4:].reshape((blocks, 10) + trailing)[:, 8:10]
    middle = jnp.zeros((blocks, 4) + trailing, shifted.dtype)
    summed = owned + jnp.concatenate([before, middle, following], axis=1)
    return jnp.moveaxis(summed.reshape((blocks * 8,) + trailing), 0, direction)


def reference(initial, source, metric, eigenvectors, eigenvalues):
    solution = initial
    for smooth_step in range(STEPS):
        local_res = source - apply_operator(solution, metric)
        widened = assemble(jnp.pad(local_res, 2), 2)
        extended = widen(widened)
        corrected = fast_solve(extended, eigenvectors, eigenvalues)
        padded = jnp.pad(corrected, 2)
        correction = return_axis(return_axis(return_axis(padded, 0), 1), 2)
        solution = solution + correction
    return solution
```

```python
import functools

import jax
import jax.numpy as jnp
import numpy as np
from jax import lax
from jax.experimental import pallas as pl
from jax.experimental.pallas import tpu as pltpu
from jax.sharding import PartitionSpec as P

MESH = pl.DeviceIdType.MESH
F32 = jnp.float32
BF16 = jnp.bfloat16

gll_points = np.array(
    [
        -1.0,
        -0.8717401485096066,
        -0.5917001814331423,
        -0.2092992179024789,
        0.2092992179024789,
        0.5917001814331423,
        0.8717401485096066,
        1.0,
    ]
)

DIRS = [(-1, 0), (1, 0), (0, -1), (0, 1), (-1, -1), (-1, 1), (1, -1), (1, 1)]
OPP = [1, 0, 3, 2, 7, 6, 5, 4]
OYF, OYB, OZ, OL, ROWS = 160, 320, 480, 720, 768


def derivative_table():
    number = gll_points.shape[0]
    products = np.array(
        [
            np.prod([gll_points[i] - gll_points[k] for k in range(number) if k != i])
            for i in range(number)
        ]
    )
    table = np.zeros((number, number))
    for i in range(number):
        for j in range(number):
            if i != j:
                table[i, j] = products[i] / products[j] / (gll_points[i] - gll_points[j])
        table[i, i] = -np.sum(table[i])
    return table


def operator_tables():
    table = derivative_table().astype(np.float32)
    eye = np.eye(8, dtype=np.float32)
    left = np.concatenate([np.kron(table, eye), np.kron(eye, table)], axis=0)
    left = np.concatenate([left, np.zeros((128, 64), np.float32)], axis=1)
    left_t = np.ascontiguousarray(left.T[:64])
    right = np.kron(np.eye(16, dtype=np.float32), table.T)
    full = np.concatenate([left, left_t, right, right.T], axis=0)
    high = full.astype(jnp.bfloat16)
    low = (full - high.astype(np.float32)).astype(jnp.bfloat16)
    return np.stack([high, low])


def dot(a, b, dims=((1,), (0,))):
    return lax.dot_general(a, b, (dims, ((), ())), preferred_element_type=F32)


def halves(value):
    high = value.astype(BF16)
    return high, (value - high.astype(F32)).astype(BF16)


def thirds(value):
    high = value.astype(BF16)
    rest = value - high.astype(F32)
    mid = rest.astype(BF16)
    return high, mid, (rest - mid.astype(F32)).astype(BF16)


def dot3(a, b, dims=((1,), (0,))):
    return dot(a[0], b[0], dims) + (dot(a[1], b[0], dims) + dot(a[0], b[1], dims))


def lanes(group):
    lane = lax.broadcasted_iota(jnp.int32, (1, 128), 1)
    if group == 0:
        return lane & 15, lane >> 4
    inside, low, high = lane < 32, lane < 42, lane < 52
    element = jnp.where(inside, lane & 15, jnp.where(low, -1, jnp.where(high, 16, 99)))
    mode = jnp.where(
        inside, 8 + (lane >> 4), jnp.where(low, lane - 32, jnp.where(high, lane - 42, 99))
    )
    return element, mode


def kernel(
    nx, ny, nz,
    u_h, f_h, m_h, eig_h, lam_h, cst_h, out_ref,
    u_v, f_v, m_v, cst_v, ex, eyf, eyb, ez, el, in_sem,
    send_x, send_y, send_d, recv_x, recv_y, recv_d, near_send, near_recv,
    fe_send, fe_recv, fx_send, fx_recv, far_send, far_recv, ready,
    xs, xc, cm, cxb, inv, wh, wl, zs,
):
    ix, iy, iz = lax.axis_index("gx"), lax.axis_index("gy"), lax.axis_index("gz")

    first = [(u_h, u_v), (cst_h, cst_v), (m_h, m_v), (f_h, f_v)]
    second = [
        (eig_h.at[0, 1:9, :, 0, 0], ex.at[0:8, 0:10]),
        (eig_h.at[0, 0, :, 0, 0], ex.at[8, 0:10]),
        (eig_h.at[0, 9, :, 0, 0], ex.at[9, 0:10]),
        (eig_h.at[1, 1:9, :, 0, 0], eyf.at[0:8, 0:10]),
        (eig_h.at[1, 0, :, 0, 0], eyf.at[8, 0:10]),
        (eig_h.at[1, 9, :, 0, 0], eyf.at[9, 0:10]),
        (lam_h.at[:, :, 0, 0], el.at[:, 0:10]),
    ]
    for row, pos in enumerate([1, 2, 3, 4, 5, 6, 7, 8, 0, 9]):
        second.append((eig_h.at[1, pos, :, 0, 0], eyb.at[:, row]))
    for row, pos in enumerate([1, 2, 3, 4, 5, 6, 7, 8]):
        second.append((eig_h.at[2, pos, :, 0, 0], ez.at[:, row]))
    for row, pos in [(14, 0), (15, 1), (16, 8), (17, 9)]:
        second.append((eig_h.at[2, pos, :, 0, 0], ez.at[:, row]))
    loads = [
        pltpu.make_async_copy(src, dst, in_sem.at[i])
        for i, (src, dst) in enumerate(first + second)
    ]
    for load in loads:
        load.start()

    recv_x[...] = jnp.zeros_like(recv_x)
    recv_y[...] = jnp.zeros_like(recv_y)
    recv_d[...] = jnp.zeros_like(recv_d)
    fe_recv[...] = jnp.zeros_like(fe_recv)
    fx_recv[...] = jnp.zeros_like(fx_recv)

    half = ny // 2
    spot = iz * ny + iy
    above, below = spot + half, spot - half
    has_above, has_below = above < nz * ny, below >= 0
    below_safe = jnp.maximum(below, 0)
    to_above = (ix, above % ny, above // ny)
    to_below = (ix, below_safe % ny, below_safe // ny)
    has_next, has_prev = iz < nz - 1, iz > 0
    to_next, to_prev = (ix, iy, iz + 1), (ix, iy, iz - 1)
    near, target = [], []
    for dx, dy in DIRS:
        ok = None
        for cond in (
            [ix > 0] * (dx < 0) + [ix < nx - 1] * (dx > 0)
            + [iy > 0] * (dy < 0) + [iy < ny - 1] * (dy > 0)
        ):
            ok = cond if ok is None else ok & cond
        near.append(ok)
        target.append((ix + dx, iy + dy, iz))
    barrier = pltpu.get_barrier_semaphore()
    count = jnp.int32(0)
    for ok, device in list(zip(near, target)) + [(has_above, to_above), (has_below, to_below)]:
        @pl.when(ok)
        def _(device=device):
            pl.semaphore_signal(barrier, 1, device_id=device, device_id_type=MESH)
        count = count + ok.astype(jnp.int32)

    ex[:, 10:16, :] = jnp.zeros((10, 6, 16), F32)
    eyf[:, 10:16, :] = jnp.zeros((10, 6, 16), F32)
    eyb[:, 10:16, :] = jnp.zeros((10, 6, 16), F32)
    ez[:, 8:14, :] = jnp.zeros((10, 6, 16), F32)
    ez[:, 18:24, :] = jnp.zeros((10, 6, 16), F32)
    el[:, 10:16, :] = jnp.zeros((3, 6, 16), F32)
    xs[:, 10:16, :] = jnp.zeros((10, 6, 128), F32)
    xc[96:128, :] = jnp.zeros((32, 128), F32)

    for load in loads[:4]:
        load.wait()
    field = halves(u_v[...].reshape(64, 128))
    left = cst_v[0, 0:128, 0:64], cst_v[1, 0:128, 0:64]
    left_t = cst_v[0, 128:192], cst_v[1, 128:192]
    right = cst_v[0, 192:320], cst_v[1, 192:320]
    right_t = cst_v[0, 320:448], cst_v[1, 320:448]
    flux = dot3(left, field) * m_v[0:2].reshape(128, 128)
    flux_z = dot3(field, right) * m_v[2].reshape(64, 128)
    applied = dot3(left_t, halves(flux)) + dot3(halves(flux_z), right_t)
    res = f_v[...] - applied.reshape(8, 8, 128)

    def recv_of(turn, k):
        if k < 2:
            return recv_x.at[turn, k]
        return recv_y.at[turn, k - 2] if k < 4 else recv_d.at[turn, k - 4]

    def send_of(turn, k):
        if k < 2:
            return send_x.at[turn, k]
        return send_y.at[turn, k - 2] if k < 4 else send_d.at[turn, k - 4]

    def outgoing(turn, k):
        return pltpu.make_async_remote_copy(
            src_ref=send_of(turn, k),
            dst_ref=recv_of(turn, OPP[k]),
            send_sem=near_send.at[turn, k],
            recv_sem=near_recv.at[turn, OPP[k]],
            device_id=target[k],
            device_id_type=MESH,
        )

    def incoming(turn, k):
        return pltpu.make_async_remote_copy(
            src_ref=send_of(turn, k),
            dst_ref=recv_of(turn, k),
            send_sem=near_send.at[turn, k],
            recv_sem=near_recv.at[turn, k],
            device_id=target[k],
            device_id_type=MESH,
        )

    ORDER = [4, 5, 6, 7, 0, 1, 2, 3]

    def send_near(turn):
        for k in ORDER:
            @pl.when(near[k])
            def _(k=k):
                outgoing(turn, k).start()

    def wait_near(turn):
        for k in ORDER:
            @pl.when(near[k])
            def _(k=k):
                incoming(turn, k).wait_recv()

    def pack(turn, value, low, high):
        for side, rows in enumerate((low, high)):
            for j, row in enumerate(rows):
                send_x[turn, side, j] = value[row, 0:8]
                send_y[turn, side, :, j : j + 1, :] = value[0:8, row : row + 1]
        for k in range(4, 8):
            rows_x = low if DIRS[k][0] < 0 else high
            rows_y = low if DIRS[k][1] < 0 else high
            for i, row_x in enumerate(rows_x):
                for j, row_y in enumerate(rows_y):
                    send_d[turn, k - 4, i, j : j + 1, :] = value[row_x, row_y : row_y + 1]

    pack(0, res, (0, 1), (6, 7))
    pl.semaphore_wait(barrier, count)
    send_near(0)

    @pl.when(has_above & has_below)
    def _():
        pl.semaphore_signal(ready.at[0], 1, device_id=to_below, device_id_type=MESH)
        pl.semaphore_signal(ready.at[1], 1, device_id=to_above, device_id_type=MESH)

    for load in loads[4:]:
        load.wait()
    eigen = jnp.concatenate(
        [
            ex[...].reshape(160, 16),
            eyf[...].reshape(160, 16),
            eyb[...].reshape(160, 16),
            ez[...].reshape(240, 16),
            el[...].reshape(48, 16),
        ],
        axis=0,
    )
    parts = thirds(eigen)
    wanted = lax.broadcasted_iota(jnp.int32, (8, 16), 0) * 15
    picks = jnp.where(lax.broadcasted_iota(jnp.int32, (8, 16), 1) == wanted, 1.0, 0.0).astype(BF16)
    ends = sum(dot(picks, part, ((1,), (1,))) for part in parts)
    fe_send[0] = ends[0:1]
    fe_send[1] = ends[1:2]

    def prepare(g):
        element, mode = lanes(g)
        spread = jnp.where(
            lax.broadcasted_iota(jnp.int32, (16, 128), 0) == element, 1.0, 0.0
        ).astype(BF16)
        table = sum(dot(part, spread) for part in parts)
        if g == 1:
            row = lax.broadcasted_iota(jnp.int32, (8, ROWS), 0)
            other = jnp.where(row == 0, fe_recv[0], jnp.where(row == 1, fe_recv[1], 0.0))
            far_row = lax.broadcasted_iota(jnp.int32, (8, 128), 0)
            spread_far = jnp.where(
                ((far_row == 0) & (element == -1)) | ((far_row == 1) & (element == 16)), 1.0, 0.0
            ).astype(BF16)
            far = sum(dot(part, spread_far, ((0,), (0,))) for part in thirds(other))
            table = table + far
        cm[g] = table
        for r in range(100):
            at = 16 * (r // 10) + r % 10
            cxb[g, r // 10, r % 10] = jnp.broadcast_to(cm[g, at : at + 1, :], (8, 128))
        tiles = jnp.zeros((24, 128), F32)
        for s in range(10):
            tiles = tiles + jnp.where(mode == s, cm[g, OZ + 24 * s : OZ + 24 * s + 24, :], 0.0)
        inner, lower, upper = tiles[0:8], tiles[8:16], tiles[16:24]
        columns = []
        for e in list(range(16)) + [-2, -1, 16, 17]:
            columns.append(
                jnp.where(
                    element == e,
                    inner,
                    jnp.where(element == e + 1, lower, jnp.where(element == e - 1, upper, 0.0)),
                )
            )
        wh[g], wl[g] = halves(jnp.concatenate(columns, axis=0))
        rate_z = jnp.where(
            lax.broadcasted_iota(jnp.int32, (16, 128), 0) == mode, cm[g, OL + 32 : OL + 48, :], 0.0
        ).sum(axis=0, keepdims=True)
        rate_yz = cm[g, OL + 16 : OL + 32, :] + rate_z
        for p in range(10):
            rate = rate_yz + cm[g, OL + p : OL + p + 1, :]
            some = rate > 0.0
            inv[g, p] = jnp.where(some, 1.0 / jnp.where(some, rate, 1.0), 0.0)

    def far_copy(kind, way, arriving):
        if kind == 0:
            src, dst = fe_send.at[1 - way], fe_recv.at[way]
        else:
            src, dst = fx_send.at[way], fx_recv.at[way]
        return pltpu.make_async_remote_copy(
            src_ref=src,
            dst_ref=dst,
            send_sem=far_send.at[kind, way],
            recv_sem=far_recv.at[kind, way],
            device_id=to_next if (way == 0) != arriving else to_prev,
            device_id_type=MESH,
        )

    prepare(0)

    @pl.when(has_next)
    def _():
        pl.semaphore_wait(ready.at[0], 1)
        far_copy(0, 0, False).start()

    @pl.when(has_prev)
    def _():
        pl.semaphore_wait(ready.at[1], 1)
        far_copy(0, 1, False).start()

    wait_near(0)

    def join(own, prev, after):
        return jnp.concatenate(
            [own[0:1] + prev[1:2], own[1:7], own[7:8] + after[0:1], prev[0:1], after[1:2]], axis=0
        )

    xs[:, 0:8, :] = join(res, recv_x[0, 0], recv_x[0, 1])
    before = join(recv_y[0, 0], recv_d[0, 0], recv_d[0, 2])
    behind = join(recv_y[0, 1], recv_d[0, 1], recv_d[0, 3])
    xs[:, 0:1, :] = xs[:, 0:1, :] + before[:, 1:2]
    xs[:, 7:8, :] = xs[:, 7:8, :] + behind[:, 0:1]
    xs[:, 8:9, :] = before[:, 0:1]
    xs[:, 9:10, :] = behind[:, 1:2]
    xc[0:80, :] = xs[:, 0:8, :].reshape(80, 128)
    for a in range(10):
        xc[80 + 2 * a : 82 + 2 * a, :] = xs[a, 8:10, :]
    turned = xc[...].T
    fx_send[0] = turned[112:128]
    fx_send[1] = turned[0:16]

    @pl.when(has_next)
    def _():
        far_copy(1, 0, False).start()

    @pl.when(has_prev)
    def _():
        far_copy(1, 1, False).start()

    nodes = halves(xs[...].reshape(160, 128))

    def to_modes(g):
        zs[g] = dot3(nodes, (wh[g, 0:128], wl[g, 0:128])).reshape(10, 16, 128)

    to_modes(0)

    @pl.when(has_next)
    def _():
        far_copy(0, 1, True).wait_recv()

    @pl.when(has_prev)
    def _():
        far_copy(0, 0, True).wait_recv()

    prepare(1)
    to_modes(1)

    @pl.when(has_next)
    def _():
        far_copy(1, 1, True).wait_recv()

    @pl.when(has_prev)
    def _():
        far_copy(1, 0, True).wait_recv()

    beyond = halves(fx_recv[...].reshape(32, 128))

    def solve(g):
        more = dot3(beyond, (wh[g, 128:160], wl[g, 128:160]), ((0,), (0,)))
        zs[g, :, 0:8, :] = zs[g, :, 0:8, :] + more[0:80].reshape(10, 8, 128)
        for a in range(10):
            zs[g, a, 8:10, :] = zs[g, a, 8:10, :] + more[80 + 2 * a : 82 + 2 * a]
        value = zs[g].reshape(10, 2, 8, 128)
        total = None
        for a in range(10):
            term = cxb[g, a][:, None] * value[a][None]
            total = term if total is None else total + term
        value, total = total, None
        for b in range(10):
            row = value[:, b // 8, b % 8 : b % 8 + 1, :][:, None]
            pick = cm[g, OYF + 16 * b : OYF + 16 * b + 16, :].reshape(1, 2, 8, 128)
            term = pick * row
            total = term if total is None else total + term
        value, total = total * inv[g].reshape(10, 2, 8, 128), None
        for q in range(10):
            row = value[:, q // 8, q % 8 : q % 8 + 1, :][:, None]
            pick = cm[g, OYB + 16 * q : OYB + 16 * q + 16, :].reshape(1, 2, 8, 128)
            term = pick * row
            total = term if total is None else total + term
        value, total = total, None
        for p in range(10):
            term = cxb[g, :, p][:, None] * value[p][None]
            total = term if total is None else total + term
        return dot3(
            halves(total.reshape(160, 128)), (wh[g, 0:128], wl[g, 0:128]), ((1,), (1,))
        )

    found = (solve(0) + solve(1)).reshape(10, 16, 128)
    pack(1, found, (8, 0), (7, 9))
    send_near(1)
    wait_near(1)

    def gather(own, prev, after):
        return jnp.concatenate([own[0:2] + prev, own[2:6], own[6:8] + after], axis=0)

    out_ref[...] = gather(found[0:8, 0:8], recv_x[1, 0], recv_x[1, 1])
    out_ref[:, 0:2, :] = out_ref[:, 0:2, :] + gather(recv_y[1, 0], recv_d[1, 0], recv_d[1, 2])
    out_ref[:, 6:8, :] = out_ref[:, 6:8, :] + gather(recv_y[1, 1], recv_d[1, 1], recv_d[1, 3])

    for turn in range(2):
        for k in range(8):
            @pl.when(near[k])
            def _(turn=turn, k=k):
                outgoing(turn, k).wait_send()

    for kind in range(2):
        @pl.when(has_next)
        def _(kind=kind):
            far_copy(kind, 0, False).wait_send()

        @pl.when(has_prev)
        def _(kind=kind):
            far_copy(kind, 1, False).wait_send()


def solution(mesh):
    nx, ny, nz = mesh.shape["gx"], mesh.shape["gy"], mesh.shape["gz"]

    def body(initial, source, metric, eigenvectors, eigenvalues):
        hbm = pl.BlockSpec(memory_space=pl.ANY)
        vmem = pltpu.VMEM
        correction = pl.pallas_call(
            functools.partial(kernel, nx, ny, nz),
            out_shape=jax.ShapeDtypeStruct((8, 8, 128), F32),
            in_specs=[hbm] * 6,
            out_specs=pl.BlockSpec(memory_space=vmem),
            scratch_shapes=[
                vmem((8, 8, 128), F32),
                vmem((8, 8, 128), F32),
                vmem((3, 8, 8, 128), F32),
                vmem((2, 448, 128), BF16),
                vmem((10, 16, 16), F32),
                vmem((10, 16, 16), F32),
                vmem((10, 16, 16), F32),
                vmem((10, 24, 16), F32),
                vmem((3, 16, 16), F32),
                pltpu.SemaphoreType.DMA((33,)),
                vmem((2, 2, 2, 8, 128), F32),
                vmem((2, 2, 8, 2, 128), F32),
                vmem((2, 4, 2, 2, 128), F32),
                vmem((2, 2, 2, 8, 128), F32),
                vmem((2, 2, 8, 2, 128), F32),
                vmem((2, 4, 2, 2, 128), F32),
                pltpu.SemaphoreType.DMA((2, 8)),
                pltpu.SemaphoreType.DMA((2, 8)),
                vmem((2, 1, ROWS), F32),
                vmem((2, 1, ROWS), F32),
                vmem((2, 16, 128), F32),
                vmem((2, 16, 128), F32),
                pltpu.SemaphoreType.DMA((2, 2)),
                pltpu.SemaphoreType.DMA((2, 2)),
                pltpu.SemaphoreType.REGULAR((2,)),
                vmem((10, 16, 128), F32),
                vmem((128, 128), F32),
                vmem((2, ROWS, 128), F32),
                vmem((2, 10, 10, 8, 128), F32),
                vmem((2, 10, 16, 128), F32),
                vmem((2, 160, 128), BF16),
                vmem((2, 160, 128), BF16),
                vmem((2, 10, 16, 128), F32),
            ],
            compiler_params=pltpu.CompilerParams(collective_id=0, has_side_effects=True),
        )(
            initial,
            source,
            metric,
            eigenvectors,
            eigenvalues,
            jnp.asarray(operator_tables()),
        )
        return initial + correction

    placed = (
        P("gx", "gy", "gz"),
        P("gx", "gy", "gz"),
        P(None, "gx", "gy", "gz"),
        P(None, None, None, "gx", "gy", "gz"),
        P(None, None, "gx", "gy", "gz"),
    )
    return jax.shard_map(
        body, mesh=mesh, in_specs=placed, out_specs=P("gx", "gy", "gz"), check_vma=False
    )
```

```python
import functools

import jax
import jax.numpy as jnp
import numpy as np
from jax import lax
from jax.experimental import pallas as pl
from jax.experimental.pallas import tpu as pltpu
from jax.sharding import PartitionSpec as P

MESH = pl.DeviceIdType.MESH
F32 = jnp.float32
BF16 = jnp.bfloat16

gll_points = np.array(
    [
        -1.0,
        -0.8717401485096066,
        -0.5917001814331423,
        -0.2092992179024789,
        0.2092992179024789,
        0.5917001814331423,
        0.8717401485096066,
        1.0,
    ]
)

DIRS = [(-1, 0), (1, 0), (0, -1), (0, 1), (-1, -1), (-1, 1), (1, -1), (1, 1)]
OPP = [1, 0, 3, 2, 7, 6, 5, 4]
OYF, OYB, OZ, OL, ROWS = 160, 320, 480, 720, 768


def derivative_table():
    number = gll_points.shape[0]
    products = np.array(
        [
            np.prod([gll_points[i] - gll_points[k] for k in range(number) if k != i])
            for i in range(number)
        ]
    )
    table = np.zeros((number, number))
    for i in range(number):
        for j in range(number):
            if i != j:
                table[i, j] = products[i] / products[j] / (gll_points[i] - gll_points[j])
        table[i, i] = -np.sum(table[i])
    return table


def operator_tables():
    table = derivative_table().astype(np.float32)
    eye = np.eye(8, dtype=np.float32)
    left = np.concatenate([np.kron(table, eye), np.kron(eye, table)], axis=0)
    left = np.concatenate([left, np.zeros((128, 64), np.float32)], axis=1)
    left_t = np.ascontiguousarray(left.T[:64])
    right = np.kron(np.eye(16, dtype=np.float32), table.T)
    full = np.concatenate([left, left_t, right, right.T], axis=0)
    high = full.astype(jnp.bfloat16)
    low = (full - high.astype(np.float32)).astype(jnp.bfloat16)
    return np.stack([high, low])


def dot(a, b, dims=((1,), (0,))):
    return lax.dot_general(a, b, (dims, ((), ())), preferred_element_type=F32)


def halves(value):
    high = value.astype(BF16)
    return high, (value - high.astype(F32)).astype(BF16)


def thirds(value):
    high = value.astype(BF16)
    rest = value - high.astype(F32)
    mid = rest.astype(BF16)
    return high, mid, (rest - mid.astype(F32)).astype(BF16)


def dot3(a, b, dims=((1,), (0,))):
    return dot(a[0], b[0], dims) + (dot(a[1], b[0], dims) + dot(a[0], b[1], dims))


def lanes(group):
    lane = lax.broadcasted_iota(jnp.int32, (1, 128), 1)
    if group == 0:
        return lane & 15, lane >> 4
    inside, low, high = lane < 32, lane < 42, lane < 52
    element = jnp.where(inside, lane & 15, jnp.where(low, -1, jnp.where(high, 16, 99)))
    mode = jnp.where(
        inside, 8 + (lane >> 4), jnp.where(low, lane - 32, jnp.where(high, lane - 42, 99))
    )
    return element, mode


def kernel(
    nx, ny, nz,
    u_h, f_h, m_h, eig_h, lam_h, cst_h, out_ref,
    u_v, f_v, m_v, cst_v, ex, eyf, eyb, ez, el, in_sem,
    send_x, send_y, send_d, recv_x, recv_y, recv_d, near_send, near_recv,
    fe_send, fe_recv, fx_send, fx_recv, far_send, far_recv, ready, pe, px, side_send, side_recv,
    xs, xc, cm, cxb, inv, wh, wl, zs,
):
    ix, iy, iz = lax.axis_index("gx"), lax.axis_index("gy"), lax.axis_index("gz")

    first = [(u_h, u_v), (cst_h, cst_v), (m_h, m_v), (f_h, f_v)]
    second = [
        (eig_h.at[0, 1:9, :, 0, 0], ex.at[0:8, 0:10]),
        (eig_h.at[0, 0, :, 0, 0], ex.at[8, 0:10]),
        (eig_h.at[0, 9, :, 0, 0], ex.at[9, 0:10]),
        (eig_h.at[1, 1:9, :, 0, 0], eyf.at[0:8, 0:10]),
        (eig_h.at[1, 0, :, 0, 0], eyf.at[8, 0:10]),
        (eig_h.at[1, 9, :, 0, 0], eyf.at[9, 0:10]),
        (lam_h.at[:, :, 0, 0], el.at[:, 0:10]),
    ]
    for row, pos in enumerate([1, 2, 3, 4, 5, 6, 7, 8, 0, 9]):
        second.append((eig_h.at[1, pos, :, 0, 0], eyb.at[:, row]))
    for row, pos in enumerate([1, 2, 3, 4, 5, 6, 7, 8]):
        second.append((eig_h.at[2, pos, :, 0, 0], ez.at[:, row]))
    for row, pos in [(14, 0), (15, 1), (16, 8), (17, 9)]:
        second.append((eig_h.at[2, pos, :, 0, 0], ez.at[:, row]))
    loads = [
        pltpu.make_async_copy(src, dst, in_sem.at[i])
        for i, (src, dst) in enumerate(first + second)
    ]
    for load in loads:
        load.start()

    recv_x[...] = jnp.zeros_like(recv_x)
    recv_y[...] = jnp.zeros_like(recv_y)
    recv_d[...] = jnp.zeros_like(recv_d)
    fe_recv[...] = jnp.zeros_like(fe_recv)
    fx_recv[...] = jnp.zeros_like(fx_recv)

    has_next, has_prev = iz < nz - 1, iz > 0
    to_next, to_prev = (ix, iy, iz + 1), (ix, iy, iz - 1)
    detour = nx > 1 and nz > 1
    in_line = (ix == 0) & (iy == 0)
    origin = in_line & (iz == 0) & detour
    after_origin = in_line & (iz == 1) & detour
    helper = (ix == 1) & (iy == 0) & (iz == 0) & detour
    near, target = [], []
    for dx, dy in DIRS:
        ok = None
        for cond in (
            [ix > 0] * (dx < 0) + [ix < nx - 1] * (dx > 0)
            + [iy > 0] * (dy < 0) + [iy < ny - 1] * (dy > 0)
        ):
            ok = cond if ok is None else ok & cond
        near.append(ok)
        target.append((ix + dx, iy + dy, iz))
    barrier = pltpu.get_barrier_semaphore()
    count = jnp.int32(0)
    greeted = list(zip(near, target)) + [
        (has_next & ~origin, to_next), (helper, (0, 0, 1)), (after_origin, (0, 0, 0))
    ]
    for ok, device in greeted:
        @pl.when(ok)
        def _(device=device):
            pl.semaphore_signal(barrier, 1, device_id=device, device_id_type=MESH)
    count = jnp.int32(0)
    for ok in near + [has_prev, origin]:
        count = count + ok.astype(jnp.int32)

    ex[:, 10:16, :] = jnp.zeros((10, 6, 16), F32)
    eyf[:, 10:16, :] = jnp.zeros((10, 6, 16), F32)
    eyb[:, 10:16, :] = jnp.zeros((10, 6, 16), F32)
    ez[:, 8:14, :] = jnp.zeros((10, 6, 16), F32)
    ez[:, 18:24, :] = jnp.zeros((10, 6, 16), F32)
    el[:, 10:16, :] = jnp.zeros((3, 6, 16), F32)
    xs[:, 10:16, :] = jnp.zeros((10, 6, 128), F32)
    xc[96:128, :] = jnp.zeros((32, 128), F32)

    for load in loads[:4]:
        load.wait()
    field = halves(u_v[...].reshape(64, 128))
    left = cst_v[0, 0:128, 0:64], cst_v[1, 0:128, 0:64]
    left_t = cst_v[0, 128:192], cst_v[1, 128:192]
    right = cst_v[0, 192:320], cst_v[1, 192:320]
    right_t = cst_v[0, 320:448], cst_v[1, 320:448]
    flux = dot3(left, field) * m_v[0:2].reshape(128, 128)
    flux_z = dot3(field, right) * m_v[2].reshape(64, 128)
    applied = dot3(left_t, halves(flux)) + dot3(halves(flux_z), right_t)
    res = f_v[...] - applied.reshape(8, 8, 128)

    def recv_of(turn, k):
        if k < 2:
            return recv_x.at[turn, k]
        return recv_y.at[turn, k - 2] if k < 4 else recv_d.at[turn, k - 4]

    def send_of(turn, k):
        if k < 2:
            return send_x.at[turn, k]
        return send_y.at[turn, k - 2] if k < 4 else send_d.at[turn, k - 4]

    def outgoing(turn, k):
        return pltpu.make_async_remote_copy(
            src_ref=send_of(turn, k),
            dst_ref=recv_of(turn, OPP[k]),
            send_sem=near_send.at[turn, k],
            recv_sem=near_recv.at[turn, OPP[k]],
            device_id=target[k],
            device_id_type=MESH,
        )

    def incoming(turn, k):
        return pltpu.make_async_remote_copy(
            src_ref=send_of(turn, k),
            dst_ref=recv_of(turn, k),
            send_sem=near_send.at[turn, k],
            recv_sem=near_recv.at[turn, k],
            device_id=target[k],
            device_id_type=MESH,
        )

    ORDER = [4, 5, 6, 7, 0, 1, 2, 3]

    def send_near(turn):
        for k in ORDER:
            @pl.when(near[k])
            def _(k=k):
                outgoing(turn, k).start()

    def wait_near(turn):
        for k in ORDER:
            @pl.when(near[k])
            def _(k=k):
                incoming(turn, k).wait_recv()

    def pack(turn, value, low, high):
        for side, rows in enumerate((low, high)):
            for j, row in enumerate(rows):
                send_x[turn, side, j] = value[row, 0:8]
                send_y[turn, side, :, j : j + 1, :] = value[0:8, row : row + 1]
        for k in range(4, 8):
            rows_x = low if DIRS[k][0] < 0 else high
            rows_y = low if DIRS[k][1] < 0 else high
            for i, row_x in enumerate(rows_x):
                for j, row_y in enumerate(rows_y):
                    send_d[turn, k - 4, i, j : j + 1, :] = value[row_x, row_y : row_y + 1]

    pack(0, res, (0, 1), (6, 7))
    pl.semaphore_wait(barrier, count)
    send_near(0)

    @pl.when(has_prev & ~after_origin)
    def _():
        pl.semaphore_signal(ready, 1, device_id=to_prev, device_id_type=MESH)

    for load in loads[4:]:
        load.wait()
    eigen = jnp.concatenate(
        [
            ex[...].reshape(160, 16),
            eyf[...].reshape(160, 16),
            eyb[...].reshape(160, 16),
            ez[...].reshape(240, 16),
            el[...].reshape(48, 16),
        ],
        axis=0,
    )
    parts = thirds(eigen)
    wanted = lax.broadcasted_iota(jnp.int32, (8, 16), 0) * 15
    picks = jnp.where(lax.broadcasted_iota(jnp.int32, (8, 16), 1) == wanted, 1.0, 0.0).astype(BF16)
    ends = sum(dot(picks, part, ((1,), (1,))) for part in parts)
    fe_send[0] = ends[0:1]
    fe_send[1] = ends[1:2]

    def prepare(g):
        element, mode = lanes(g)
        spread = jnp.where(
            lax.broadcasted_iota(jnp.int32, (16, 128), 0) == element, 1.0, 0.0
        ).astype(BF16)
        table = sum(dot(part, spread) for part in parts)
        if g == 1:
            row = lax.broadcasted_iota(jnp.int32, (8, ROWS), 0)
            other = jnp.where(row == 0, fe_recv[0], jnp.where(row == 1, fe_recv[1], 0.0))
            far_row = lax.broadcasted_iota(jnp.int32, (8, 128), 0)
            spread_far = jnp.where(
                ((far_row == 0) & (element == -1)) | ((far_row == 1) & (element == 16)), 1.0, 0.0
            ).astype(BF16)
            far = sum(dot(part, spread_far, ((0,), (0,))) for part in thirds(other))
            table = table + far
        cm[g] = table
        for r in range(100):
            at = 16 * (r // 10) + r % 10
            cxb[g, r // 10, r % 10] = jnp.broadcast_to(cm[g, at : at + 1, :], (8, 128))
        tiles = jnp.zeros((24, 128), F32)
        for s in range(10):
            tiles = tiles + jnp.where(mode == s, cm[g, OZ + 24 * s : OZ + 24 * s + 24, :], 0.0)
        inner, lower, upper = tiles[0:8], tiles[8:16], tiles[16:24]
        columns = []
        for e in list(range(16)) + [-2, -1, 16, 17]:
            columns.append(
                jnp.where(
                    element == e,
                    inner,
                    jnp.where(element == e + 1, lower, jnp.where(element == e - 1, upper, 0.0)),
                )
            )
        wh[g], wl[g] = halves(jnp.concatenate(columns, axis=0))
        rate_z = jnp.where(
            lax.broadcasted_iota(jnp.int32, (16, 128), 0) == mode, cm[g, OL + 32 : OL + 48, :], 0.0
        ).sum(axis=0, keepdims=True)
        rate_yz = cm[g, OL + 16 : OL + 32, :] + rate_z
        for p in range(10):
            rate = rate_yz + cm[g, OL + p : OL + p + 1, :]
            some = rate > 0.0
            inv[g, p] = jnp.where(some, 1.0 / jnp.where(some, rate, 1.0), 0.0)

    def rows_of(way):
        return pl.ds(6, 10) if way == 0 else pl.ds(0, 10)

    def far_copy(kind, way, arriving):
        if kind == 0:
            src, dst = fe_send.at[1 - way], fe_recv.at[way]
        else:
            src, dst = fx_send.at[way, rows_of(way)], fx_recv.at[way, rows_of(way)]
        return pltpu.make_async_remote_copy(
            src_ref=src,
            dst_ref=dst,
            send_sem=far_send.at[kind, way],
            recv_sem=far_recv.at[kind, way],
            device_id=to_next if (way == 0) != arriving else to_prev,
            device_id_type=MESH,
        )

    def aside(kind, passing):
        held = pe if kind == 0 else px
        if passing:
            src, dst = held, fe_recv.at[1] if kind == 0 else fx_recv.at[1, rows_of(1)]
        else:
            src, dst = fe_send.at[0] if kind == 0 else fx_send.at[1, rows_of(1)], held
        return pltpu.make_async_remote_copy(
            src_ref=src,
            dst_ref=dst,
            send_sem=side_send.at[kind] if passing else far_send.at[kind, 1],
            recv_sem=far_recv.at[kind, 1] if passing else side_recv.at[kind],
            device_id=(0, 0, 0) if passing else (1, 0, 0),
            device_id_type=MESH,
        )

    def send_down(kind):
        @pl.when(has_prev & ~after_origin)
        def _():
            far_copy(kind, 1, False).start()

        @pl.when(after_origin)
        def _():
            aside(kind, False).start()

    def send_up(kind):
        @pl.when(has_next)
        def _():
            far_copy(kind, 0, False).start()

    def pass_on(kind):
        @pl.when(helper)
        def _():
            aside(kind, False).wait_recv()
            aside(kind, True).start()

    def wait_far(kind):
        @pl.when(has_next)
        def _():
            far_copy(kind, 1, True).wait_recv()

        @pl.when(has_prev)
        def _():
            far_copy(kind, 0, True).wait_recv()

    send_down(0)
    prepare(0)

    wait_near(0)

    def join(own, prev, after):
        return jnp.concatenate(
            [own[0:1] + prev[1:2], own[1:7], own[7:8] + after[0:1], prev[0:1], after[1:2]], axis=0
        )

    xs[:, 0:8, :] = join(res, recv_x[0, 0], recv_x[0, 1])
    before = join(recv_y[0, 0], recv_d[0, 0], recv_d[0, 2])
    behind = join(recv_y[0, 1], recv_d[0, 1], recv_d[0, 3])
    xs[:, 0:1, :] = xs[:, 0:1, :] + before[:, 1:2]
    xs[:, 7:8, :] = xs[:, 7:8, :] + behind[:, 0:1]
    xs[:, 8:9, :] = before[:, 0:1]
    xs[:, 9:10, :] = behind[:, 1:2]
    xc[0:80, :] = xs[:, 0:8, :].reshape(80, 128)
    for a in range(10):
        xc[80 + 2 * a : 82 + 2 * a, :] = xs[a, 8:10, :]
    turned = xc[...].T
    fx_send[0] = turned[112:128]
    fx_send[1] = turned[0:16]

    send_down(1)
    nodes = halves(xs[...].reshape(160, 128))

    def to_modes(g):
        zs[g] = dot3(nodes, (wh[g, 0:128], wl[g, 0:128])).reshape(10, 16, 128)

    to_modes(0)

    @pl.when(has_next & ~origin)
    def _():
        pl.semaphore_wait(ready, 1)

    send_up(0)
    send_up(1)
    pass_on(0)
    wait_far(0)
    prepare(1)
    to_modes(1)
    pass_on(1)
    wait_far(1)

    beyond = halves(fx_recv[...].reshape(32, 128))

    def solve(g):
        more = dot3(beyond, (wh[g, 128:160], wl[g, 128:160]), ((0,), (0,)))
        zs[g, :, 0:8, :] = zs[g, :, 0:8, :] + more[0:80].reshape(10, 8, 128)
        for a in range(10):
            zs[g, a, 8:10, :] = zs[g, a, 8:10, :] + more[80 + 2 * a : 82 + 2 * a]
        value = zs[g].reshape(10, 2, 8, 128)
        total = None
        for a in range(10):
            term = cxb[g, a][:, None] * value[a][None]
            total = term if total is None else total + term
        value, total = total, None
        for b in range(10):
            row = value[:, b // 8, b % 8 : b % 8 + 1, :][:, None]
            pick = cm[g, OYF + 16 * b : OYF + 16 * b + 16, :].reshape(1, 2, 8, 128)
            term = pick * row
            total = term if total is None else total + term
        value, total = total * inv[g].reshape(10, 2, 8, 128), None
        for q in range(10):
            row = value[:, q // 8, q % 8 : q % 8 + 1, :][:, None]
            pick = cm[g, OYB + 16 * q : OYB + 16 * q + 16, :].reshape(1, 2, 8, 128)
            term = pick * row
            total = term if total is None else total + term
        value, total = total, None
        for p in range(10):
            term = cxb[g, :, p][:, None] * value[p][None]
            total = term if total is None else total + term
        return dot3(
            halves(total.reshape(160, 128)), (wh[g, 0:128], wl[g, 0:128]), ((1,), (1,))
        )

    found = (solve(0) + solve(1)).reshape(10, 16, 128)
    pack(1, found, (8, 0), (7, 9))
    send_near(1)
    wait_near(1)

    def gather(own, prev, after):
        return jnp.concatenate([own[0:2] + prev, own[2:6], own[6:8] + after], axis=0)

    out_ref[...] = gather(found[0:8, 0:8], recv_x[1, 0], recv_x[1, 1])
    out_ref[:, 0:2, :] = out_ref[:, 0:2, :] + gather(recv_y[1, 0], recv_d[1, 0], recv_d[1, 2])
    out_ref[:, 6:8, :] = out_ref[:, 6:8, :] + gather(recv_y[1, 1], recv_d[1, 1], recv_d[1, 3])

    for turn in range(2):
        for k in range(8):
            @pl.when(near[k])
            def _(turn=turn, k=k):
                outgoing(turn, k).wait_send()

    for kind in range(2):
        @pl.when(has_next)
        def _(kind=kind):
            far_copy(kind, 0, False).wait_send()

        @pl.when(has_prev & ~after_origin)
        def _(kind=kind):
            far_copy(kind, 1, False).wait_send()

        @pl.when(after_origin)
        def _(kind=kind):
            aside(kind, False).wait_send()

        @pl.when(helper)
        def _(kind=kind):
            aside(kind, True).wait_send()


def solution(mesh):
    nx, ny, nz = mesh.shape["gx"], mesh.shape["gy"], mesh.shape["gz"]

    def body(initial, source, metric, eigenvectors, eigenvalues):
        hbm = pl.BlockSpec(memory_space=pl.ANY)
        vmem = pltpu.VMEM
        correction = pl.pallas_call(
            functools.partial(kernel, nx, ny, nz),
            out_shape=jax.ShapeDtypeStruct((8, 8, 128), F32),
            in_specs=[hbm] * 6,
            out_specs=pl.BlockSpec(memory_space=vmem),
            scratch_shapes=[
                vmem((8, 8, 128), F32),
                vmem((8, 8, 128), F32),
                vmem((3, 8, 8, 128), F32),
                vmem((2, 448, 128), BF16),
                vmem((10, 16, 16), F32),
                vmem((10, 16, 16), F32),
                vmem((10, 16, 16), F32),
                vmem((10, 24, 16), F32),
                vmem((3, 16, 16), F32),
                pltpu.SemaphoreType.DMA((33,)),
                vmem((2, 2, 2, 8, 128), F32),
                vmem((2, 2, 8, 2, 128), F32),
                vmem((2, 4, 2, 2, 128), F32),
                vmem((2, 2, 2, 8, 128), F32),
                vmem((2, 2, 8, 2, 128), F32),
                vmem((2, 4, 2, 2, 128), F32),
                pltpu.SemaphoreType.DMA((2, 8)),
                pltpu.SemaphoreType.DMA((2, 8)),
                vmem((2, 1, ROWS), F32),
                vmem((2, 1, ROWS), F32),
                vmem((2, 16, 128), F32),
                vmem((2, 16, 128), F32),
                pltpu.SemaphoreType.DMA((2, 2)),
                pltpu.SemaphoreType.DMA((2, 2)),
                pltpu.SemaphoreType.REGULAR,
                vmem((1, ROWS), F32),
                vmem((10, 128), F32),
                pltpu.SemaphoreType.DMA((2,)),
                pltpu.SemaphoreType.DMA((2,)),
                vmem((10, 16, 128), F32),
                vmem((128, 128), F32),
                vmem((2, ROWS, 128), F32),
                vmem((2, 10, 10, 8, 128), F32),
                vmem((2, 10, 16, 128), F32),
                vmem((2, 160, 128), BF16),
                vmem((2, 160, 128), BF16),
                vmem((2, 10, 16, 128), F32),
            ],
            compiler_params=pltpu.CompilerParams(collective_id=0, has_side_effects=True),
        )(
            initial,
            source,
            metric,
            eigenvectors,
            eigenvalues,
            jnp.asarray(operator_tables()),
        )
        return initial + correction

    placed = (
        P("gx", "gy", "gz"),
        P("gx", "gy", "gz"),
        P(None, "gx", "gy", "gz"),
        P(None, None, None, "gx", "gy", "gz"),
        P(None, None, "gx", "gy", "gz"),
    )
    return jax.shard_map(
        body, mesh=mesh, in_specs=placed, out_specs=P("gx", "gy", "gz"), check_vma=False
    )
```

```python
import functools

import jax
import jax.numpy as jnp
import numpy as np
from jax import lax
from jax.experimental import pallas as pl
from jax.experimental.pallas import tpu as pltpu
from jax.sharding import PartitionSpec as P

MESH = pl.DeviceIdType.MESH
F32 = jnp.float32
BF16 = jnp.bfloat16

gll_points = np.array(
    [
        -1.0,
        -0.8717401485096066,
        -0.5917001814331423,
        -0.2092992179024789,
        0.2092992179024789,
        0.5917001814331423,
        0.8717401485096066,
        1.0,
    ]
)

DIRS = [(-1, 0), (1, 0), (0, -1), (0, 1), (-1, -1), (-1, 1), (1, -1), (1, 1)]
OPP = [1, 0, 3, 2, 7, 6, 5, 4]
OYF, OYB, OZ, OL, ROWS = 160, 320, 480, 720, 768


def derivative_table():
    number = gll_points.shape[0]
    products = np.array(
        [
            np.prod([gll_points[i] - gll_points[k] for k in range(number) if k != i])
            for i in range(number)
        ]
    )
    table = np.zeros((number, number))
    for i in range(number):
        for j in range(number):
            if i != j:
                table[i, j] = products[i] / products[j] / (gll_points[i] - gll_points[j])
        table[i, i] = -np.sum(table[i])
    return table


def operator_tables():
    table = derivative_table().astype(np.float32)
    eye = np.eye(8, dtype=np.float32)
    left = np.concatenate([np.kron(table, eye), np.kron(eye, table)], axis=0)
    left = np.concatenate([left, np.zeros((128, 64), np.float32)], axis=1)
    left_t = np.ascontiguousarray(left.T[:64])
    right = np.kron(np.eye(16, dtype=np.float32), table.T)
    full = np.concatenate([left, left_t, right, right.T], axis=0)
    high = full.astype(jnp.bfloat16)
    low = (full - high.astype(np.float32)).astype(jnp.bfloat16)
    return np.stack([high, low])


def dot(a, b, dims=((1,), (0,))):
    return lax.dot_general(a, b, (dims, ((), ())), preferred_element_type=F32)


def halves(value):
    high = value.astype(BF16)
    return high, (value - high.astype(F32)).astype(BF16)


def thirds(value):
    high = value.astype(BF16)
    rest = value - high.astype(F32)
    mid = rest.astype(BF16)
    return high, mid, (rest - mid.astype(F32)).astype(BF16)


def dot3(a, b, dims=((1,), (0,))):
    return dot(a[0], b[0], dims) + (dot(a[1], b[0], dims) + dot(a[0], b[1], dims))


def lanes(group):
    lane = lax.broadcasted_iota(jnp.int32, (1, 128), 1)
    block = (lane * 205) >> 11
    mode = lane - 10 * block
    if group == 0:
        return jnp.where(lane < 120, block + 1, 99), mode
    ends = jnp.where(block < 2, block - 1, block + 11)
    return jnp.where(lane < 60, ends, 99), mode


def kernel(
    nx, ny, nz,
    u_h, f_h, m_h, eig_h, lam_h, cst_h, out_ref,
    u_v, f_v, m_v, cst_v, ex, eyf, eyb, ez, el, in_sem,
    send_x, send_y, send_d, recv_x, recv_y, recv_d, near_send, near_recv,
    fe_send, fe_recv, fx_send, fx_recv, far_send, far_recv, ready, near_ready, pe, px, side_send, side_recv,
    xs, xc, cm, cxb, inv, wh, wl, zs,
):
    ix, iy, iz = lax.axis_index("gx"), lax.axis_index("gy"), lax.axis_index("gz")

    first = [(u_h, u_v), (cst_h, cst_v), (m_h, m_v), (f_h, f_v)]
    second = [
        (eig_h.at[0, 1:9, :, 0, 0], ex.at[0:8, 0:10]),
        (eig_h.at[0, 0, :, 0, 0], ex.at[8, 0:10]),
        (eig_h.at[0, 9, :, 0, 0], ex.at[9, 0:10]),
        (eig_h.at[1, 1:9, :, 0, 0], eyf.at[0:8, 0:10]),
        (eig_h.at[1, 0, :, 0, 0], eyf.at[8, 0:10]),
        (eig_h.at[1, 9, :, 0, 0], eyf.at[9, 0:10]),
        (lam_h.at[:, :, 0, 0], el.at[:, 0:10]),
    ]
    for row, pos in enumerate([1, 2, 3, 4, 5, 6, 7, 8, 0, 9]):
        second.append((eig_h.at[1, pos, :, 0, 0], eyb.at[:, row]))
    for row, pos in enumerate([1, 2, 3, 4, 5, 6, 7, 8]):
        second.append((eig_h.at[2, pos, :, 0, 0], ez.at[:, row]))
    for row, pos in [(14, 0), (15, 1), (16, 8), (17, 9)]:
        second.append((eig_h.at[2, pos, :, 0, 0], ez.at[:, row]))
    loads = [
        pltpu.make_async_copy(src, dst, in_sem.at[i])
        for i, (src, dst) in enumerate(first + second)
    ]
    for load in loads:
        load.start()

    recv_x[...] = jnp.zeros_like(recv_x)
    recv_y[...] = jnp.zeros_like(recv_y)
    recv_d[...] = jnp.zeros_like(recv_d)
    fe_recv[...] = jnp.zeros_like(fe_recv)
    fx_recv[...] = jnp.zeros_like(fx_recv)

    has_next, has_prev = iz < nz - 1, iz > 0
    to_next, to_prev = (ix, iy, iz + 1), (ix, iy, iz - 1)
    detour = nx > 1 and nz > 1
    in_line = (ix == 0) & (iy == 0)
    origin = in_line & (iz == 0) & detour
    after_origin = in_line & (iz == 1) & detour
    helper = (ix == 1) & (iy == 0) & (iz == 0) & detour
    near, target = [], []
    for dx, dy in DIRS:
        ok = None
        for cond in (
            [ix > 0] * (dx < 0) + [ix < nx - 1] * (dx > 0)
            + [iy > 0] * (dy < 0) + [iy < ny - 1] * (dy > 0)
        ):
            ok = cond if ok is None else ok & cond
        near.append(ok)
        target.append((ix + dx, iy + dy, iz))
    barrier = pltpu.get_barrier_semaphore()
    count = jnp.int32(0)
    later = []
    for dx, dy in DIRS:
        if dy > 0 or (dy == 0 and dx < 0):
            later.append(~origin)
        else:
            later.append(detour & (iz == 0) & (ix + dx == 0) & (iy + dy == 0))
    before_me = [ok & ~after for ok, after in zip(near, later)]
    after_me = [ok & after for ok, after in zip(near, later)]
    first_row = (iy == 0) & (iz == 0) & (nx > 2)
    greeted = list(zip(after_me, target)) + [
        (has_next & ~origin, to_next), (helper, (0, 0, 1)), (after_origin, (0, 0, 0)),
        (first_row & (ix == nx - 2), (nx - 1, iy, iz)),
    ]
    for ok, device in greeted:
        @pl.when(ok)
        def _(device=device):
            pl.semaphore_signal(barrier, 1, device_id=device, device_id_type=MESH)
    count = jnp.int32(0)
    for ok in before_me + [has_prev, origin, first_row & (ix == nx - 1)]:
        count = count + ok.astype(jnp.int32)

    ex[:, 10:16, :] = jnp.zeros((10, 6, 16), F32)
    eyf[:, 10:16, :] = jnp.zeros((10, 6, 16), F32)
    eyb[:, 10:16, :] = jnp.zeros((10, 6, 16), F32)
    ez[:, 8:14, :] = jnp.zeros((10, 6, 16), F32)
    ez[:, 18:24, :] = jnp.zeros((10, 6, 16), F32)
    el[:, 10:16, :] = jnp.zeros((3, 6, 16), F32)
    xs[:, 10:16, :] = jnp.zeros((10, 6, 128), F32)
    xc[96:128, :] = jnp.zeros((32, 128), F32)

    pl.semaphore_wait(barrier, count)
    for k in range(8):
        @pl.when(before_me[k])
        def _(k=k):
            pl.semaphore_signal(
                near_ready.at[OPP[k]], 1, device_id=target[k], device_id_type=MESH
            )

    @pl.when(has_prev & ~after_origin)
    def _():
        pl.semaphore_signal(ready, 1, device_id=to_prev, device_id_type=MESH)

    for load in loads[:4]:
        load.wait()
    field = halves(u_v[...].reshape(64, 128))
    left = cst_v[0, 0:128, 0:64], cst_v[1, 0:128, 0:64]
    left_t = cst_v[0, 128:192], cst_v[1, 128:192]
    right = cst_v[0, 192:320], cst_v[1, 192:320]
    right_t = cst_v[0, 320:448], cst_v[1, 320:448]
    flux = dot3(left, field) * m_v[0:2].reshape(128, 128)
    flux_z = dot3(field, right) * m_v[2].reshape(64, 128)
    applied = dot3(left_t, halves(flux)) + dot3(halves(flux_z), right_t)
    res = f_v[...] - applied.reshape(8, 8, 128)

    def recv_of(turn, k):
        if k < 2:
            return recv_x.at[turn, k]
        return recv_y.at[turn, k - 2] if k < 4 else recv_d.at[turn, k - 4]

    def send_of(turn, k):
        if k < 2:
            return send_x.at[turn, k]
        return send_y.at[turn, k - 2] if k < 4 else send_d.at[turn, k - 4]

    def outgoing(turn, k):
        return pltpu.make_async_remote_copy(
            src_ref=send_of(turn, k),
            dst_ref=recv_of(turn, OPP[k]),
            send_sem=near_send.at[turn, k],
            recv_sem=near_recv.at[turn, OPP[k]],
            device_id=target[k],
            device_id_type=MESH,
        )

    def incoming(turn, k):
        return pltpu.make_async_remote_copy(
            src_ref=send_of(turn, k),
            dst_ref=recv_of(turn, k),
            send_sem=near_send.at[turn, k],
            recv_sem=near_recv.at[turn, k],
            device_id=target[k],
            device_id_type=MESH,
        )

    ORDER = [4, 5, 6, 7, 0, 1, 2, 3]

    def send_near(turn, where):
        for k in ORDER:
            @pl.when(where[k])
            def _(k=k):
                if where is after_me:
                    pl.semaphore_wait(near_ready.at[k], 1)
                outgoing(turn, k).start()

    def wait_near(turn):
        for k in ORDER:
            @pl.when(near[k])
            def _(k=k):
                incoming(turn, k).wait_recv()

    def pack(turn, value, low, high):
        for side, rows in enumerate((low, high)):
            for j, row in enumerate(rows):
                send_x[turn, side, j] = value[row, 0:8]
                send_y[turn, side, :, j : j + 1, :] = value[0:8, row : row + 1]
        for k in range(4, 8):
            rows_x = low if DIRS[k][0] < 0 else high
            rows_y = low if DIRS[k][1] < 0 else high
            for i, row_x in enumerate(rows_x):
                for j, row_y in enumerate(rows_y):
                    send_d[turn, k - 4, i, j : j + 1, :] = value[row_x, row_y : row_y + 1]

    pack(0, res, (0, 1), (6, 7))
    send_near(0, before_me)

    for load in loads[4:]:
        load.wait()
    eigen = jnp.concatenate(
        [
            ex[...].reshape(160, 16),
            eyf[...].reshape(160, 16),
            eyb[...].reshape(160, 16),
            ez[...].reshape(240, 16),
            el[...].reshape(48, 16),
        ],
        axis=0,
    )
    parts = thirds(eigen)
    wanted = lax.broadcasted_iota(jnp.int32, (8, 16), 0) * 15
    picks = jnp.where(lax.broadcasted_iota(jnp.int32, (8, 16), 1) == wanted, 1.0, 0.0).astype(BF16)
    ends = sum(dot(picks, part, ((1,), (1,))) for part in parts)
    fe_send[0] = ends[0:1]
    fe_send[1] = ends[1:2]

    def prepare(g):
        element, mode = lanes(g)
        spread = jnp.where(
            lax.broadcasted_iota(jnp.int32, (16, 128), 0) == element, 1.0, 0.0
        ).astype(BF16)
        table = sum(dot(part, spread) for part in parts)
        if g == 1:
            row = lax.broadcasted_iota(jnp.int32, (8, ROWS), 0)
            other = jnp.where(row == 0, fe_recv[0], jnp.where(row == 1, fe_recv[1], 0.0))
            far_row = lax.broadcasted_iota(jnp.int32, (8, 128), 0)
            spread_far = jnp.where(
                ((far_row == 0) & (element == -1)) | ((far_row == 1) & (element == 16)), 1.0, 0.0
            ).astype(BF16)
            far = sum(dot(part, spread_far, ((0,), (0,))) for part in thirds(other))
            table = table + far
        cm[g] = table
        for r in range(100):
            at = 16 * (r // 10) + r % 10
            cxb[g, r // 10, r % 10] = jnp.broadcast_to(cm[g, at : at + 1, :], (8, 128))
        tiles = jnp.zeros((24, 128), F32)
        for s in range(10):
            tiles = tiles + jnp.where(mode == s, cm[g, OZ + 24 * s : OZ + 24 * s + 24, :], 0.0)
        inner, lower, upper = tiles[0:8], tiles[8:16], tiles[16:24]
        columns = []
        for e in list(range(16)) + [-2, -1, 16, 17]:
            columns.append(
                jnp.where(
                    element == e,
                    inner,
                    jnp.where(element == e + 1, lower, jnp.where(element == e - 1, upper, 0.0)),
                )
            )
        wh[g], wl[g] = halves(jnp.concatenate(columns, axis=0))
        rate_z = jnp.where(
            lax.broadcasted_iota(jnp.int32, (16, 128), 0) == mode, cm[g, OL + 32 : OL + 48, :], 0.0
        ).sum(axis=0, keepdims=True)
        rate_yz = cm[g, OL + 16 : OL + 32, :] + rate_z
        for p in range(10):
            rate = rate_yz + cm[g, OL + p : OL + p + 1, :]
            some = rate > 0.0
            inv[g, p] = jnp.where(some, 1.0 / jnp.where(some, rate, 1.0), 0.0)

    def rows_of(way):
        return pl.ds(6, 10) if way == 0 else pl.ds(0, 10)

    def far_copy(kind, way, arriving):
        if kind == 0:
            src, dst = fe_send.at[1 - way], fe_recv.at[way]
        else:
            src, dst = fx_send.at[way, rows_of(way)], fx_recv.at[way, rows_of(way)]
        return pltpu.make_async_remote_copy(
            src_ref=src,
            dst_ref=dst,
            send_sem=far_send.at[kind, way],
            recv_sem=far_recv.at[kind, way],
            device_id=to_next if (way == 0) != arriving else to_prev,
            device_id_type=MESH,
        )

    def aside(kind, passing):
        held = pe if kind == 0 else px
        if passing:
            src, dst = held, fe_recv.at[1] if kind == 0 else fx_recv.at[1, rows_of(1)]
        else:
            src, dst = fe_send.at[0] if kind == 0 else fx_send.at[1, rows_of(1)], held
        return pltpu.make_async_remote_copy(
            src_ref=src,
            dst_ref=dst,
            send_sem=side_send.at[kind] if passing else far_send.at[kind, 1],
            recv_sem=far_recv.at[kind, 1] if passing else side_recv.at[kind],
            device_id=(0, 0, 0) if passing else (1, 0, 0),
            device_id_type=MESH,
        )

    def send_down(kind):
        @pl.when(has_prev & ~after_origin)
        def _():
            far_copy(kind, 1, False).start()

        @pl.when(after_origin)
        def _():
            aside(kind, False).start()

    def send_up(kind):
        @pl.when(has_next)
        def _():
            far_copy(kind, 0, False).start()

    def pass_on(kind):
        @pl.when(helper)
        def _():
            aside(kind, False).wait_recv()
            aside(kind, True).start()

    def wait_far(kind):
        @pl.when(has_next)
        def _():
            far_copy(kind, 1, True).wait_recv()

        @pl.when(has_prev)
        def _():
            far_copy(kind, 0, True).wait_recv()

    send_down(0)
    send_near(0, after_me)
    prepare(0)

    wait_near(0)

    def join(own, prev, after):
        return jnp.concatenate(
            [own[0:1] + prev[1:2], own[1:7], own[7:8] + after[0:1], prev[0:1], after[1:2]], axis=0
        )

    xs[:, 0:8, :] = join(res, recv_x[0, 0], recv_x[0, 1])
    before = join(recv_y[0, 0], recv_d[0, 0], recv_d[0, 2])
    behind = join(recv_y[0, 1], recv_d[0, 1], recv_d[0, 3])
    xs[:, 0:1, :] = xs[:, 0:1, :] + before[:, 1:2]
    xs[:, 7:8, :] = xs[:, 7:8, :] + behind[:, 0:1]
    xs[:, 8:9, :] = before[:, 0:1]
    xs[:, 9:10, :] = behind[:, 1:2]
    xc[0:80, :] = xs[:, 0:8, :].reshape(80, 128)
    for a in range(10):
        xc[80 + 2 * a : 82 + 2 * a, :] = xs[a, 8:10, :]
    turned = xc[...].T
    fx_send[0] = turned[112:128]
    fx_send[1] = turned[0:16]

    send_down(1)
    nodes = halves(xs[...].reshape(160, 128))

    def to_modes(g):
        zs[g] = dot3(nodes, (wh[g, 0:128], wl[g, 0:128])).reshape(10, 16, 128)

    def solve(g):
        value = zs[g].reshape(10, 2, 8, 128)
        total = None
        for a in range(10):
            term = cxb[g, a][:, None] * value[a][None]
            total = term if total is None else total + term
        value, total = total, None
        for b in range(10):
            row = value[:, b // 8, b % 8 : b % 8 + 1, :][:, None]
            pick = cm[g, OYF + 16 * b : OYF + 16 * b + 16, :].reshape(1, 2, 8, 128)
            term = pick * row
            total = term if total is None else total + term
        value, total = total * inv[g].reshape(10, 2, 8, 128), None
        for q in range(10):
            row = value[:, q // 8, q % 8 : q % 8 + 1, :][:, None]
            pick = cm[g, OYB + 16 * q : OYB + 16 * q + 16, :].reshape(1, 2, 8, 128)
            term = pick * row
            total = term if total is None else total + term
        value, total = total, None
        for p in range(10):
            term = cxb[g, :, p][:, None] * value[p][None]
            total = term if total is None else total + term
        return dot3(
            halves(total.reshape(160, 128)), (wh[g, 0:128], wl[g, 0:128]), ((1,), (1,))
        )

    to_modes(0)

    @pl.when(has_next & ~origin)
    def _():
        pl.semaphore_wait(ready, 1)

    send_up(0)
    send_up(1)
    found = solve(0)
    pass_on(0)
    wait_far(0)
    prepare(1)
    to_modes(1)
    pass_on(1)
    wait_far(1)

    beyond = halves(fx_recv[...].reshape(32, 128))

    more = dot3(beyond, (wh[1, 128:160], wl[1, 128:160]), ((0,), (0,)))
    zs[1, :, 0:8, :] = zs[1, :, 0:8, :] + more[0:80].reshape(10, 8, 128)
    for a in range(10):
        zs[1, a, 8:10, :] = zs[1, a, 8:10, :] + more[80 + 2 * a : 82 + 2 * a]
    found = (found + solve(1)).reshape(10, 16, 128)
    pack(1, found, (8, 0), (7, 9))
    send_near(1, near)
    wait_near(1)

    def gather(own, prev, after):
        return jnp.concatenate([own[0:2] + prev, own[2:6], own[6:8] + after], axis=0)

    out_ref[...] = gather(found[0:8, 0:8], recv_x[1, 0], recv_x[1, 1])
    out_ref[:, 0:2, :] = out_ref[:, 0:2, :] + gather(recv_y[1, 0], recv_d[1, 0], recv_d[1, 2])
    out_ref[:, 6:8, :] = out_ref[:, 6:8, :] + gather(recv_y[1, 1], recv_d[1, 1], recv_d[1, 3])

    for turn in range(2):
        for k in range(8):
            @pl.when(near[k])
            def _(turn=turn, k=k):
                outgoing(turn, k).wait_send()

    for kind in range(2):
        @pl.when(has_next)
        def _(kind=kind):
            far_copy(kind, 0, False).wait_send()

        @pl.when(has_prev & ~after_origin)
        def _(kind=kind):
            far_copy(kind, 1, False).wait_send()

        @pl.when(after_origin)
        def _(kind=kind):
            aside(kind, False).wait_send()

        @pl.when(helper)
        def _(kind=kind):
            aside(kind, True).wait_send()


def solution(mesh):
    nx, ny, nz = mesh.shape["gx"], mesh.shape["gy"], mesh.shape["gz"]

    def body(initial, source, metric, eigenvectors, eigenvalues):
        hbm = pl.BlockSpec(memory_space=pl.ANY)
        vmem = pltpu.VMEM
        correction = pl.pallas_call(
            functools.partial(kernel, nx, ny, nz),
            out_shape=vmem((8, 8, 128), F32),
            in_specs=[hbm] * 6,
            out_specs=pl.BlockSpec(memory_space=vmem),
            scratch_shapes=[
                vmem((8, 8, 128), F32),
                vmem((8, 8, 128), F32),
                vmem((3, 8, 8, 128), F32),
                vmem((2, 448, 128), BF16),
                vmem((10, 16, 16), F32),
                vmem((10, 16, 16), F32),
                vmem((10, 16, 16), F32),
                vmem((10, 24, 16), F32),
                vmem((3, 16, 16), F32),
                pltpu.SemaphoreType.DMA((33,)),
                vmem((2, 2, 2, 8, 128), F32),
                vmem((2, 2, 8, 2, 128), F32),
                vmem((2, 4, 2, 2, 128), F32),
                vmem((2, 2, 2, 8, 128), F32),
                vmem((2, 2, 8, 2, 128), F32),
                vmem((2, 4, 2, 2, 128), F32),
                pltpu.SemaphoreType.DMA((2, 8)),
                pltpu.SemaphoreType.DMA((2, 8)),
                vmem((2, 1, ROWS), F32),
                vmem((2, 1, ROWS), F32),
                vmem((2, 16, 128), F32),
                vmem((2, 16, 128), F32),
                pltpu.SemaphoreType.DMA((2, 2)),
                pltpu.SemaphoreType.DMA((2, 2)),
                pltpu.SemaphoreType.REGULAR,
                pltpu.SemaphoreType.REGULAR((8,)),
                vmem((1, ROWS), F32),
                vmem((10, 128), F32),
                pltpu.SemaphoreType.DMA((2,)),
                pltpu.SemaphoreType.DMA((2,)),
                vmem((10, 16, 128), F32),
                vmem((128, 128), F32),
                vmem((2, ROWS, 128), F32),
                vmem((2, 10, 10, 8, 128), F32),
                vmem((2, 10, 16, 128), F32),
                vmem((2, 160, 128), BF16),
                vmem((2, 160, 128), BF16),
                vmem((2, 10, 16, 128), F32),
            ],
            compiler_params=pltpu.CompilerParams(collective_id=0, has_side_effects=True),
        )(
            initial,
            source,
            metric,
            eigenvectors,
            eigenvalues,
            jnp.asarray(operator_tables()),
        )
        return initial + correction

    placed = (
        P("gx", "gy", "gz"),
        P("gx", "gy", "gz"),
        P(None, "gx", "gy", "gz"),
        P(None, None, None, "gx", "gy", "gz"),
        P(None, None, "gx", "gy", "gz"),
    )
    return jax.shard_map(
        body, mesh=mesh, in_specs=placed, out_specs=P("gx", "gy", "gz"), check_vma=False
    )
```

```python
import functools

import jax
import jax.numpy as jnp
import numpy as np
from jax import lax
from jax.experimental import pallas as pl
from jax.experimental.pallas import tpu as pltpu
from jax.sharding import PartitionSpec as P

MESH = pl.DeviceIdType.MESH
F32 = jnp.float32
BF16 = jnp.bfloat16

gll_points = np.array(
    [
        -1.0,
        -0.8717401485096066,
        -0.5917001814331423,
        -0.2092992179024789,
        0.2092992179024789,
        0.5917001814331423,
        0.8717401485096066,
        1.0,
    ]
)

DIRS = [(-1, 0), (1, 0), (0, -1), (0, 1), (-1, -1), (-1, 1), (1, -1), (1, 1)]
OPP = [1, 0, 3, 2, 7, 6, 5, 4]
PIECES = [4, 6, 2, 5, 7, 3, 0, 1, 8]
HELD = {0: 0, 2: 1, 4: 2, 8: 3}
OYF, OYB, OZ, OL, ROWS = 160, 320, 480, 720, 768


def derivative_table():
    number = gll_points.shape[0]
    products = np.array(
        [
            np.prod([gll_points[i] - gll_points[k] for k in range(number) if k != i])
            for i in range(number)
        ]
    )
    table = np.zeros((number, number))
    for i in range(number):
        for j in range(number):
            if i != j:
                table[i, j] = products[i] / products[j] / (gll_points[i] - gll_points[j])
        table[i, i] = -np.sum(table[i])
    return table


def operator_tables():
    table = derivative_table().astype(np.float32)
    eye = np.eye(8, dtype=np.float32)
    left = np.concatenate([np.kron(table, eye), np.kron(eye, table)], axis=0)
    left = np.concatenate([left, np.zeros((128, 64), np.float32)], axis=1)
    left_t = np.ascontiguousarray(left.T[:64])
    right = np.kron(np.eye(16, dtype=np.float32), table.T)
    full = np.concatenate([left, left_t, right, right.T], axis=0)
    high = full.astype(jnp.bfloat16)
    low = (full - high.astype(np.float32)).astype(jnp.bfloat16)
    return np.stack([high, low])


def dot(a, b, dims=((1,), (0,))):
    return lax.dot_general(a, b, (dims, ((), ())), preferred_element_type=F32)


def halves(value):
    high = value.astype(BF16)
    return high, (value - high.astype(F32)).astype(BF16)


def thirds(value):
    high = value.astype(BF16)
    rest = value - high.astype(F32)
    mid = rest.astype(BF16)
    return high, mid, (rest - mid.astype(F32)).astype(BF16)


def dot3(a, b, dims=((1,), (0,))):
    return dot(a[0], b[0], dims) + (dot(a[1], b[0], dims) + dot(a[0], b[1], dims))


def lanes(group):
    lane = lax.broadcasted_iota(jnp.int32, (1, 128), 1)
    block = (lane * 205) >> 11
    mode = lane - 10 * block
    if group == 0:
        return jnp.where(lane < 120, block + 1, 99), mode
    ends = jnp.where(block < 2, block - 1, block + 11)
    return jnp.where(lane < 60, ends, 99), mode


def kernel(
    nx, ny, nz,
    u_h, f_h, m_h, eig_h, lam_h, cst_h, out_ref,
    u_v, f_v, m_v, cst_v, ex, eyf, eyb, ez, el, in_sem,
    send_x, send_y, send_d, recv_x, recv_y, recv_d, near_send, near_recv,
    fe_send, fe_recv, fx_send, fx_recv, far_send, far_recv, ready, near_ready, pe, side_send, side_recv,
    slab_send, slab_recv, slab_held, part_send, part_recv, part_held, piece_send, piece_recv, held_send, held_recv, xf, fan,
    xs, xc, cm, cxb, inv, wh, wl, zs,
):
    ix, iy, iz = lax.axis_index("gx"), lax.axis_index("gy"), lax.axis_index("gz")

    first = [(u_h, u_v), (cst_h, cst_v), (m_h, m_v), (f_h, f_v)]
    second = [
        (eig_h.at[0, 1:9, :, 0, 0], ex.at[0:8, 0:10]),
        (eig_h.at[0, 0, :, 0, 0], ex.at[8, 0:10]),
        (eig_h.at[0, 9, :, 0, 0], ex.at[9, 0:10]),
        (eig_h.at[1, 1:9, :, 0, 0], eyf.at[0:8, 0:10]),
        (eig_h.at[1, 0, :, 0, 0], eyf.at[8, 0:10]),
        (eig_h.at[1, 9, :, 0, 0], eyf.at[9, 0:10]),
        (lam_h.at[:, :, 0, 0], el.at[:, 0:10]),
    ]
    for row, pos in enumerate([1, 2, 3, 4, 5, 6, 7, 8, 0, 9]):
        second.append((eig_h.at[1, pos, :, 0, 0], eyb.at[:, row]))
    for row, pos in enumerate([1, 2, 3, 4, 5, 6, 7, 8]):
        second.append((eig_h.at[2, pos, :, 0, 0], ez.at[:, row]))
    for row, pos in [(14, 0), (15, 1), (16, 8), (17, 9)]:
        second.append((eig_h.at[2, pos, :, 0, 0], ez.at[:, row]))
    loads = [
        pltpu.make_async_copy(src, dst, in_sem.at[i])
        for i, (src, dst) in enumerate(first + second)
    ]
    for load in loads:
        load.start()

    recv_x[...] = jnp.zeros_like(recv_x)
    recv_y[...] = jnp.zeros_like(recv_y)
    recv_d[...] = jnp.zeros_like(recv_d)
    fe_recv[...] = jnp.zeros_like(fe_recv)
    fx_recv[...] = jnp.zeros_like(fx_recv)
    slab_recv[...] = jnp.zeros_like(slab_recv)
    part_recv[...] = jnp.zeros_like(part_recv)
    xf[...] = jnp.zeros_like(xf)
    fan[...] = jnp.zeros_like(fan)

    has_next, has_prev = iz < nz - 1, iz > 0
    to_next, to_prev = (ix, iy, iz + 1), (ix, iy, iz - 1)
    detour = nx > 1 and nz > 1
    in_line = (ix == 0) & (iy == 0)
    origin = in_line & (iz == 0) & detour
    after_origin = in_line & (iz == 1) & detour
    helper = (ix == 1) & (iy == 0) & (iz == 0) & detour
    near, target = [], []
    for dx, dy in DIRS:
        ok = None
        for cond in (
            [ix > 0] * (dx < 0) + [ix < nx - 1] * (dx > 0)
            + [iy > 0] * (dy < 0) + [iy < ny - 1] * (dy > 0)
        ):
            ok = cond if ok is None else ok & cond
        near.append(ok)
        target.append((ix + dx, iy + dy, iz))
    barrier = pltpu.get_barrier_semaphore()
    count = jnp.int32(0)
    later = []
    for dx, dy in DIRS:
        if dy > 0 or (dy == 0 and dx < 0):
            later.append(~origin)
        else:
            later.append(detour & (iz == 0) & (ix + dx == 0) & (iy + dy == 0))
    before_me = [ok & ~after for ok, after in zip(near, later)]
    after_me = [ok & after for ok, after in zip(near, later)]
    first_row = (iy == 0) & (iz == 0) & (nx > 2)
    greeted = list(zip(after_me, target)) + [
        (has_next & ~origin, to_next), (after_origin, (0, 0, 0)),
        (first_row & (ix == nx - 2), (nx - 1, iy, iz)),
    ]
    over, under, from_origin = [], [], []
    for k, (dx, dy) in enumerate(DIRS + [(0, 0)]):
        inside = near[k] if k < 8 else (ix >= 0)
        over.append(has_next & inside)
        under.append(has_prev & inside)
        from_origin.append(detour & (iz == 1) & (ix + dx == 0) & (iy + dy == 0))
        if k < 8:
            greeted.append((over[k] & ~origin, (ix + dx, iy + dy, iz + 1)))
    for ok, device in greeted:
        @pl.when(ok)
        def _(device=device):
            pl.semaphore_signal(barrier, 1, device_id=device, device_id_type=MESH)
    count = jnp.int32(0)
    below = [ok & ~start for ok, start in zip(under, from_origin)]
    for ok in before_me + below + [origin, first_row & (ix == nx - 1)]:
        count = count + ok.astype(jnp.int32)

    ex[:, 10:16, :] = jnp.zeros((10, 6, 16), F32)
    eyf[:, 10:16, :] = jnp.zeros((10, 6, 16), F32)
    eyb[:, 10:16, :] = jnp.zeros((10, 6, 16), F32)
    ez[:, 8:14, :] = jnp.zeros((10, 6, 16), F32)
    ez[:, 18:24, :] = jnp.zeros((10, 6, 16), F32)
    el[:, 10:16, :] = jnp.zeros((3, 6, 16), F32)
    xs[:, 10:16, :] = jnp.zeros((10, 6, 128), F32)
    xc[96:128, :] = jnp.zeros((32, 128), F32)

    pl.semaphore_wait(barrier, count)
    for k in range(8):
        @pl.when(before_me[k])
        def _(k=k):
            pl.semaphore_signal(
                near_ready.at[OPP[k]], 1, device_id=target[k], device_id_type=MESH
            )

    @pl.when(has_prev & ~after_origin)
    def _():
        pl.semaphore_signal(ready, 1, device_id=to_prev, device_id_type=MESH)

    for load in loads[:4]:
        load.wait()
    field = halves(u_v[...].reshape(64, 128))
    left = cst_v[0, 0:128, 0:64], cst_v[1, 0:128, 0:64]
    left_t = cst_v[0, 128:192], cst_v[1, 128:192]
    right = cst_v[0, 192:320], cst_v[1, 192:320]
    right_t = cst_v[0, 320:448], cst_v[1, 320:448]
    flux = dot3(left, field) * m_v[0:2].reshape(128, 128)
    flux_z = dot3(field, right) * m_v[2].reshape(64, 128)
    applied = dot3(left_t, halves(flux)) + dot3(halves(flux_z), right_t)
    res = f_v[...] - applied.reshape(8, 8, 128)

    def recv_of(turn, k):
        if k < 2:
            return recv_x.at[turn, k]
        return recv_y.at[turn, k - 2] if k < 4 else recv_d.at[turn, k - 4]

    def send_of(turn, k):
        if k < 2:
            return send_x.at[turn, k]
        return send_y.at[turn, k - 2] if k < 4 else send_d.at[turn, k - 4]

    def outgoing(turn, k):
        return pltpu.make_async_remote_copy(
            src_ref=send_of(turn, k),
            dst_ref=recv_of(turn, OPP[k]),
            send_sem=near_send.at[turn, k],
            recv_sem=near_recv.at[turn, OPP[k]],
            device_id=target[k],
            device_id_type=MESH,
        )

    def incoming(turn, k):
        return pltpu.make_async_remote_copy(
            src_ref=send_of(turn, k),
            dst_ref=recv_of(turn, k),
            send_sem=near_send.at[turn, k],
            recv_sem=near_recv.at[turn, k],
            device_id=target[k],
            device_id_type=MESH,
        )

    ORDER = [4, 5, 6, 7, 0, 1, 2, 3]

    def send_near(turn, where):
        for k in ORDER:
            @pl.when(where[k])
            def _(k=k):
                if where is after_me:
                    pl.semaphore_wait(near_ready.at[k], 1)
                outgoing(turn, k).start()

    def wait_near(turn):
        for k in ORDER:
            @pl.when(near[k])
            def _(k=k):
                incoming(turn, k).wait_recv()

    def pack(turn, value, low, high):
        for side, rows in enumerate((low, high)):
            for j, row in enumerate(rows):
                send_x[turn, side, j] = value[row, 0:8]
                send_y[turn, side, :, j : j + 1, :] = value[0:8, row : row + 1]
        for k in range(4, 8):
            rows_x = low if DIRS[k][0] < 0 else high
            rows_y = low if DIRS[k][1] < 0 else high
            for i, row_x in enumerate(rows_x):
                for j, row_y in enumerate(rows_y):
                    send_d[turn, k - 4, i, j : j + 1, :] = value[row_x, row_y : row_y + 1]

    pack(0, res, (0, 1), (6, 7))
    first16 = lax.broadcasted_iota(jnp.int32, (8, 128), 1) < 16
    low = [jnp.where(first16, res[x], 0.0) for x in range(8)]
    packed = low[0]
    for x in range(1, 8):
        packed = packed + pltpu.roll(low[x], 16 * x, 1)
    slab_send[...] = packed
    row8 = lax.broadcasted_iota(jnp.int32, (8, 128), 0)
    for side, pair in enumerate(((0, 1), (6, 7))):
        for j, x in enumerate(pair):
            line = jnp.where(row8 == 0, low[x], 0.0)
            for y in range(1, 8):
                line = line + jnp.where(row8 == y, pltpu.roll(low[x], 16 * y, 1), 0.0)
            part_send[side, j : j + 1, :] = line.sum(axis=0, keepdims=True)

    def piece(k, arriving, held=False):
        dx, dy = (DIRS + [(0, 0)])[k]
        if k == 8:
            src, slot, dst = slab_send, 8, slab_recv
        else:
            slot = k if arriving else OPP[k]
            src = part_send.at[k] if k < 2 else slab_send.at[pl.ds(6 if dy > 0 else 0, 2)]
            dst = part_recv.at[slot]
        if held:
            dst = slab_held if k == 8 else part_held.at[HELD[k]]
        return pltpu.make_async_remote_copy(
            src_ref=src,
            dst_ref=dst,
            send_sem=piece_send.at[k],
            recv_sem=held_recv.at[HELD[k]] if held else piece_recv.at[slot],
            device_id=(1, 0, 0) if held else (ix + dx, iy + dy, iz + 1 if arriving else iz - 1),
            device_id_type=MESH,
        )

    def pass_piece(k):
        slot = 8 if k == 8 else OPP[k]
        return pltpu.make_async_remote_copy(
            src_ref=slab_held if k == 8 else part_held.at[HELD[k]],
            dst_ref=slab_recv if k == 8 else part_recv.at[slot],
            send_sem=held_send.at[HELD[k]],
            recv_sem=piece_recv.at[slot],
            device_id=(0, 0, 0),
            device_id_type=MESH,
        )

    for k in PIECES:
        @pl.when(below[k])
        def _(k=k):
            piece(k, False).start()

        if k in HELD:
            @pl.when(under[k] & from_origin[k])
            def _(k=k):
                piece(k, False, True).start()

    send_near(0, before_me)

    for load in loads[4:]:
        load.wait()
    eigen = jnp.concatenate(
        [
            ex[...].reshape(160, 16),
            eyf[...].reshape(160, 16),
            eyb[...].reshape(160, 16),
            ez[...].reshape(240, 16),
            el[...].reshape(48, 16),
        ],
        axis=0,
    )
    parts = thirds(eigen)
    wanted = lax.broadcasted_iota(jnp.int32, (8, 16), 0) * 15
    picks = jnp.where(lax.broadcasted_iota(jnp.int32, (8, 16), 1) == wanted, 1.0, 0.0).astype(BF16)
    ends = sum(dot(picks, part, ((1,), (1,))) for part in parts)
    fe_send[0] = ends[0:1]
    fe_send[1] = ends[1:2]

    def prepare(g):
        element, mode = lanes(g)
        spread = jnp.where(
            lax.broadcasted_iota(jnp.int32, (16, 128), 0) == element, 1.0, 0.0
        ).astype(BF16)
        table = sum(dot(part, spread) for part in parts)
        if g == 1:
            row = lax.broadcasted_iota(jnp.int32, (8, ROWS), 0)
            other = jnp.where(row == 0, fe_recv[0], jnp.where(row == 1, fe_recv[1], 0.0))
            far_row = lax.broadcasted_iota(jnp.int32, (8, 128), 0)
            spread_far = jnp.where(
                ((far_row == 0) & (element == -1)) | ((far_row == 1) & (element == 16)), 1.0, 0.0
            ).astype(BF16)
            far = sum(dot(part, spread_far, ((0,), (0,))) for part in thirds(other))
            table = table + far
        cm[g] = table
        for r in range(100):
            at = 16 * (r // 10) + r % 10
            cxb[g, r // 10, r % 10] = jnp.broadcast_to(cm[g, at : at + 1, :], (8, 128))
        tiles = jnp.zeros((24, 128), F32)
        for s in range(10):
            tiles = tiles + jnp.where(mode == s, cm[g, OZ + 24 * s : OZ + 24 * s + 24, :], 0.0)
        inner, lower, upper = tiles[0:8], tiles[8:16], tiles[16:24]
        columns = []
        for e in list(range(16)) + [-2, -1, 16, 17]:
            columns.append(
                jnp.where(
                    element == e,
                    inner,
                    jnp.where(element == e + 1, lower, jnp.where(element == e - 1, upper, 0.0)),
                )
            )
        wh[g], wl[g] = halves(jnp.concatenate(columns, axis=0))
        rate_z = jnp.where(
            lax.broadcasted_iota(jnp.int32, (16, 128), 0) == mode, cm[g, OL + 32 : OL + 48, :], 0.0
        ).sum(axis=0, keepdims=True)
        rate_yz = cm[g, OL + 16 : OL + 32, :] + rate_z
        for p in range(10):
            rate = rate_yz + cm[g, OL + p : OL + p + 1, :]
            some = rate > 0.0
            inv[g, p] = jnp.where(some, 1.0 / jnp.where(some, rate, 1.0), 0.0)

    def far_copy(kind, way, arriving):
        if kind == 0:
            src, dst = fe_send.at[1 - way], fe_recv.at[way]
        else:
            src, dst = fx_send.at[pl.ds(6, 10)], fx_recv.at[pl.ds(6, 10)]
        return pltpu.make_async_remote_copy(
            src_ref=src,
            dst_ref=dst,
            send_sem=far_send.at[kind, way],
            recv_sem=far_recv.at[kind, way],
            device_id=to_next if (way == 0) != arriving else to_prev,
            device_id_type=MESH,
        )

    def aside(passing):
        return pltpu.make_async_remote_copy(
            src_ref=pe if passing else fe_send.at[0],
            dst_ref=fe_recv.at[1] if passing else pe,
            send_sem=side_send if passing else far_send.at[0, 1],
            recv_sem=far_recv.at[0, 1] if passing else side_recv,
            device_id=(0, 0, 0) if passing else (1, 0, 0),
            device_id_type=MESH,
        )

    @pl.when(below[8])
    def _():
        far_copy(0, 1, False).start()

    @pl.when(after_origin)
    def _():
        aside(False).start()

    def send_up(kind):
        @pl.when(has_next)
        def _():
            far_copy(kind, 0, False).start()

    send_near(0, after_me)
    prepare(0)

    wait_near(0)

    def join(own, prev, after):
        return jnp.concatenate(
            [own[0:1] + prev[1:2], own[1:7], own[7:8] + after[0:1], prev[0:1], after[1:2]], axis=0
        )

    xs[:, 0:8, :] = join(res, recv_x[0, 0], recv_x[0, 1])
    before = join(recv_y[0, 0], recv_d[0, 0], recv_d[0, 2])
    behind = join(recv_y[0, 1], recv_d[0, 1], recv_d[0, 3])
    xs[:, 0:1, :] = xs[:, 0:1, :] + before[:, 1:2]
    xs[:, 7:8, :] = xs[:, 7:8, :] + behind[:, 0:1]
    xs[:, 8:9, :] = before[:, 0:1]
    xs[:, 9:10, :] = behind[:, 1:2]
    xc[0:80, :] = xs[:, 0:8, :].reshape(80, 128)
    for a in range(10):
        xc[80 + 2 * a : 82 + 2 * a, :] = xs[a, 8:10, :]
    turned = xc[...].T
    fx_send[...] = turned[112:128]

    nodes = halves(xs[...].reshape(160, 128))

    def to_modes(g):
        zs[g] = dot3(nodes, (wh[g, 0:128], wl[g, 0:128])).reshape(10, 16, 128)

    def solve(g):
        value = zs[g].reshape(10, 2, 8, 128)
        total = None
        for a in range(10):
            term = cxb[g, a][:, None] * value[a][None]
            total = term if total is None else total + term
        value, total = total, None
        for b in range(10):
            row = value[:, b // 8, b % 8 : b % 8 + 1, :][:, None]
            pick = cm[g, OYF + 16 * b : OYF + 16 * b + 16, :].reshape(1, 2, 8, 128)
            term = pick * row
            total = term if total is None else total + term
        value, total = total * inv[g].reshape(10, 2, 8, 128), None
        for q in range(10):
            row = value[:, q // 8, q % 8 : q % 8 + 1, :][:, None]
            pick = cm[g, OYB + 16 * q : OYB + 16 * q + 16, :].reshape(1, 2, 8, 128)
            term = pick * row
            total = term if total is None else total + term
        value, total = total, None
        for p in range(10):
            term = cxb[g, :, p][:, None] * value[p][None]
            total = term if total is None else total + term
        return dot3(
            halves(total.reshape(160, 128)), (wh[g, 0:128], wl[g, 0:128]), ((1,), (1,))
        )

    to_modes(0)

    @pl.when(has_next & ~origin)
    def _():
        pl.semaphore_wait(ready, 1)

    send_up(0)
    send_up(1)
    found = solve(0)

    @pl.when(helper)
    def _():
        aside(False).wait_recv()
        aside(True).start()

    @pl.when(has_next)
    def _():
        far_copy(0, 1, True).wait_recv()

    @pl.when(has_prev)
    def _():
        far_copy(0, 0, True).wait_recv()

    prepare(1)
    to_modes(1)

    @pl.when(helper)
    def _():
        for k in HELD:
            piece(k, False, True).wait_recv()
            pass_piece(k).start()

    @pl.when(has_prev)
    def _():
        far_copy(1, 0, True).wait_recv()

    for k in PIECES:
        @pl.when(over[k])
        def _(k=k):
            piece(k, True).wait_recv()

    def unpack(rows):
        return jnp.concatenate(
            [(pltpu.roll(rows, 128 - 16 * x, 1) if x else rows)[None] for x in range(8)], axis=0
        )

    own = unpack(slab_recv[...])
    sides = []
    for side in range(2):
        lines = []
        for j in range(2):
            line = jnp.broadcast_to(part_recv[side, j : j + 1, :], (8, 128))
            tile = jnp.where(row8 == 0, line, 0.0)
            for y in range(1, 8):
                tile = tile + jnp.where(row8 == y, pltpu.roll(line, 128 - 16 * y, 1), 0.0)
            lines.append(tile[None])
        sides.append(jnp.concatenate(lines, axis=0))
    for i in range(6):
        fan[2 * i : 2 * i + 2, :] = part_recv[2 + i]
    wide = unpack(fan[...])
    xf[:, 0:8, :] = join(own, sides[0], sides[1])
    before = join(wide[:, 0:2], wide[6:8, 4:6], wide[0:2, 8:10])
    behind = join(wide[:, 2:4], wide[6:8, 6:8], wide[0:2, 10:12])
    xf[:, 0:1, :] = xf[:, 0:1, :] + before[:, 1:2]
    xf[:, 7:8, :] = xf[:, 7:8, :] + behind[:, 0:1]
    xf[:, 8:9, :] = before[:, 0:1]
    xf[:, 9:10, :] = behind[:, 1:2]
    above = halves(xf[:, :, 0:16].reshape(160, 16))
    risen = dot3(above, (wh[1, 144:160], wl[1, 144:160])).reshape(10, 16, 128)

    beyond = halves(fx_recv[...])

    more = dot3(beyond, (wh[1, 128:144], wl[1, 128:144]), ((0,), (0,)))
    zs[1] = zs[1] + risen
    zs[1, :, 0:8, :] = zs[1, :, 0:8, :] + more[0:80].reshape(10, 8, 128)
    for a in range(10):
        zs[1, a, 8:10, :] = zs[1, a, 8:10, :] + more[80 + 2 * a : 82 + 2 * a]
    found = (found + solve(1)).reshape(10, 16, 128)
    pack(1, found, (8, 0), (7, 9))
    send_near(1, near)
    wait_near(1)

    def gather(own, prev, after):
        return jnp.concatenate([own[0:2] + prev, own[2:6], own[6:8] + after], axis=0)

    out_ref[...] = gather(found[0:8, 0:8], recv_x[1, 0], recv_x[1, 1])
    out_ref[:, 0:2, :] = out_ref[:, 0:2, :] + gather(recv_y[1, 0], recv_d[1, 0], recv_d[1, 2])
    out_ref[:, 6:8, :] = out_ref[:, 6:8, :] + gather(recv_y[1, 1], recv_d[1, 1], recv_d[1, 3])

    for turn in range(2):
        for k in range(8):
            @pl.when(near[k])
            def _(turn=turn, k=k):
                outgoing(turn, k).wait_send()

    for kind in range(2):
        @pl.when(has_next)
        def _(kind=kind):
            far_copy(kind, 0, False).wait_send()

    @pl.when(below[8])
    def _():
        far_copy(0, 1, False).wait_send()

    @pl.when(after_origin)
    def _():
        aside(False).wait_send()

    @pl.when(helper)
    def _():
        aside(True).wait_send()
        for k in HELD:
            pass_piece(k).wait_send()

    for k in PIECES:
        @pl.when(under[k])
        def _(k=k):
            piece(k, False).wait_send()


def solution(mesh):
    nx, ny, nz = mesh.shape["gx"], mesh.shape["gy"], mesh.shape["gz"]

    def body(initial, source, metric, eigenvectors, eigenvalues):
        hbm = pl.BlockSpec(memory_space=pl.ANY)
        vmem = pltpu.VMEM
        correction = pl.pallas_call(
            functools.partial(kernel, nx, ny, nz),
            out_shape=vmem((8, 8, 128), F32),
            in_specs=[hbm] * 6,
            out_specs=pl.BlockSpec(memory_space=vmem),
            scratch_shapes=[
                vmem((8, 8, 128), F32),
                vmem((8, 8, 128), F32),
                vmem((3, 8, 8, 128), F32),
                vmem((2, 448, 128), BF16),
                vmem((10, 16, 16), F32),
                vmem((10, 16, 16), F32),
                vmem((10, 16, 16), F32),
                vmem((10, 24, 16), F32),
                vmem((3, 16, 16), F32),
                pltpu.SemaphoreType.DMA((33,)),
                vmem((2, 2, 2, 8, 128), F32),
                vmem((2, 2, 8, 2, 128), F32),
                vmem((2, 4, 2, 2, 128), F32),
                vmem((2, 2, 2, 8, 128), F32),
                vmem((2, 2, 8, 2, 128), F32),
                vmem((2, 4, 2, 2, 128), F32),
                pltpu.SemaphoreType.DMA((2, 8)),
                pltpu.SemaphoreType.DMA((2, 8)),
                vmem((2, 1, ROWS), F32),
                vmem((2, 1, ROWS), F32),
                vmem((16, 128), F32),
                vmem((16, 128), F32),
                pltpu.SemaphoreType.DMA((2, 2)),
                pltpu.SemaphoreType.DMA((2, 2)),
                pltpu.SemaphoreType.REGULAR,
                pltpu.SemaphoreType.REGULAR((8,)),
                vmem((1, ROWS), F32),
                pltpu.SemaphoreType.DMA,
                pltpu.SemaphoreType.DMA,
                vmem((8, 128), F32),
                vmem((8, 128), F32),
                vmem((8, 128), F32),
                vmem((2, 2, 128), F32),
                vmem((8, 2, 128), F32),
                vmem((3, 2, 128), F32),
                pltpu.SemaphoreType.DMA((9,)),
                pltpu.SemaphoreType.DMA((9,)),
                pltpu.SemaphoreType.DMA((4,)),
                pltpu.SemaphoreType.DMA((4,)),
                vmem((10, 16, 128), F32),
                vmem((16, 128), F32),
                vmem((10, 16, 128), F32),
                vmem((128, 128), F32),
                vmem((2, ROWS, 128), F32),
                vmem((2, 10, 10, 8, 128), F32),
                vmem((2, 10, 16, 128), F32),
                vmem((2, 160, 128), BF16),
                vmem((2, 160, 128), BF16),
                vmem((2, 10, 16, 128), F32),
            ],
            compiler_params=pltpu.CompilerParams(collective_id=0, has_side_effects=True),
        )(
            initial,
            source,
            metric,
            eigenvectors,
            eigenvalues,
            jnp.asarray(operator_tables()),
        )
        return initial + correction

    placed = (
        P("gx", "gy", "gz"),
        P("gx", "gy", "gz"),
        P(None, "gx", "gy", "gz"),
        P(None, None, None, "gx", "gy", "gz"),
        P(None, None, "gx", "gy", "gz"),
    )
    return jax.shard_map(
        body, mesh=mesh, in_specs=placed, out_specs=P("gx", "gy", "gz"), check_vma=False
    )
```

```python
import functools

import jax
import jax.numpy as jnp
import numpy as np
from jax import lax
from jax.experimental import pallas as pl
from jax.experimental.pallas import tpu as pltpu
from jax.sharding import PartitionSpec as P

MESH = pl.DeviceIdType.MESH
F32 = jnp.float32
BF16 = jnp.bfloat16

gll_points = np.array(
    [
        -1.0,
        -0.8717401485096066,
        -0.5917001814331423,
        -0.2092992179024789,
        0.2092992179024789,
        0.5917001814331423,
        0.8717401485096066,
        1.0,
    ]
)

DIRS = [(-1, 0), (1, 0), (0, -1), (0, 1), (-1, -1), (-1, 1), (1, -1), (1, 1)]
OPP = [1, 0, 3, 2, 7, 6, 5, 4]
PIECES = [4, 6, 2, 5, 7, 3, 0, 1, 8]
HELD = {0: 0, 2: 1, 4: 2, 8: 3}
OYF, OYB, OZ, OL, ROWS = 160, 320, 480, 720, 768


def derivative_table():
    number = gll_points.shape[0]
    products = np.array(
        [
            np.prod([gll_points[i] - gll_points[k] for k in range(number) if k != i])
            for i in range(number)
        ]
    )
    table = np.zeros((number, number))
    for i in range(number):
        for j in range(number):
            if i != j:
                table[i, j] = products[i] / products[j] / (gll_points[i] - gll_points[j])
        table[i, i] = -np.sum(table[i])
    return table


def operator_tables():
    table = derivative_table().astype(np.float32)
    eye = np.eye(8, dtype=np.float32)
    left = np.concatenate([np.kron(table, eye), np.kron(eye, table)], axis=0)
    left = np.concatenate([left, np.zeros((128, 64), np.float32)], axis=1)
    left_t = np.ascontiguousarray(left.T[:64])
    right = np.kron(np.eye(16, dtype=np.float32), table.T)
    full = np.concatenate([left, left_t, right, right.T], axis=0)
    high = full.astype(jnp.bfloat16)
    low = (full - high.astype(np.float32)).astype(jnp.bfloat16)
    return np.stack([high, low])


def dot(a, b, dims=((1,), (0,))):
    return lax.dot_general(a, b, (dims, ((), ())), preferred_element_type=F32)


def halves(value):
    high = value.astype(BF16)
    return high, (value - high.astype(F32)).astype(BF16)


def thirds(value):
    high = value.astype(BF16)
    rest = value - high.astype(F32)
    mid = rest.astype(BF16)
    return high, mid, (rest - mid.astype(F32)).astype(BF16)


def dot3(a, b, dims=((1,), (0,))):
    return dot(a[0], b[0], dims) + (dot(a[1], b[0], dims) + dot(a[0], b[1], dims))


def lanes(group):
    lane = lax.broadcasted_iota(jnp.int32, (1, 128), 1)
    block = (lane * 205) >> 11
    mode = lane - 10 * block
    if group == 0:
        return jnp.where(lane < 120, block + 1, 99), mode
    ends = jnp.where(block < 2, block - 1, block + 11)
    return jnp.where(lane < 60, ends, 99), mode


def kernel(
    nx, ny, nz,
    u_h, f_h, m_h, eig_h, lam_h, cst_h, out_ref,
    u_v, f_v, m_v, cst_v, ex, eyf, eyb, ez, el, in_sem,
    send_x, send_y, send_d, recv_x, recv_y, recv_d, near_send, near_recv,
    fe_send, fe_recv, fx_send, fx_recv, far_send, far_recv, ready, near_ready, pe, side_send, side_recv,
    slab_send, slab_recv, slab_held, part_send, part_recv, part_held, piece_send, piece_recv, held_send, held_recv, xf, fan,
    xs, xc, cm, cxb, inv, wh, wl, zs,
):
    ix, iy, iz = lax.axis_index("gx"), lax.axis_index("gy"), lax.axis_index("gz")

    first = [(u_h, u_v), (cst_h, cst_v), (m_h, m_v), (f_h, f_v)]
    second = [
        (eig_h.at[0, 1:9, :, 0, 0], ex.at[0:8, 0:10]),
        (eig_h.at[0, 0, :, 0, 0], ex.at[8, 0:10]),
        (eig_h.at[0, 9, :, 0, 0], ex.at[9, 0:10]),
        (eig_h.at[1, 1:9, :, 0, 0], eyf.at[0:8, 0:10]),
        (eig_h.at[1, 0, :, 0, 0], eyf.at[8, 0:10]),
        (eig_h.at[1, 9, :, 0, 0], eyf.at[9, 0:10]),
        (lam_h.at[:, :, 0, 0], el.at[:, 0:10]),
    ]
    for row, pos in enumerate([1, 2, 3, 4, 5, 6, 7, 8, 0, 9]):
        second.append((eig_h.at[1, pos, :, 0, 0], eyb.at[:, row]))
    for row, pos in enumerate([1, 2, 3, 4, 5, 6, 7, 8]):
        second.append((eig_h.at[2, pos, :, 0, 0], ez.at[:, row]))
    for row, pos in [(14, 0), (15, 1), (16, 8), (17, 9)]:
        second.append((eig_h.at[2, pos, :, 0, 0], ez.at[:, row]))
    loads = [
        pltpu.make_async_copy(src, dst, in_sem.at[i])
        for i, (src, dst) in enumerate(first + second)
    ]
    for load in loads:
        load.start()

    recv_x[...] = jnp.zeros_like(recv_x)
    recv_y[...] = jnp.zeros_like(recv_y)
    recv_d[...] = jnp.zeros_like(recv_d)
    fe_recv[...] = jnp.zeros_like(fe_recv)
    fx_recv[...] = jnp.zeros_like(fx_recv)
    slab_recv[...] = jnp.zeros_like(slab_recv)
    part_recv[...] = jnp.zeros_like(part_recv)
    xf[...] = jnp.zeros_like(xf)
    fan[...] = jnp.zeros_like(fan)

    has_next, has_prev = iz < nz - 1, iz > 0
    to_next, to_prev = (ix, iy, iz + 1), (ix, iy, iz - 1)
    detour = nx > 1 and nz > 1
    in_line = (ix == 0) & (iy == 0)
    origin = in_line & (iz == 0) & detour
    after_origin = in_line & (iz == 1) & detour
    helper = (ix == 1) & (iy == 0) & (iz == 0) & detour
    near, target = [], []
    for dx, dy in DIRS:
        ok = None
        for cond in (
            [ix > 0] * (dx < 0) + [ix < nx - 1] * (dx > 0)
            + [iy > 0] * (dy < 0) + [iy < ny - 1] * (dy > 0)
        ):
            ok = cond if ok is None else ok & cond
        near.append(ok)
        target.append((ix + dx, iy + dy, iz))
    barrier = pltpu.get_barrier_semaphore()
    count = jnp.int32(0)
    later = []
    for dx, dy in DIRS:
        if dy > 0 or (dy == 0 and dx < 0):
            later.append(~origin)
        else:
            later.append(detour & (iz == 0) & (ix + dx == 0) & (iy + dy == 0))
    before_me = [ok & ~after for ok, after in zip(near, later)]
    after_me = [ok & after for ok, after in zip(near, later)]
    first_row = (iy == 0) & (iz == 0) & (nx > 2)
    greeted = list(zip(after_me, target)) + [
        (has_next & ~origin, to_next), (after_origin, (0, 0, 0)),
        (first_row & (ix == nx - 2), (nx - 1, iy, iz)),
    ]
    spot, half = iz * ny + iy, max(ny // 2, 1)
    relayed = nz > 2
    last, second = relayed & (iz == nz - 1), relayed & (iz == nz - 2)
    middle = relayed & (spot >= (nz - 2) * ny + half) & (spot < (nz - 1) * ny + half)
    down_spot, up_spot = jnp.maximum(spot - half, 0), spot + half
    half_down = (ix, down_spot % ny, down_spot // ny)
    half_up = (ix, up_spot % ny, up_spot // ny)
    greeted += [(last, half_down), (second, half_up)]
    over, under, from_origin = [], [], []
    for k, (dx, dy) in enumerate(DIRS + [(0, 0)]):
        inside = near[k] if k < 8 else (ix >= 0)
        over.append(has_next & inside)
        under.append(has_prev & inside)
        from_origin.append(detour & (iz == 1) & (ix + dx == 0) & (iy + dy == 0))
        if k < 8:
            greeted.append((over[k] & ~origin, (ix + dx, iy + dy, iz + 1)))
    for ok, device in greeted:
        @pl.when(ok)
        def _(device=device):
            pl.semaphore_signal(barrier, 1, device_id=device, device_id_type=MESH)
    count = jnp.int32(0)
    below = [ok & ~start for ok, start in zip(under, from_origin)]
    for ok in before_me + below + [origin, first_row & (ix == nx - 1)]:
        count = count + ok.astype(jnp.int32)
    count = count + 2 * middle.astype(jnp.int32)

    ex[:, 10:16, :] = jnp.zeros((10, 6, 16), F32)
    eyf[:, 10:16, :] = jnp.zeros((10, 6, 16), F32)
    eyb[:, 10:16, :] = jnp.zeros((10, 6, 16), F32)
    ez[:, 8:14, :] = jnp.zeros((10, 6, 16), F32)
    ez[:, 18:24, :] = jnp.zeros((10, 6, 16), F32)
    el[:, 10:16, :] = jnp.zeros((3, 6, 16), F32)
    xs[:, 10:16, :] = jnp.zeros((10, 6, 128), F32)
    xc[96:128, :] = jnp.zeros((32, 128), F32)

    pl.semaphore_wait(barrier, count)
    for k in range(8):
        @pl.when(before_me[k])
        def _(k=k):
            pl.semaphore_signal(
                near_ready.at[OPP[k]], 1, device_id=target[k], device_id_type=MESH
            )

    @pl.when(has_prev & ~after_origin & ~last)
    def _():
        pl.semaphore_signal(ready, 1, device_id=to_prev, device_id_type=MESH)

    @pl.when(middle)
    def _():
        pl.semaphore_signal(ready, 1, device_id=half_down, device_id_type=MESH)

    for load in loads[:4]:
        load.wait()
    field = halves(u_v[...].reshape(64, 128))
    left = cst_v[0, 0:128, 0:64], cst_v[1, 0:128, 0:64]
    left_t = cst_v[0, 128:192], cst_v[1, 128:192]
    right = cst_v[0, 192:320], cst_v[1, 192:320]
    right_t = cst_v[0, 320:448], cst_v[1, 320:448]
    flux = dot3(left, field) * m_v[0:2].reshape(128, 128)
    flux_z = dot3(field, right) * m_v[2].reshape(64, 128)
    applied = dot3(left_t, halves(flux)) + dot3(halves(flux_z), right_t)
    res = f_v[...] - applied.reshape(8, 8, 128)

    def recv_of(turn, k):
        if k < 2:
            return recv_x.at[turn, k]
        return recv_y.at[turn, k - 2] if k < 4 else recv_d.at[turn, k - 4]

    def send_of(turn, k):
        if k < 2:
            return send_x.at[turn, k]
        return send_y.at[turn, k - 2] if k < 4 else send_d.at[turn, k - 4]

    def outgoing(turn, k):
        return pltpu.make_async_remote_copy(
            src_ref=send_of(turn, k),
            dst_ref=recv_of(turn, OPP[k]),
            send_sem=near_send.at[turn, k],
            recv_sem=near_recv.at[turn, OPP[k]],
            device_id=target[k],
            device_id_type=MESH,
        )

    def incoming(turn, k):
        return pltpu.make_async_remote_copy(
            src_ref=send_of(turn, k),
            dst_ref=recv_of(turn, k),
            send_sem=near_send.at[turn, k],
            recv_sem=near_recv.at[turn, k],
            device_id=target[k],
            device_id_type=MESH,
        )

    ORDER = [4, 5, 6, 7, 0, 1, 2, 3]

    def send_near(turn, where):
        for k in ORDER:
            @pl.when(where[k])
            def _(k=k):
                if where is after_me:
                    pl.semaphore_wait(near_ready.at[k], 1)
                outgoing(turn, k).start()

    def wait_near(turn):
        for k in ORDER:
            @pl.when(near[k])
            def _(k=k):
                incoming(turn, k).wait_recv()

    def pack(turn, value, low, high):
        for side, rows in enumerate((low, high)):
            for j, row in enumerate(rows):
                send_x[turn, side, j] = value[row, 0:8]
                send_y[turn, side, :, j : j + 1, :] = value[0:8, row : row + 1]
        for k in range(4, 8):
            rows_x = low if DIRS[k][0] < 0 else high
            rows_y = low if DIRS[k][1] < 0 else high
            for i, row_x in enumerate(rows_x):
                for j, row_y in enumerate(rows_y):
                    send_d[turn, k - 4, i, j : j + 1, :] = value[row_x, row_y : row_y + 1]

    first16 = lax.broadcasted_iota(jnp.int32, (8, 128), 1) < 16
    low = [jnp.where(first16, res[x], 0.0) for x in range(8)]
    packed = low[0]
    for x in range(1, 8):
        packed = packed + pltpu.roll(low[x], 16 * x, 1)
    slab_send[...] = packed
    def piece(k, arriving, held=False):
        dx, dy = (DIRS + [(0, 0)])[k]
        if k == 8:
            src, slot, dst = slab_send, 8, slab_recv
        else:
            slot = k if arriving else OPP[k]
            src = part_send.at[k] if k < 2 else slab_send.at[pl.ds(6 if dy > 0 else 0, 2)]
            dst = part_recv.at[slot]
        if held:
            dst = slab_held if k == 8 else part_held.at[HELD[k]]
        return pltpu.make_async_remote_copy(
            src_ref=src,
            dst_ref=dst,
            send_sem=piece_send.at[k],
            recv_sem=held_recv.at[HELD[k]] if held else piece_recv.at[slot],
            device_id=(1, 0, 0) if held else (ix + dx, iy + dy, iz + 1 if arriving else iz - 1),
            device_id_type=MESH,
        )

    def pass_piece(k):
        slot = 8 if k == 8 else OPP[k]
        return pltpu.make_async_remote_copy(
            src_ref=slab_held if k == 8 else part_held.at[HELD[k]],
            dst_ref=slab_recv if k == 8 else part_recv.at[slot],
            send_sem=held_send.at[HELD[k]],
            recv_sem=piece_recv.at[slot],
            device_id=(0, 0, 0),
            device_id_type=MESH,
        )

    def send_pieces(pieces):
        for k in pieces:
            @pl.when(below[k])
            def _(k=k):
                piece(k, False).start()

            if k in HELD:
                @pl.when(under[k] & from_origin[k])
                def _(k=k):
                    piece(k, False, True).start()

    send_pieces([k for k in PIECES if k > 1])
    row8 = lax.broadcasted_iota(jnp.int32, (8, 128), 0)
    for side, pair in enumerate(((0, 1), (6, 7))):
        for j, x in enumerate(pair):
            line = jnp.where(row8 == 0, low[x], 0.0)
            for y in range(1, 8):
                line = line + jnp.where(row8 == y, pltpu.roll(low[x], 16 * y, 1), 0.0)
            part_send[side, j : j + 1, :] = line.sum(axis=0, keepdims=True)

    send_pieces([k for k in PIECES if k < 2])
    pack(0, res, (0, 1), (6, 7))
    send_near(0, before_me)

    for load in loads[4:]:
        load.wait()
    eigen = jnp.concatenate(
        [
            ex[...].reshape(160, 16),
            eyf[...].reshape(160, 16),
            eyb[...].reshape(160, 16),
            ez[...].reshape(240, 16),
            el[...].reshape(48, 16),
        ],
        axis=0,
    )
    parts = thirds(eigen)
    wanted = lax.broadcasted_iota(jnp.int32, (8, 16), 0) * 15
    picks = jnp.where(lax.broadcasted_iota(jnp.int32, (8, 16), 1) == wanted, 1.0, 0.0).astype(BF16)
    ends = sum(dot(picks, part, ((1,), (1,))) for part in parts)
    fe_send[0] = ends[0:1]
    fe_send[1] = ends[1:2]

    def prepare(g):
        element, mode = lanes(g)
        spread = jnp.where(
            lax.broadcasted_iota(jnp.int32, (16, 128), 0) == element, 1.0, 0.0
        ).astype(BF16)
        table = sum(dot(part, spread) for part in parts)
        if g == 1:
            row = lax.broadcasted_iota(jnp.int32, (8, ROWS), 0)
            other = jnp.where(row == 0, fe_recv[0], jnp.where(row == 1, fe_recv[1], 0.0))
            far_row = lax.broadcasted_iota(jnp.int32, (8, 128), 0)
            spread_far = jnp.where(
                ((far_row == 0) & (element == -1)) | ((far_row == 1) & (element == 16)), 1.0, 0.0
            ).astype(BF16)
            far = sum(dot(part, spread_far, ((0,), (0,))) for part in thirds(other))
            table = table + far
        cm[g] = table
        for r in range(100):
            at = 16 * (r // 10) + r % 10
            cxb[g, r // 10, r % 10] = jnp.broadcast_to(cm[g, at : at + 1, :], (8, 128))
        tiles = jnp.zeros((24, 128), F32)
        for s in range(10):
            tiles = tiles + jnp.where(mode == s, cm[g, OZ + 24 * s : OZ + 24 * s + 24, :], 0.0)
        inner, lower, upper = tiles[0:8], tiles[8:16], tiles[16:24]
        columns = []
        for e in list(range(16)) + [-2, -1, 16, 17]:
            columns.append(
                jnp.where(
                    element == e,
                    inner,
                    jnp.where(element == e + 1, lower, jnp.where(element == e - 1, upper, 0.0)),
                )
            )
        wh[g], wl[g] = halves(jnp.concatenate(columns, axis=0))
        rate_z = jnp.where(
            lax.broadcasted_iota(jnp.int32, (16, 128), 0) == mode, cm[g, OL + 32 : OL + 48, :], 0.0
        ).sum(axis=0, keepdims=True)
        rate_yz = cm[g, OL + 16 : OL + 32, :] + rate_z
        for p in range(10):
            rate = rate_yz + cm[g, OL + p : OL + p + 1, :]
            some = rate > 0.0
            inv[g, p] = jnp.where(some, 1.0 / jnp.where(some, rate, 1.0), 0.0)

    def far_copy(kind, way, arriving):
        if kind == 0:
            src, dst = fe_send.at[1 - way], fe_recv.at[way]
        else:
            src, dst = fx_send.at[pl.ds(6, 10)], fx_recv.at[pl.ds(6, 10)]
        return pltpu.make_async_remote_copy(
            src_ref=src,
            dst_ref=dst,
            send_sem=far_send.at[kind, way],
            recv_sem=far_recv.at[kind, way],
            device_id=to_next if (way == 0) != arriving else to_prev,
            device_id_type=MESH,
        )

    def aside(passing):
        return pltpu.make_async_remote_copy(
            src_ref=pe if passing else fe_send.at[0],
            dst_ref=fe_recv.at[1] if passing else pe,
            send_sem=side_send if passing else far_send.at[0, 1],
            recv_sem=far_recv.at[0, 1] if passing else side_recv,
            device_id=(0, 0, 0) if passing else (1, 0, 0),
            device_id_type=MESH,
        )

    @pl.when(below[8])
    def _():
        far_copy(0, 1, False).start()

    @pl.when(after_origin)
    def _():
        aside(False).start()

    def send_up(kind):
        @pl.when(has_next)
        def _():
            far_copy(kind, 0, False).start()

    send_near(0, after_me)
    prepare(0)

    wait_near(0)

    def join(own, prev, after):
        return jnp.concatenate(
            [own[0:1] + prev[1:2], own[1:7], own[7:8] + after[0:1], prev[0:1], after[1:2]], axis=0
        )

    xs[:, 0:8, :] = join(res, recv_x[0, 0], recv_x[0, 1])
    before = join(recv_y[0, 0], recv_d[0, 0], recv_d[0, 2])
    behind = join(recv_y[0, 1], recv_d[0, 1], recv_d[0, 3])
    xs[:, 0:1, :] = xs[:, 0:1, :] + before[:, 1:2]
    xs[:, 7:8, :] = xs[:, 7:8, :] + behind[:, 0:1]
    xs[:, 8:9, :] = before[:, 0:1]
    xs[:, 9:10, :] = behind[:, 1:2]
    xc[0:80, :] = xs[:, 0:8, :].reshape(80, 128)
    for a in range(10):
        xc[80 + 2 * a : 82 + 2 * a, :] = xs[a, 8:10, :]
    turned = xc[...].T
    fx_send[...] = turned[112:128]

    nodes = halves(xs[...].reshape(160, 128))

    def to_modes(g):
        zs[g] = dot3(nodes, (wh[g, 0:128], wl[g, 0:128])).reshape(10, 16, 128)

    def solve(g):
        value = zs[g].reshape(10, 2, 8, 128)
        total = None
        for a in range(10):
            term = cxb[g, a][:, None] * value[a][None]
            total = term if total is None else total + term
        value, total = total, None
        for b in range(10):
            row = value[:, b // 8, b % 8 : b % 8 + 1, :][:, None]
            pick = cm[g, OYF + 16 * b : OYF + 16 * b + 16, :].reshape(1, 2, 8, 128)
            term = pick * row
            total = term if total is None else total + term
        value, total = total * inv[g].reshape(10, 2, 8, 128), None
        for q in range(10):
            row = value[:, q // 8, q % 8 : q % 8 + 1, :][:, None]
            pick = cm[g, OYB + 16 * q : OYB + 16 * q + 16, :].reshape(1, 2, 8, 128)
            term = pick * row
            total = term if total is None else total + term
        value, total = total, None
        for p in range(10):
            term = cxb[g, :, p][:, None] * value[p][None]
            total = term if total is None else total + term
        return dot3(
            halves(total.reshape(160, 128)), (wh[g, 0:128], wl[g, 0:128]), ((1,), (1,))
        )

    to_modes(0)

    @pl.when(has_next & ~origin)
    def _():
        pl.semaphore_wait(ready, 1)

    send_up(0)
    send_up(1)
    found = solve(0)

    @pl.when(helper)
    def _():
        aside(False).wait_recv()
        aside(True).start()

    @pl.when(has_next)
    def _():
        far_copy(0, 1, True).wait_recv()

    @pl.when(has_prev)
    def _():
        far_copy(0, 0, True).wait_recv()

    prepare(1)
    to_modes(1)

    @pl.when(helper)
    def _():
        for k in HELD:
            piece(k, False, True).wait_recv()
            pass_piece(k).start()

    @pl.when(has_prev)
    def _():
        far_copy(1, 0, True).wait_recv()

    for k in PIECES:
        @pl.when(over[k])
        def _(k=k):
            piece(k, True).wait_recv()

    def unpack(rows):
        return jnp.concatenate(
            [(pltpu.roll(rows, 128 - 16 * x, 1) if x else rows)[None] for x in range(8)], axis=0
        )

    own = unpack(slab_recv[...])
    sides = []
    for side in range(2):
        lines = []
        for j in range(2):
            line = jnp.broadcast_to(part_recv[side, j : j + 1, :], (8, 128))
            tile = jnp.where(row8 == 0, line, 0.0)
            for y in range(1, 8):
                tile = tile + jnp.where(row8 == y, pltpu.roll(line, 128 - 16 * y, 1), 0.0)
            lines.append(tile[None])
        sides.append(jnp.concatenate(lines, axis=0))
    for i in range(6):
        fan[2 * i : 2 * i + 2, :] = part_recv[2 + i]
    wide = unpack(fan[...])
    xf[:, 0:8, :] = join(own, sides[0], sides[1])
    before = join(wide[:, 0:2], wide[6:8, 4:6], wide[0:2, 8:10])
    behind = join(wide[:, 2:4], wide[6:8, 6:8], wide[0:2, 10:12])
    xf[:, 0:1, :] = xf[:, 0:1, :] + before[:, 1:2]
    xf[:, 7:8, :] = xf[:, 7:8, :] + behind[:, 0:1]
    xf[:, 8:9, :] = before[:, 0:1]
    xf[:, 9:10, :] = behind[:, 1:2]
    above = halves(xf[:, :, 0:16].reshape(160, 16))
    risen = dot3(above, (wh[1, 144:160], wl[1, 144:160])).reshape(10, 16, 128)

    beyond = halves(fx_recv[...])

    more = dot3(beyond, (wh[1, 128:144], wl[1, 128:144]), ((0,), (0,)))
    zs[1] = zs[1] + risen
    zs[1, :, 0:8, :] = zs[1, :, 0:8, :] + more[0:80].reshape(10, 8, 128)
    for a in range(10):
        zs[1, a, 8:10, :] = zs[1, a, 8:10, :] + more[80 + 2 * a : 82 + 2 * a]
    found = (found + solve(1)).reshape(10, 16, 128)
    pack(1, found, (8, 0), (7, 9))
    send_near(1, near)

    for turn in range(2):
        for k in range(8):
            @pl.when(near[k])
            def _(turn=turn, k=k):
                outgoing(turn, k).wait_send()

    for kind in range(2):
        @pl.when(has_next)
        def _(kind=kind):
            far_copy(kind, 0, False).wait_send()

    @pl.when(below[8])
    def _():
        far_copy(0, 1, False).wait_send()

    @pl.when(after_origin)
    def _():
        aside(False).wait_send()

    @pl.when(helper)
    def _():
        aside(True).wait_send()
        for k in HELD:
            pass_piece(k).wait_send()

    for k in PIECES:
        @pl.when(under[k])
        def _(k=k):
            piece(k, False).wait_send()

    wait_near(1)

    def gather(own, prev, after):
        return jnp.concatenate([own[0:2] + prev, own[2:6], own[6:8] + after], axis=0)

    out_ref[...] = gather(found[0:8, 0:8], recv_x[1, 0], recv_x[1, 1])
    out_ref[:, 0:2, :] = out_ref[:, 0:2, :] + gather(recv_y[1, 0], recv_d[1, 0], recv_d[1, 2])
    out_ref[:, 6:8, :] = out_ref[:, 6:8, :] + gather(recv_y[1, 1], recv_d[1, 1], recv_d[1, 3])


def solution(mesh):
    nx, ny, nz = mesh.shape["gx"], mesh.shape["gy"], mesh.shape["gz"]

    def body(initial, source, metric, eigenvectors, eigenvalues):
        hbm = pl.BlockSpec(memory_space=pl.ANY)
        vmem = pltpu.VMEM
        correction = pl.pallas_call(
            functools.partial(kernel, nx, ny, nz),
            out_shape=vmem((8, 8, 128), F32),
            in_specs=[hbm] * 6,
            out_specs=pl.BlockSpec(memory_space=vmem),
            scratch_shapes=[
                vmem((8, 8, 128), F32),
                vmem((8, 8, 128), F32),
                vmem((3, 8, 8, 128), F32),
                vmem((2, 448, 128), BF16),
                vmem((10, 16, 16), F32),
                vmem((10, 16, 16), F32),
                vmem((10, 16, 16), F32),
                vmem((10, 24, 16), F32),
                vmem((3, 16, 16), F32),
                pltpu.SemaphoreType.DMA((33,)),
                vmem((2, 2, 2, 8, 128), F32),
                vmem((2, 2, 8, 2, 128), F32),
                vmem((2, 4, 2, 2, 128), F32),
                vmem((2, 2, 2, 8, 128), F32),
                vmem((2, 2, 8, 2, 128), F32),
                vmem((2, 4, 2, 2, 128), F32),
                pltpu.SemaphoreType.DMA((2, 8)),
                pltpu.SemaphoreType.DMA((2, 8)),
                vmem((2, 1, ROWS), F32),
                vmem((2, 1, ROWS), F32),
                vmem((16, 128), F32),
                vmem((16, 128), F32),
                pltpu.SemaphoreType.DMA((2, 2)),
                pltpu.SemaphoreType.DMA((2, 2)),
                pltpu.SemaphoreType.REGULAR,
                pltpu.SemaphoreType.REGULAR((8,)),
                vmem((1, ROWS), F32),
                pltpu.SemaphoreType.DMA,
                pltpu.SemaphoreType.DMA,
                vmem((8, 128), F32),
                vmem((8, 128), F32),
                vmem((8, 128), F32),
                vmem((2, 2, 128), F32),
                vmem((8, 2, 128), F32),
                vmem((3, 2, 128), F32),
                pltpu.SemaphoreType.DMA((9,)),
                pltpu.SemaphoreType.DMA((9,)),
                pltpu.SemaphoreType.DMA((4,)),
                pltpu.SemaphoreType.DMA((4,)),
                vmem((10, 16, 128), F32),
                vmem((16, 128), F32),
                vmem((10, 16, 128), F32),
                vmem((128, 128), F32),
                vmem((2, ROWS, 128), F32),
                vmem((2, 10, 10, 8, 128), F32),
                vmem((2, 10, 16, 128), F32),
                vmem((2, 160, 128), BF16),
                vmem((2, 160, 128), BF16),
                vmem((2, 10, 16, 128), F32),
            ],
            compiler_params=pltpu.CompilerParams(collective_id=0, has_side_effects=True),
        )(
            initial,
            source,
            metric,
            eigenvectors,
            eigenvalues,
            jnp.asarray(operator_tables()),
        )
        return initial + correction

    placed = (
        P("gx", "gy", "gz"),
        P("gx", "gy", "gz"),
        P(None, "gx", "gy", "gz"),
        P(None, None, None, "gx", "gy", "gz"),
        P(None, None, "gx", "gy", "gz"),
    )
    return jax.shard_map(
        body, mesh=mesh, in_specs=placed, out_specs=P("gx", "gy", "gz"), check_vma=False
    )
```

```python
import functools

import jax
import jax.numpy as jnp
import numpy as np
from jax import lax
from jax.experimental import pallas as pl
from jax.experimental.pallas import tpu as pltpu
from jax.sharding import PartitionSpec as P

MESH = pl.DeviceIdType.MESH
F32 = jnp.float32
BF16 = jnp.bfloat16

gll_points = np.array(
    [
        -1.0,
        -0.8717401485096066,
        -0.5917001814331423,
        -0.2092992179024789,
        0.2092992179024789,
        0.5917001814331423,
        0.8717401485096066,
        1.0,
    ]
)

DIRS = [(-1, 0), (1, 0), (0, -1), (0, 1), (-1, -1), (-1, 1), (1, -1), (1, 1)]
OPP = [1, 0, 3, 2, 7, 6, 5, 4]
PIECES = [4, 6, 2, 5, 7, 3, 0, 1, 8]
HELD = {0: 0, 2: 1, 4: 2, 8: 3}
OYF, OYB, OZ, OL, ROWS = 160, 320, 480, 720, 768


def derivative_table():
    number = gll_points.shape[0]
    products = np.array(
        [
            np.prod([gll_points[i] - gll_points[k] for k in range(number) if k != i])
            for i in range(number)
        ]
    )
    table = np.zeros((number, number))
    for i in range(number):
        for j in range(number):
            if i != j:
                table[i, j] = products[i] / products[j] / (gll_points[i] - gll_points[j])
        table[i, i] = -np.sum(table[i])
    return table


def operator_tables():
    table = derivative_table().astype(np.float32)
    eye = np.eye(8, dtype=np.float32)
    left = np.concatenate([np.kron(table, eye), np.kron(eye, table)], axis=0)
    left = np.concatenate([left, np.zeros((128, 64), np.float32)], axis=1)
    left_t = np.ascontiguousarray(left.T[:64])
    right = np.kron(np.eye(16, dtype=np.float32), table.T)
    full = np.concatenate([left, left_t, right, right.T], axis=0)
    high = full.astype(jnp.bfloat16)
    low = (full - high.astype(np.float32)).astype(jnp.bfloat16)
    return np.stack([high, low])


def dot(a, b, dims=((1,), (0,))):
    return lax.dot_general(a, b, (dims, ((), ())), preferred_element_type=F32)


def halves(value):
    high = value.astype(BF16)
    return high, (value - high.astype(F32)).astype(BF16)


def thirds(value):
    high = value.astype(BF16)
    rest = value - high.astype(F32)
    mid = rest.astype(BF16)
    return high, mid, (rest - mid.astype(F32)).astype(BF16)


def dot3(a, b, dims=((1,), (0,))):
    return dot(a[0], b[0], dims) + (dot(a[1], b[0], dims) + dot(a[0], b[1], dims))


def lanes(group):
    lane = lax.broadcasted_iota(jnp.int32, (1, 128), 1)
    block = (lane * 205) >> 11
    mode = lane - 10 * block
    if group == 0:
        return jnp.where(lane < 120, block + 1, 99), mode
    ends = jnp.where(block < 2, block - 1, block + 11)
    return jnp.where(lane < 60, ends, 99), mode


def kernel(
    nx, ny, nz,
    u_h, f_h, m_h, eig_h, lam_h, cst_h, out_ref,
    u_v, f_v, m_v, cst_v, ex, eyf, eyb, ez, el, in_sem,
    send_x, send_y, send_d, recv_x, recv_y, recv_d, near_send, near_recv,
    fe_send, fe_recv, fx_send, fx_recv, far_send, far_recv, ready, near_ready, pe, side_send, side_recv,
    slab_send, slab_recv, slab_held, part_send, part_recv, part_held, piece_send, piece_recv, held_send, held_recv, xf, fan,
    xs, xc, cm, cxb, inv, wh, wl, zs,
):
    ix, iy, iz = lax.axis_index("gx"), lax.axis_index("gy"), lax.axis_index("gz")

    first = [(u_h, u_v), (cst_h, cst_v), (m_h, m_v), (f_h, f_v)]
    second = [
        (eig_h.at[0, 1:9, :, 0, 0], ex.at[0:8, 0:10]),
        (eig_h.at[0, 0, :, 0, 0], ex.at[8, 0:10]),
        (eig_h.at[0, 9, :, 0, 0], ex.at[9, 0:10]),
        (eig_h.at[1, 1:9, :, 0, 0], eyf.at[0:8, 0:10]),
        (eig_h.at[1, 0, :, 0, 0], eyf.at[8, 0:10]),
        (eig_h.at[1, 9, :, 0, 0], eyf.at[9, 0:10]),
        (lam_h.at[:, :, 0, 0], el.at[:, 0:10]),
    ]
    for row, pos in enumerate([1, 2, 3, 4, 5, 6, 7, 8, 0, 9]):
        second.append((eig_h.at[1, pos, :, 0, 0], eyb.at[:, row]))
    for row, pos in enumerate([1, 2, 3, 4, 5, 6, 7, 8]):
        second.append((eig_h.at[2, pos, :, 0, 0], ez.at[:, row]))
    for row, pos in [(14, 0), (15, 1), (16, 8), (17, 9)]:
        second.append((eig_h.at[2, pos, :, 0, 0], ez.at[:, row]))
    loads = [
        pltpu.make_async_copy(src, dst, in_sem.at[i])
        for i, (src, dst) in enumerate(first + second)
    ]
    for load in loads:
        load.start()

    recv_x[...] = jnp.zeros_like(recv_x)
    recv_y[...] = jnp.zeros_like(recv_y)
    recv_d[...] = jnp.zeros_like(recv_d)
    fe_recv[...] = jnp.zeros_like(fe_recv)
    fx_recv[...] = jnp.zeros_like(fx_recv)
    slab_recv[...] = jnp.zeros_like(slab_recv)
    part_recv[...] = jnp.zeros_like(part_recv)

    has_next, has_prev = iz < nz - 1, iz > 0
    to_next, to_prev = (ix, iy, iz + 1), (ix, iy, iz - 1)
    detour = nx > 1 and nz > 1
    in_line = (ix == 0) & (iy == 0)
    origin = in_line & (iz == 0) & detour
    after_origin = in_line & (iz == 1) & detour
    helper = (ix == 1) & (iy == 0) & (iz == 0) & detour
    near, target = [], []
    for dx, dy in DIRS:
        ok = None
        for cond in (
            [ix > 0] * (dx < 0) + [ix < nx - 1] * (dx > 0)
            + [iy > 0] * (dy < 0) + [iy < ny - 1] * (dy > 0)
        ):
            ok = cond if ok is None else ok & cond
        near.append(ok)
        target.append((ix + dx, iy + dy, iz))
    barrier = pltpu.get_barrier_semaphore()
    count = jnp.int32(0)
    later = []
    for dx, dy in DIRS:
        if dy > 0 or (dy == 0 and dx < 0):
            later.append(~origin)
        else:
            later.append(detour & (iz == 0) & (ix + dx == 0) & (iy + dy == 0))
    beside = [near[k] & (iz > 0) & (iy < ny - 1) & (DIRS[k][1] == 0) for k in range(8)]
    before_me = [ok & ~after & ~x for ok, after, x in zip(near, later, beside)]
    after_me = [ok & after & ~x for ok, after, x in zip(near, later, beside)]
    first_row = (iy == 0) & (iz == 0) & (nx > 2)
    greeted = list(zip(after_me, target)) + [
        (has_next & ~origin, to_next), (after_origin, (0, 0, 0)),
        (first_row & (ix == nx - 2), (nx - 1, iy, iz)),
    ]
    spot, half = iz * ny + iy, max(ny // 2, 1)
    relayed = nz > 2
    last, second = relayed & (iz == nz - 1), relayed & (iz == nz - 2)
    middle = relayed & (spot >= (nz - 2) * ny + half) & (spot < (nz - 1) * ny + half)
    down_spot, up_spot = jnp.maximum(spot - half, 0), spot + half
    half_down = (ix, down_spot % ny, down_spot // ny)
    half_up = (ix, up_spot % ny, up_spot // ny)
    greeted += [(last, half_down), (second, half_up)]
    over, under, from_origin = [], [], []
    for k, (dx, dy) in enumerate(DIRS + [(0, 0)]):
        inside = near[k] if k < 8 else (ix >= 0)
        over.append(has_next & inside)
        under.append(has_prev & inside)
        from_origin.append(detour & (iz == 1) & (ix + dx == 0) & (iy + dy == 0))
        if k < 8:
            greeted.append((over[k] & ~origin, (ix + dx, iy + dy, iz + 1)))
    for ok, device in greeted:
        @pl.when(ok)
        def _(device=device):
            pl.semaphore_signal(barrier, 1, device_id=device, device_id_type=MESH)
    count = jnp.int32(0)
    below = [ok & ~start for ok, start in zip(under, from_origin)]
    for ok in before_me + below + [origin, first_row & (ix == nx - 1)]:
        count = count + ok.astype(jnp.int32)
    count = count + 2 * middle.astype(jnp.int32)

    xf[...] = jnp.zeros_like(xf)
    fan[...] = jnp.zeros_like(fan)
    ex[:, 10:16, :] = jnp.zeros((10, 6, 16), F32)
    eyf[:, 10:16, :] = jnp.zeros((10, 6, 16), F32)
    eyb[:, 10:16, :] = jnp.zeros((10, 6, 16), F32)
    ez[:, 8:14, :] = jnp.zeros((10, 6, 16), F32)
    ez[:, 18:24, :] = jnp.zeros((10, 6, 16), F32)
    el[:, 10:16, :] = jnp.zeros((3, 6, 16), F32)
    xs[:, 10:16, :] = jnp.zeros((10, 6, 128), F32)
    xc[96:128, :] = jnp.zeros((32, 128), F32)

    for load in loads[:4]:
        load.wait()
    field = halves(u_v[...].reshape(64, 128))
    left = cst_v[0, 0:128, 0:64], cst_v[1, 0:128, 0:64]
    left_t = cst_v[0, 128:192], cst_v[1, 128:192]
    right = cst_v[0, 192:320], cst_v[1, 192:320]
    right_t = cst_v[0, 320:448], cst_v[1, 320:448]
    flux = dot3(left, field) * m_v[0:2].reshape(128, 128)
    flux_z = dot3(field, right) * m_v[2].reshape(64, 128)
    applied = dot3(left_t, halves(flux)) + dot3(halves(flux_z), right_t)
    res = f_v[...] - applied.reshape(8, 8, 128)

    def recv_of(turn, k):
        if k < 2:
            return recv_x.at[turn, k]
        return recv_y.at[turn, k - 2] if k < 4 else recv_d.at[turn, k - 4]

    def send_of(turn, k):
        if k < 2:
            return send_x.at[turn, k]
        return send_y.at[turn, k - 2] if k < 4 else send_d.at[turn, k - 4]

    def outgoing(turn, k):
        return pltpu.make_async_remote_copy(
            src_ref=send_of(turn, k),
            dst_ref=recv_of(turn, OPP[k]),
            send_sem=near_send.at[turn, k],
            recv_sem=near_recv.at[turn, OPP[k]],
            device_id=target[k],
            device_id_type=MESH,
        )

    def incoming(turn, k):
        return pltpu.make_async_remote_copy(
            src_ref=send_of(turn, k),
            dst_ref=recv_of(turn, k),
            send_sem=near_send.at[turn, k],
            recv_sem=near_recv.at[turn, k],
            device_id=target[k],
            device_id_type=MESH,
        )

    ORDER = [4, 5, 6, 7, 0, 1, 2, 3]

    def send_near(turn, where):
        for k in ORDER:
            @pl.when(where[k])
            def _(k=k):
                if where is after_me:
                    pl.semaphore_wait(near_ready.at[k], 1)
                outgoing(turn, k).start()

    def wait_near(turn):
        for k in ORDER:
            @pl.when(near[k])
            def _(k=k):
                incoming(turn, k).wait_recv()

    def pack(turn, value, low, high):
        for side, rows in enumerate((low, high)):
            for j, row in enumerate(rows):
                send_x[turn, side, j] = value[row, 0:8]
                send_y[turn, side, :, j : j + 1, :] = value[0:8, row : row + 1]
        for k in range(4, 8):
            rows_x = low if DIRS[k][0] < 0 else high
            rows_y = low if DIRS[k][1] < 0 else high
            for i, row_x in enumerate(rows_x):
                for j, row_y in enumerate(rows_y):
                    send_d[turn, k - 4, i, j : j + 1, :] = value[row_x, row_y : row_y + 1]

    first16 = lax.broadcasted_iota(jnp.int32, (8, 128), 1) < 16
    low = [jnp.where(first16, res[x], 0.0) for x in range(8)]
    packed = low[0]
    for x in range(1, 8):
        packed = packed + pltpu.roll(low[x], 16 * x, 1)
    slab_send[...] = packed
    def piece(k, arriving, held=False):
        dx, dy = (DIRS + [(0, 0)])[k]
        if k == 8:
            src, slot, dst = slab_send, 8, slab_recv
        else:
            slot = k if arriving else OPP[k]
            src = part_send.at[k] if k < 2 else slab_send.at[pl.ds(6 if dy > 0 else 0, 2)]
            dst = part_recv.at[slot]
        if held:
            dst = slab_held if k == 8 else part_held.at[HELD[k]]
        return pltpu.make_async_remote_copy(
            src_ref=src,
            dst_ref=dst,
            send_sem=piece_send.at[k],
            recv_sem=held_recv.at[HELD[k]] if held else piece_recv.at[slot],
            device_id=(1, 0, 0) if held else (ix + dx, iy + dy, iz + 1 if arriving else iz - 1),
            device_id_type=MESH,
        )

    def pass_piece(k):
        slot = 8 if k == 8 else OPP[k]
        return pltpu.make_async_remote_copy(
            src_ref=slab_held if k == 8 else part_held.at[HELD[k]],
            dst_ref=slab_recv if k == 8 else part_recv.at[slot],
            send_sem=held_send.at[HELD[k]],
            recv_sem=piece_recv.at[slot],
            device_id=(0, 0, 0),
            device_id_type=MESH,
        )

    def send_pieces(pieces):
        for k in pieces:
            @pl.when(below[k])
            def _(k=k):
                piece(k, False).start()

            if k in HELD:
                @pl.when(under[k] & from_origin[k])
                def _(k=k):
                    piece(k, False, True).start()

    pl.semaphore_wait(barrier, count)
    send_pieces([k for k in PIECES if k > 1])
    for k in range(8):
        @pl.when(before_me[k])
        def _(k=k):
            pl.semaphore_signal(
                near_ready.at[OPP[k]], 1, device_id=target[k], device_id_type=MESH
            )

    @pl.when(has_prev & ~after_origin & ~last)
    def _():
        pl.semaphore_signal(ready, 1, device_id=to_prev, device_id_type=MESH)

    @pl.when(middle)
    def _():
        pl.semaphore_signal(ready, 1, device_id=half_down, device_id_type=MESH)

    row8 = lax.broadcasted_iota(jnp.int32, (8, 128), 0)
    for side, pair in enumerate(((0, 1), (6, 7))):
        for j, x in enumerate(pair):
            line = jnp.where(row8 == 0, low[x], 0.0)
            for y in range(1, 8):
                line = line + jnp.where(row8 == y, pltpu.roll(low[x], 16 * y, 1), 0.0)
            part_send[side, j : j + 1, :] = line.sum(axis=0, keepdims=True)

    send_pieces([k for k in PIECES if k < 2])
    pack(0, res, (0, 1), (6, 7))
    send_near(0, before_me)

    for load in loads[4:]:
        load.wait()
    eigen = jnp.concatenate(
        [
            ex[...].reshape(160, 16),
            eyf[...].reshape(160, 16),
            eyb[...].reshape(160, 16),
            ez[...].reshape(240, 16),
            el[...].reshape(48, 16),
        ],
        axis=0,
    )
    parts = thirds(eigen)
    wanted = lax.broadcasted_iota(jnp.int32, (8, 16), 0) * 15
    picks = jnp.where(lax.broadcasted_iota(jnp.int32, (8, 16), 1) == wanted, 1.0, 0.0).astype(BF16)
    ends = sum(dot(picks, part, ((1,), (1,))) for part in parts)
    fe_send[0] = ends[0:1]
    fe_send[1] = ends[1:2]

    def prepare(g):
        element, mode = lanes(g)
        spread = jnp.where(
            lax.broadcasted_iota(jnp.int32, (16, 128), 0) == element, 1.0, 0.0
        ).astype(BF16)
        table = sum(dot(part, spread) for part in parts)
        if g == 1:
            row = lax.broadcasted_iota(jnp.int32, (8, ROWS), 0)
            other = jnp.where(row == 0, fe_recv[0], jnp.where(row == 1, fe_recv[1], 0.0))
            far_row = lax.broadcasted_iota(jnp.int32, (8, 128), 0)
            spread_far = jnp.where(
                ((far_row == 0) & (element == -1)) | ((far_row == 1) & (element == 16)), 1.0, 0.0
            ).astype(BF16)
            far = sum(dot(part, spread_far, ((0,), (0,))) for part in thirds(other))
            table = table + far
        cm[g] = table
        for r in range(100):
            at = 16 * (r // 10) + r % 10
            cxb[g, r // 10, r % 10] = jnp.broadcast_to(cm[g, at : at + 1, :], (8, 128))
        tiles = jnp.zeros((24, 128), F32)
        for s in range(10):
            tiles = tiles + jnp.where(mode == s, cm[g, OZ + 24 * s : OZ + 24 * s + 24, :], 0.0)
        inner, lower, upper = tiles[0:8], tiles[8:16], tiles[16:24]
        columns = []
        for e in list(range(16)) + [-2, -1, 16, 17]:
            columns.append(
                jnp.where(
                    element == e,
                    inner,
                    jnp.where(element == e + 1, lower, jnp.where(element == e - 1, upper, 0.0)),
                )
            )
        wh[g], wl[g] = halves(jnp.concatenate(columns, axis=0))
        rate_z = jnp.where(
            lax.broadcasted_iota(jnp.int32, (16, 128), 0) == mode, cm[g, OL + 32 : OL + 48, :], 0.0
        ).sum(axis=0, keepdims=True)
        rate_yz = cm[g, OL + 16 : OL + 32, :] + rate_z
        for p in range(10):
            rate = rate_yz + cm[g, OL + p : OL + p + 1, :]
            some = rate > 0.0
            inv[g, p] = jnp.where(some, 1.0 / jnp.where(some, rate, 1.0), 0.0)

    def far_copy(kind, way, arriving):
        if kind == 0:
            src, dst = fe_send.at[1 - way], fe_recv.at[way]
        else:
            src, dst = fx_send.at[pl.ds(6, 10)], fx_recv.at[pl.ds(6, 10)]
        return pltpu.make_async_remote_copy(
            src_ref=src,
            dst_ref=dst,
            send_sem=far_send.at[kind, way],
            recv_sem=far_recv.at[kind, way],
            device_id=to_next if (way == 0) != arriving else to_prev,
            device_id_type=MESH,
        )

    def aside(passing):
        return pltpu.make_async_remote_copy(
            src_ref=pe if passing else fe_send.at[0],
            dst_ref=fe_recv.at[1] if passing else pe,
            send_sem=side_send if passing else far_send.at[0, 1],
            recv_sem=far_recv.at[0, 1] if passing else side_recv,
            device_id=(0, 0, 0) if passing else (1, 0, 0),
            device_id_type=MESH,
        )

    @pl.when(below[8])
    def _():
        far_copy(0, 1, False).start()

    @pl.when(after_origin)
    def _():
        aside(False).start()

    def send_up(kind):
        @pl.when(has_next)
        def _():
            far_copy(kind, 0, False).start()

    send_near(0, after_me)
    send_near(0, beside)
    prepare(0)

    wait_near(0)

    def join(own, prev, after):
        return jnp.concatenate(
            [own[0:1] + prev[1:2], own[1:7], own[7:8] + after[0:1], prev[0:1], after[1:2]], axis=0
        )

    xs[:, 0:8, :] = join(res, recv_x[0, 0], recv_x[0, 1])
    before = join(recv_y[0, 0], recv_d[0, 0], recv_d[0, 2])
    behind = join(recv_y[0, 1], recv_d[0, 1], recv_d[0, 3])
    xs[:, 0:1, :] = xs[:, 0:1, :] + before[:, 1:2]
    xs[:, 7:8, :] = xs[:, 7:8, :] + behind[:, 0:1]
    xs[:, 8:9, :] = before[:, 0:1]
    xs[:, 9:10, :] = behind[:, 1:2]
    xc[0:80, :] = xs[:, 0:8, :].reshape(80, 128)
    for a in range(10):
        xc[80 + 2 * a : 82 + 2 * a, :] = xs[a, 8:10, :]
    turned = xc[...].T
    fx_send[...] = turned[112:128]

    nodes = halves(xs[...].reshape(160, 128))

    def to_modes(g):
        zs[g] = dot3(nodes, (wh[g, 0:128], wl[g, 0:128])).reshape(10, 16, 128)

    def solve(g):
        value = zs[g].reshape(10, 2, 8, 128)
        total = None
        for a in range(10):
            term = cxb[g, a][:, None] * value[a][None]
            total = term if total is None else total + term
        value, total = total, None
        for b in range(10):
            row = value[:, b // 8, b % 8 : b % 8 + 1, :][:, None]
            pick = cm[g, OYF + 16 * b : OYF + 16 * b + 16, :].reshape(1, 2, 8, 128)
            term = pick * row
            total = term if total is None else total + term
        value, total = total * inv[g].reshape(10, 2, 8, 128), None
        for q in range(10):
            row = value[:, q // 8, q % 8 : q % 8 + 1, :][:, None]
            pick = cm[g, OYB + 16 * q : OYB + 16 * q + 16, :].reshape(1, 2, 8, 128)
            term = pick * row
            total = term if total is None else total + term
        value, total = total, None
        for p in range(10):
            term = cxb[g, :, p][:, None] * value[p][None]
            total = term if total is None else total + term
        return dot3(
            halves(total.reshape(160, 128)), (wh[g, 0:128], wl[g, 0:128]), ((1,), (1,))
        )

    to_modes(0)

    @pl.when(has_next & ~origin)
    def _():
        pl.semaphore_wait(ready, 1)

    send_up(0)
    send_up(1)
    found = solve(0)

    @pl.when(helper)
    def _():
        aside(False).wait_recv()
        aside(True).start()

    @pl.when(has_next)
    def _():
        far_copy(0, 1, True).wait_recv()

    @pl.when(has_prev)
    def _():
        far_copy(0, 0, True).wait_recv()

    prepare(1)
    to_modes(1)

    @pl.when(helper)
    def _():
        for k in HELD:
            piece(k, False, True).wait_recv()
            pass_piece(k).start()

    @pl.when(has_prev)
    def _():
        far_copy(1, 0, True).wait_recv()

    for k in PIECES:
        @pl.when(over[k])
        def _(k=k):
            piece(k, True).wait_recv()

    def unpack(rows):
        return jnp.concatenate(
            [(pltpu.roll(rows, 128 - 16 * x, 1) if x else rows)[None] for x in range(8)], axis=0
        )

    own = unpack(slab_recv[...])
    sides = []
    for side in range(2):
        lines = []
        for j in range(2):
            line = jnp.broadcast_to(part_recv[side, j : j + 1, :], (8, 128))
            tile = jnp.where(row8 == 0, line, 0.0)
            for y in range(1, 8):
                tile = tile + jnp.where(row8 == y, pltpu.roll(line, 128 - 16 * y, 1), 0.0)
            lines.append(tile[None])
        sides.append(jnp.concatenate(lines, axis=0))
    for i in range(6):
        fan[2 * i : 2 * i + 2, :] = part_recv[2 + i]
    wide = unpack(fan[...])
    xf[:, 0:8, :] = join(own, sides[0], sides[1])
    before = join(wide[:, 0:2], wide[6:8, 4:6], wide[0:2, 8:10])
    behind = join(wide[:, 2:4], wide[6:8, 6:8], wide[0:2, 10:12])
    xf[:, 0:1, :] = xf[:, 0:1, :] + before[:, 1:2]
    xf[:, 7:8, :] = xf[:, 7:8, :] + behind[:, 0:1]
    xf[:, 8:9, :] = before[:, 0:1]
    xf[:, 9:10, :] = behind[:, 1:2]
    above = halves(xf[:, :, 0:16].reshape(160, 16))
    risen = dot3(above, (wh[1, 144:160], wl[1, 144:160])).reshape(10, 16, 128)

    beyond = halves(fx_recv[...])

    more = dot3(beyond, (wh[1, 128:144], wl[1, 128:144]), ((0,), (0,)))
    zs[1] = zs[1] + risen
    zs[1, :, 0:8, :] = zs[1, :, 0:8, :] + more[0:80].reshape(10, 8, 128)
    for a in range(10):
        zs[1, a, 8:10, :] = zs[1, a, 8:10, :] + more[80 + 2 * a : 82 + 2 * a]
    found = (found + solve(1)).reshape(10, 16, 128)
    pack(1, found, (8, 0), (7, 9))
    send_near(1, near)

    for turn in range(2):
        for k in range(8):
            @pl.when(near[k])
            def _(turn=turn, k=k):
                outgoing(turn, k).wait_send()

    for kind in range(2):
        @pl.when(has_next)
        def _(kind=kind):
            far_copy(kind, 0, False).wait_send()

    @pl.when(below[8])
    def _():
        far_copy(0, 1, False).wait_send()

    @pl.when(after_origin)
    def _():
        aside(False).wait_send()

    @pl.when(helper)
    def _():
        aside(True).wait_send()
        for k in HELD:
            pass_piece(k).wait_send()

    for k in PIECES:
        @pl.when(under[k])
        def _(k=k):
            piece(k, False).wait_send()

    wait_near(1)

    def gather(own, prev, after):
        return jnp.concatenate([own[0:2] + prev, own[2:6], own[6:8] + after], axis=0)

    out_ref[...] = gather(found[0:8, 0:8], recv_x[1, 0], recv_x[1, 1])
    out_ref[:, 0:2, :] = out_ref[:, 0:2, :] + gather(recv_y[1, 0], recv_d[1, 0], recv_d[1, 2])
    out_ref[:, 6:8, :] = out_ref[:, 6:8, :] + gather(recv_y[1, 1], recv_d[1, 1], recv_d[1, 3])


def solution(mesh):
    nx, ny, nz = mesh.shape["gx"], mesh.shape["gy"], mesh.shape["gz"]

    def body(initial, source, metric, eigenvectors, eigenvalues):
        hbm = pl.BlockSpec(memory_space=pl.ANY)
        vmem = pltpu.VMEM
        correction = pl.pallas_call(
            functools.partial(kernel, nx, ny, nz),
            out_shape=vmem((8, 8, 128), F32),
            in_specs=[hbm] * 6,
            out_specs=pl.BlockSpec(memory_space=vmem),
            scratch_shapes=[
                vmem((8, 8, 128), F32),
                vmem((8, 8, 128), F32),
                vmem((3, 8, 8, 128), F32),
                vmem((2, 448, 128), BF16),
                vmem((10, 16, 16), F32),
                vmem((10, 16, 16), F32),
                vmem((10, 16, 16), F32),
                vmem((10, 24, 16), F32),
                vmem((3, 16, 16), F32),
                pltpu.SemaphoreType.DMA((33,)),
                vmem((2, 2, 2, 8, 128), F32),
                vmem((2, 2, 8, 2, 128), F32),
                vmem((2, 4, 2, 2, 128), F32),
                vmem((2, 2, 2, 8, 128), F32),
                vmem((2, 2, 8, 2, 128), F32),
                vmem((2, 4, 2, 2, 128), F32),
                pltpu.SemaphoreType.DMA((2, 8)),
                pltpu.SemaphoreType.DMA((2, 8)),
                vmem((2, 1, ROWS), F32),
                vmem((2, 1, ROWS), F32),
                vmem((16, 128), F32),
                vmem((16, 128), F32),
                pltpu.SemaphoreType.DMA((2, 2)),
                pltpu.SemaphoreType.DMA((2, 2)),
                pltpu.SemaphoreType.REGULAR,
                pltpu.SemaphoreType.REGULAR((8,)),
                vmem((1, ROWS), F32),
                pltpu.SemaphoreType.DMA,
                pltpu.SemaphoreType.DMA,
                vmem((8, 128), F32),
                vmem((8, 128), F32),
                vmem((8, 128), F32),
                vmem((2, 2, 128), F32),
                vmem((8, 2, 128), F32),
                vmem((3, 2, 128), F32),
                pltpu.SemaphoreType.DMA((9,)),
                pltpu.SemaphoreType.DMA((9,)),
                pltpu.SemaphoreType.DMA((4,)),
                pltpu.SemaphoreType.DMA((4,)),
                vmem((10, 16, 128), F32),
                vmem((16, 128), F32),
                vmem((10, 16, 128), F32),
                vmem((128, 128), F32),
                vmem((2, ROWS, 128), F32),
                vmem((2, 10, 10, 8, 128), F32),
                vmem((2, 10, 16, 128), F32),
                vmem((2, 160, 128), BF16),
                vmem((2, 160, 128), BF16),
                vmem((2, 10, 16, 128), F32),
            ],
            compiler_params=pltpu.CompilerParams(collective_id=0, has_side_effects=True),
        )(
            initial,
            source,
            metric,
            eigenvectors,
            eigenvalues,
            jnp.asarray(operator_tables()),
        )
        return initial + correction

    placed = (
        P("gx", "gy", "gz"),
        P("gx", "gy", "gz"),
        P(None, "gx", "gy", "gz"),
        P(None, None, None, "gx", "gy", "gz"),
        P(None, None, "gx", "gy", "gz"),
    )
    return jax.shard_map(
        body, mesh=mesh, in_specs=placed, out_specs=P("gx", "gy", "gz"), check_vma=False
    )
```

```python
import functools

import jax
import jax.numpy as jnp
import numpy as np
from jax import lax
from jax.experimental import pallas as pl
from jax.experimental.pallas import tpu as pltpu
from jax.sharding import PartitionSpec as P

MESH = pl.DeviceIdType.MESH
F32 = jnp.float32
BF16 = jnp.bfloat16

gll_points = np.array(
    [
        -1.0,
        -0.8717401485096066,
        -0.5917001814331423,
        -0.2092992179024789,
        0.2092992179024789,
        0.5917001814331423,
        0.8717401485096066,
        1.0,
    ]
)

DIRS = [(-1, 0), (1, 0), (0, -1), (0, 1), (-1, -1), (-1, 1), (1, -1), (1, 1)]
OPP = [1, 0, 3, 2, 7, 6, 5, 4]
PIECES = [4, 6, 2, 5, 7, 3, 0, 1, 8]
HELD = {0: 0, 2: 1, 4: 2, 8: 3}
OYF, OYB, OZ, OL, ROWS = 160, 320, 480, 720, 768


def derivative_table():
    number = gll_points.shape[0]
    products = np.array(
        [
            np.prod([gll_points[i] - gll_points[k] for k in range(number) if k != i])
            for i in range(number)
        ]
    )
    table = np.zeros((number, number))
    for i in range(number):
        for j in range(number):
            if i != j:
                table[i, j] = products[i] / products[j] / (gll_points[i] - gll_points[j])
        table[i, i] = -np.sum(table[i])
    return table


def operator_tables():
    table = derivative_table().astype(np.float32)
    eye = np.eye(8, dtype=np.float32)
    left = np.concatenate([np.kron(table, eye), np.kron(eye, table)], axis=0)
    left = np.concatenate([left, np.zeros((128, 64), np.float32)], axis=1)
    left_t = np.ascontiguousarray(left.T[:64])
    right = np.kron(np.eye(16, dtype=np.float32), table.T)
    full = np.concatenate([left, left_t, right, right.T], axis=0)
    high = full.astype(jnp.bfloat16)
    low = (full - high.astype(np.float32)).astype(jnp.bfloat16)
    return np.stack([high, low])


def dot(a, b, dims=((1,), (0,))):
    return lax.dot_general(a, b, (dims, ((), ())), preferred_element_type=F32)


def halves(value):
    high = value.astype(BF16)
    return high, (value - high.astype(F32)).astype(BF16)


def thirds(value):
    high = value.astype(BF16)
    rest = value - high.astype(F32)
    mid = rest.astype(BF16)
    return high, mid, (rest - mid.astype(F32)).astype(BF16)


def dot3(a, b, dims=((1,), (0,))):
    return dot(a[0], b[0], dims) + (dot(a[1], b[0], dims) + dot(a[0], b[1], dims))


def lanes(group):
    lane = lax.broadcasted_iota(jnp.int32, (1, 128), 1)
    block = (lane * 205) >> 11
    mode = lane - 10 * block
    if group == 0:
        return jnp.where(lane < 120, block + 1, 99), mode
    ends = jnp.where(block < 2, block - 1, block + 11)
    return jnp.where(lane < 60, ends, 99), mode


def kernel(
    nx, ny, nz,
    u_h, f_h, m_h, eig_h, lam_h, cst_h, out_ref,
    u_v, f_v, m_v, cst_v, ex, eyf, eyb, ez, el, in_sem,
    send_x, send_y, send_d, recv_x, recv_y, recv_d, near_send, near_recv,
    fe_send, fe_recv, fx_send, fx_recv, far_send, far_recv, ready, near_ready, pe, side_send, side_recv,
    slab_send, slab_recv, slab_held, part_send, part_recv, part_held, piece_send, piece_recv, held_send, held_recv, xf, fan,
    xs, xc, cm, cxb, inv, wh, wl, zs,
):
    ix, iy, iz = lax.axis_index("gx"), lax.axis_index("gy"), lax.axis_index("gz")

    first = [(u_h, u_v), (cst_h, cst_v), (m_h, m_v), (f_h, f_v)]
    second = [
        (eig_h.at[0, 1:9, :, 0, 0], ex.at[0:8, 0:10]),
        (eig_h.at[0, 0, :, 0, 0], ex.at[8, 0:10]),
        (eig_h.at[0, 9, :, 0, 0], ex.at[9, 0:10]),
        (eig_h.at[1, 1:9, :, 0, 0], eyf.at[0:8, 0:10]),
        (eig_h.at[1, 0, :, 0, 0], eyf.at[8, 0:10]),
        (eig_h.at[1, 9, :, 0, 0], eyf.at[9, 0:10]),
        (lam_h.at[:, :, 0, 0], el.at[:, 0:10]),
    ]
    for row, pos in enumerate([1, 2, 3, 4, 5, 6, 7, 8, 0, 9]):
        second.append((eig_h.at[1, pos, :, 0, 0], eyb.at[:, row]))
    for row, pos in enumerate([1, 2, 3, 4, 5, 6, 7, 8]):
        second.append((eig_h.at[2, pos, :, 0, 0], ez.at[:, row]))
    for row, pos in [(14, 0), (15, 1), (16, 8), (17, 9)]:
        second.append((eig_h.at[2, pos, :, 0, 0], ez.at[:, row]))
    loads = [
        pltpu.make_async_copy(src, dst, in_sem.at[i])
        for i, (src, dst) in enumerate(first + second)
    ]
    for load in loads:
        load.start()

    recv_x[...] = jnp.zeros_like(recv_x)
    recv_y[...] = jnp.zeros_like(recv_y)
    recv_d[...] = jnp.zeros_like(recv_d)
    fe_recv[...] = jnp.zeros_like(fe_recv)
    fx_recv[...] = jnp.zeros_like(fx_recv)
    slab_recv[...] = jnp.zeros_like(slab_recv)
    part_recv[...] = jnp.zeros_like(part_recv)

    has_next, has_prev = iz < nz - 1, iz > 0
    to_next, to_prev = (ix, iy, iz + 1), (ix, iy, iz - 1)
    detour = nx > 1 and nz > 1
    in_line = (ix == 0) & (iy == 0)
    origin = in_line & (iz == 0) & detour
    after_origin = in_line & (iz == 1) & detour
    helper = (ix == 1) & (iy == 0) & (iz == 0) & detour
    near, target = [], []
    for dx, dy in DIRS:
        ok = None
        for cond in (
            [ix > 0] * (dx < 0) + [ix < nx - 1] * (dx > 0)
            + [iy > 0] * (dy < 0) + [iy < ny - 1] * (dy > 0)
        ):
            ok = cond if ok is None else ok & cond
        near.append(ok)
        target.append((ix + dx, iy + dy, iz))
    barrier = pltpu.get_barrier_semaphore()
    count = jnp.int32(0)
    later = []
    for dx, dy in DIRS:
        if dy > 0 or (dy == 0 and dx < 0):
            later.append(~origin)
        else:
            later.append(detour & (iz == 0) & (ix + dx == 0) & (iy + dy == 0))
    beside = [near[k] & (iz > 0) & (iy < ny - 1) & (DIRS[k][1] == 0) for k in range(8)]
    before_me = [ok & ~after & ~x for ok, after, x in zip(near, later, beside)]
    after_me = [ok & after & ~x for ok, after, x in zip(near, later, beside)]
    first_row = (iy == 0) & (iz == 0) & (nx > 2)
    greeted = list(zip(after_me, target)) + [
        (has_next & ~origin, to_next), (after_origin, (0, 0, 0)),
        (first_row & (ix == nx - 2), (nx - 1, iy, iz)),
    ]
    spot, half = iz * ny + iy, max(ny // 2, 1)
    relayed = nz > 2
    last, second = relayed & (iz == nz - 1), relayed & (iz == nz - 2)
    middle = relayed & (spot >= (nz - 2) * ny + half) & (spot < (nz - 1) * ny + half)
    down_spot, up_spot = jnp.maximum(spot - half, 0), spot + half
    half_down = (ix, down_spot % ny, down_spot // ny)
    half_up = (ix, up_spot % ny, up_spot // ny)
    greeted += [(last, half_down), (second, half_up)]
    over, under, from_origin = [], [], []
    for k, (dx, dy) in enumerate(DIRS + [(0, 0)]):
        inside = near[k] if k < 8 else (ix >= 0)
        over.append(has_next & inside)
        under.append(has_prev & inside)
        from_origin.append(detour & (iz == 1) & (ix + dx == 0) & (iy + dy == 0))
        if k < 8:
            greeted.append((over[k] & ~origin, (ix + dx, iy + dy, iz + 1)))
    for ok, device in greeted:
        @pl.when(ok)
        def _(device=device):
            pl.semaphore_signal(barrier, 1, device_id=device, device_id_type=MESH)
    count = jnp.int32(0)
    below = [ok & ~start for ok, start in zip(under, from_origin)]
    for ok in before_me + below + [origin, first_row & (ix == nx - 1)]:
        count = count + ok.astype(jnp.int32)
    count = count + 2 * middle.astype(jnp.int32)

    xf[...] = jnp.zeros_like(xf)
    fan[...] = jnp.zeros_like(fan)
    ex[:, 10:16, :] = jnp.zeros((10, 6, 16), F32)
    eyf[:, 10:16, :] = jnp.zeros((10, 6, 16), F32)
    eyb[:, 10:16, :] = jnp.zeros((10, 6, 16), F32)
    ez[:, 8:14, :] = jnp.zeros((10, 6, 16), F32)
    ez[:, 18:24, :] = jnp.zeros((10, 6, 16), F32)
    el[:, 10:16, :] = jnp.zeros((3, 6, 16), F32)
    xs[:, 10:16, :] = jnp.zeros((10, 6, 128), F32)
    xc[96:128, :] = jnp.zeros((32, 128), F32)

    for load in loads[:4]:
        load.wait()
    field = halves(u_v[...].reshape(64, 128))
    left = cst_v[0, 0:128, 0:64], cst_v[1, 0:128, 0:64]
    left_t = cst_v[0, 128:192], cst_v[1, 128:192]
    right = cst_v[0, 192:320], cst_v[1, 192:320]
    right_t = cst_v[0, 320:448], cst_v[1, 320:448]
    flux = dot3(left, field) * m_v[0:2].reshape(128, 128)
    flux_z = dot3(field, right) * m_v[2].reshape(64, 128)
    applied = dot3(left_t, halves(flux)) + dot3(halves(flux_z), right_t)
    res = f_v[...] - applied.reshape(8, 8, 128)

    def recv_of(turn, k):
        if k < 2:
            return recv_x.at[turn, k]
        return recv_y.at[turn, k - 2] if k < 4 else recv_d.at[turn, k - 4]

    def send_of(turn, k):
        if k < 2:
            return send_x.at[turn, k]
        return send_y.at[turn, k - 2] if k < 4 else send_d.at[turn, k - 4]

    def outgoing(turn, k):
        return pltpu.make_async_remote_copy(
            src_ref=send_of(turn, k),
            dst_ref=recv_of(turn, OPP[k]),
            send_sem=near_send.at[turn, k],
            recv_sem=near_recv.at[turn, OPP[k]],
            device_id=target[k],
            device_id_type=MESH,
        )

    def incoming(turn, k):
        return pltpu.make_async_remote_copy(
            src_ref=send_of(turn, k),
            dst_ref=recv_of(turn, k),
            send_sem=near_send.at[turn, k],
            recv_sem=near_recv.at[turn, k],
            device_id=target[k],
            device_id_type=MESH,
        )

    ORDER = [4, 5, 6, 7, 0, 1, 2, 3]

    def send_near(turn, where, order=ORDER):
        for k in order:
            @pl.when(where[k])
            def _(k=k):
                if where is after_me:
                    pl.semaphore_wait(near_ready.at[k], 1)
                outgoing(turn, k).start()

    def wait_near(turn):
        for k in ORDER:
            @pl.when(near[k])
            def _(k=k):
                incoming(turn, k).wait_recv()

    def pack_sides(turn, value, low, high):
        for side, rows in enumerate((low, high)):
            for j, row in enumerate(rows):
                send_x[turn, side, j] = value[row, 0:8]
                send_y[turn, side, :, j : j + 1, :] = value[0:8, row : row + 1]

    def pack_corners(turn, value, low, high):
        for k in range(4, 8):
            rows_x = low if DIRS[k][0] < 0 else high
            rows_y = low if DIRS[k][1] < 0 else high
            for i, row_x in enumerate(rows_x):
                for j, row_y in enumerate(rows_y):
                    send_d[turn, k - 4, i, j : j + 1, :] = value[row_x, row_y : row_y + 1]

    first16 = lax.broadcasted_iota(jnp.int32, (8, 128), 1) < 16
    low = [jnp.where(first16, res[x], 0.0) for x in range(8)]
    packed = low[0]
    for x in range(1, 8):
        packed = packed + pltpu.roll(low[x], 16 * x, 1)
    slab_send[...] = packed
    def piece(k, arriving, held=False):
        dx, dy = (DIRS + [(0, 0)])[k]
        if k == 8:
            src, slot, dst = slab_send, 8, slab_recv
        else:
            slot = k if arriving else OPP[k]
            src = part_send.at[k] if k < 2 else slab_send.at[pl.ds(6 if dy > 0 else 0, 2)]
            dst = part_recv.at[slot]
        if held:
            dst = slab_held if k == 8 else part_held.at[HELD[k]]
        return pltpu.make_async_remote_copy(
            src_ref=src,
            dst_ref=dst,
            send_sem=piece_send.at[k],
            recv_sem=held_recv.at[HELD[k]] if held else piece_recv.at[slot],
            device_id=(1, 0, 0) if held else (ix + dx, iy + dy, iz + 1 if arriving else iz - 1),
            device_id_type=MESH,
        )

    def pass_piece(k):
        slot = 8 if k == 8 else OPP[k]
        return pltpu.make_async_remote_copy(
            src_ref=slab_held if k == 8 else part_held.at[HELD[k]],
            dst_ref=slab_recv if k == 8 else part_recv.at[slot],
            send_sem=held_send.at[HELD[k]],
            recv_sem=piece_recv.at[slot],
            device_id=(0, 0, 0),
            device_id_type=MESH,
        )

    def send_pieces(pieces):
        for k in pieces:
            @pl.when(below[k])
            def _(k=k):
                piece(k, False).start()

            if k in HELD:
                @pl.when(under[k] & from_origin[k])
                def _(k=k):
                    piece(k, False, True).start()

    pl.semaphore_wait(barrier, count)
    send_pieces([k for k in PIECES if k > 1])
    for k in range(8):
        @pl.when(before_me[k])
        def _(k=k):
            pl.semaphore_signal(
                near_ready.at[OPP[k]], 1, device_id=target[k], device_id_type=MESH
            )

    @pl.when(has_prev & ~after_origin & ~last)
    def _():
        pl.semaphore_signal(ready, 1, device_id=to_prev, device_id_type=MESH)

    @pl.when(middle)
    def _():
        pl.semaphore_signal(ready, 1, device_id=half_down, device_id_type=MESH)

    row8 = lax.broadcasted_iota(jnp.int32, (8, 128), 0)
    for side, pair in enumerate(((0, 1), (6, 7))):
        for j, x in enumerate(pair):
            line = jnp.where(row8 == 0, low[x], 0.0)
            for y in range(1, 8):
                line = line + jnp.where(row8 == y, pltpu.roll(low[x], 16 * y, 1), 0.0)
            part_send[side, j : j + 1, :] = line.sum(axis=0, keepdims=True)

    send_pieces([k for k in PIECES if k < 2])
    pack_corners(0, res, (0, 1), (6, 7))
    pack_sides(0, res, (0, 1), (6, 7))
    send_near(0, before_me)

    for load in loads[4:]:
        load.wait()
    eigen = jnp.concatenate(
        [
            ex[...].reshape(160, 16),
            eyf[...].reshape(160, 16),
            eyb[...].reshape(160, 16),
            ez[...].reshape(240, 16),
            el[...].reshape(48, 16),
        ],
        axis=0,
    )
    parts = thirds(eigen)
    wanted = lax.broadcasted_iota(jnp.int32, (8, 16), 0) * 15
    picks = jnp.where(lax.broadcasted_iota(jnp.int32, (8, 16), 1) == wanted, 1.0, 0.0).astype(BF16)
    ends = sum(dot(picks, part, ((1,), (1,))) for part in parts)
    fe_send[0] = ends[0:1]
    fe_send[1] = ends[1:2]

    def prepare(g):
        element, mode = lanes(g)
        spread = jnp.where(
            lax.broadcasted_iota(jnp.int32, (16, 128), 0) == element, 1.0, 0.0
        ).astype(BF16)
        table = sum(dot(part, spread) for part in parts)
        if g == 1:
            row = lax.broadcasted_iota(jnp.int32, (8, ROWS), 0)
            other = jnp.where(row == 0, fe_recv[0], jnp.where(row == 1, fe_recv[1], 0.0))
            far_row = lax.broadcasted_iota(jnp.int32, (8, 128), 0)
            spread_far = jnp.where(
                ((far_row == 0) & (element == -1)) | ((far_row == 1) & (element == 16)), 1.0, 0.0
            ).astype(BF16)
            far = sum(dot(part, spread_far, ((0,), (0,))) for part in thirds(other))
            table = table + far
        cm[g] = table
        for r in range(100):
            at = 16 * (r // 10) + r % 10
            cxb[g, r // 10, r % 10] = jnp.broadcast_to(cm[g, at : at + 1, :], (8, 128))
        tiles = jnp.zeros((24, 128), F32)
        for s in range(10):
            tiles = tiles + jnp.where(mode == s, cm[g, OZ + 24 * s : OZ + 24 * s + 24, :], 0.0)
        inner, lower, upper = tiles[0:8], tiles[8:16], tiles[16:24]
        columns = []
        for e in list(range(16)) + [-2, -1, 16, 17]:
            columns.append(
                jnp.where(
                    element == e,
                    inner,
                    jnp.where(element == e + 1, lower, jnp.where(element == e - 1, upper, 0.0)),
                )
            )
        wh[g], wl[g] = halves(jnp.concatenate(columns, axis=0))
        rate_z = jnp.where(
            lax.broadcasted_iota(jnp.int32, (16, 128), 0) == mode, cm[g, OL + 32 : OL + 48, :], 0.0
        ).sum(axis=0, keepdims=True)
        rate_yz = cm[g, OL + 16 : OL + 32, :] + rate_z
        for p in range(10):
            rate = rate_yz + cm[g, OL + p : OL + p + 1, :]
            some = rate > 0.0
            inv[g, p] = jnp.where(some, 1.0 / jnp.where(some, rate, 1.0), 0.0)

    def far_copy(kind, way, arriving):
        if kind == 0:
            src, dst = fe_send.at[1 - way], fe_recv.at[way]
        else:
            src, dst = fx_send.at[pl.ds(6, 10)], fx_recv.at[pl.ds(6, 10)]
        return pltpu.make_async_remote_copy(
            src_ref=src,
            dst_ref=dst,
            send_sem=far_send.at[kind, way],
            recv_sem=far_recv.at[kind, way],
            device_id=to_next if (way == 0) != arriving else to_prev,
            device_id_type=MESH,
        )

    def aside(passing):
        return pltpu.make_async_remote_copy(
            src_ref=pe if passing else fe_send.at[0],
            dst_ref=fe_recv.at[1] if passing else pe,
            send_sem=side_send if passing else far_send.at[0, 1],
            recv_sem=far_recv.at[0, 1] if passing else side_recv,
            device_id=(0, 0, 0) if passing else (1, 0, 0),
            device_id_type=MESH,
        )

    @pl.when(below[8])
    def _():
        far_copy(0, 1, False).start()

    @pl.when(after_origin)
    def _():
        aside(False).start()

    def send_up(kind):
        @pl.when(has_next)
        def _():
            far_copy(kind, 0, False).start()

    send_near(0, after_me)
    send_near(0, beside)
    prepare(0)

    wait_near(0)

    def join(own, prev, after):
        return jnp.concatenate(
            [own[0:1] + prev[1:2], own[1:7], own[7:8] + after[0:1], prev[0:1], after[1:2]], axis=0
        )

    xs[:, 0:8, :] = join(res, recv_x[0, 0], recv_x[0, 1])
    before = join(recv_y[0, 0], recv_d[0, 0], recv_d[0, 2])
    behind = join(recv_y[0, 1], recv_d[0, 1], recv_d[0, 3])
    xs[:, 0:1, :] = xs[:, 0:1, :] + before[:, 1:2]
    xs[:, 7:8, :] = xs[:, 7:8, :] + behind[:, 0:1]
    xs[:, 8:9, :] = before[:, 0:1]
    xs[:, 9:10, :] = behind[:, 1:2]
    xc[0:80, :] = xs[:, 0:8, :].reshape(80, 128)
    for a in range(10):
        xc[80 + 2 * a : 82 + 2 * a, :] = xs[a, 8:10, :]
    turned = xc[...].T
    fx_send[...] = turned[112:128]

    nodes = halves(xs[...].reshape(160, 128))

    def to_modes(g):
        zs[g] = dot3(nodes, (wh[g, 0:128], wl[g, 0:128])).reshape(10, 16, 128)

    def solve(g):
        value = zs[g].reshape(10, 2, 8, 128)
        total = None
        for a in range(10):
            term = cxb[g, a][:, None] * value[a][None]
            total = term if total is None else total + term
        value, total = total, None
        for b in range(10):
            row = value[:, b // 8, b % 8 : b % 8 + 1, :][:, None]
            pick = cm[g, OYF + 16 * b : OYF + 16 * b + 16, :].reshape(1, 2, 8, 128)
            term = pick * row
            total = term if total is None else total + term
        value, total = total * inv[g].reshape(10, 2, 8, 128), None
        for q in range(10):
            row = value[:, q // 8, q % 8 : q % 8 + 1, :][:, None]
            pick = cm[g, OYB + 16 * q : OYB + 16 * q + 16, :].reshape(1, 2, 8, 128)
            term = pick * row
            total = term if total is None else total + term
        value, total = total, None
        for p in range(10):
            term = cxb[g, :, p][:, None] * value[p][None]
            total = term if total is None else total + term
        return dot3(
            halves(total.reshape(160, 128)), (wh[g, 0:128], wl[g, 0:128]), ((1,), (1,))
        )

    to_modes(0)

    @pl.when(has_next & ~origin)
    def _():
        pl.semaphore_wait(ready, 1)

    send_up(0)
    send_up(1)
    found = solve(0)

    @pl.when(helper)
    def _():
        aside(False).wait_recv()
        aside(True).start()

    @pl.when(has_next)
    def _():
        far_copy(0, 1, True).wait_recv()

    @pl.when(has_prev)
    def _():
        far_copy(0, 0, True).wait_recv()

    prepare(1)
    to_modes(1)

    @pl.when(helper)
    def _():
        for k in HELD:
            piece(k, False, True).wait_recv()
            pass_piece(k).start()

    @pl.when(has_prev)
    def _():
        far_copy(1, 0, True).wait_recv()

    beyond = halves(fx_recv[...])

    more = dot3(beyond, (wh[1, 128:144], wl[1, 128:144]), ((0,), (0,)))
    zs[1, :, 0:8, :] = zs[1, :, 0:8, :] + more[0:80].reshape(10, 8, 128)
    for a in range(10):
        zs[1, a, 8:10, :] = zs[1, a, 8:10, :] + more[80 + 2 * a : 82 + 2 * a]

    for k in PIECES:
        @pl.when(over[k])
        def _(k=k):
            piece(k, True).wait_recv()

    def unpack(rows):
        return jnp.concatenate(
            [(pltpu.roll(rows, 128 - 16 * x, 1) if x else rows)[None] for x in range(8)], axis=0
        )

    own = unpack(slab_recv[...])
    sides = []
    for side in range(2):
        lines = []
        for j in range(2):
            line = jnp.broadcast_to(part_recv[side, j : j + 1, :], (8, 128))
            tile = jnp.where(row8 == 0, line, 0.0)
            for y in range(1, 8):
                tile = tile + jnp.where(row8 == y, pltpu.roll(line, 128 - 16 * y, 1), 0.0)
            lines.append(tile[None])
        sides.append(jnp.concatenate(lines, axis=0))
    for i in range(6):
        fan[2 * i : 2 * i + 2, :] = part_recv[2 + i]
    wide = unpack(fan[...])
    xf[:, 0:8, :] = join(own, sides[0], sides[1])
    before = join(wide[:, 0:2], wide[6:8, 4:6], wide[0:2, 8:10])
    behind = join(wide[:, 2:4], wide[6:8, 6:8], wide[0:2, 10:12])
    xf[:, 0:1, :] = xf[:, 0:1, :] + before[:, 1:2]
    xf[:, 7:8, :] = xf[:, 7:8, :] + behind[:, 0:1]
    xf[:, 8:9, :] = before[:, 0:1]
    xf[:, 9:10, :] = behind[:, 1:2]
    above = halves(xf[:, :, 0:16].reshape(160, 16))
    risen = dot3(above, (wh[1, 144:160], wl[1, 144:160])).reshape(10, 16, 128)

    zs[1] = zs[1] + risen
    found = (found + solve(1)).reshape(10, 16, 128)
    pack_corners(1, found, (8, 0), (7, 9))
    send_near(1, near, ORDER[:4])
    pack_sides(1, found, (8, 0), (7, 9))
    send_near(1, near, ORDER[4:])

    for turn in range(2):
        for k in range(8):
            @pl.when(near[k])
            def _(turn=turn, k=k):
                outgoing(turn, k).wait_send()

    for kind in range(2):
        @pl.when(has_next)
        def _(kind=kind):
            far_copy(kind, 0, False).wait_send()

    @pl.when(below[8])
    def _():
        far_copy(0, 1, False).wait_send()

    @pl.when(after_origin)
    def _():
        aside(False).wait_send()

    @pl.when(helper)
    def _():
        aside(True).wait_send()
        for k in HELD:
            pass_piece(k).wait_send()

    for k in PIECES:
        @pl.when(under[k])
        def _(k=k):
            piece(k, False).wait_send()

    wait_near(1)

    def gather(own, prev, after):
        return jnp.concatenate([own[0:2] + prev, own[2:6], own[6:8] + after], axis=0)

    out_ref[...] = gather(found[0:8, 0:8], recv_x[1, 0], recv_x[1, 1])
    out_ref[:, 0:2, :] = out_ref[:, 0:2, :] + gather(recv_y[1, 0], recv_d[1, 0], recv_d[1, 2])
    out_ref[:, 6:8, :] = out_ref[:, 6:8, :] + gather(recv_y[1, 1], recv_d[1, 1], recv_d[1, 3])


def solution(mesh):
    nx, ny, nz = mesh.shape["gx"], mesh.shape["gy"], mesh.shape["gz"]

    def body(initial, source, metric, eigenvectors, eigenvalues):
        hbm = pl.BlockSpec(memory_space=pl.ANY)
        vmem = pltpu.VMEM
        correction = pl.pallas_call(
            functools.partial(kernel, nx, ny, nz),
            out_shape=vmem((8, 8, 128), F32),
            in_specs=[hbm] * 6,
            out_specs=pl.BlockSpec(memory_space=vmem),
            scratch_shapes=[
                vmem((8, 8, 128), F32),
                vmem((8, 8, 128), F32),
                vmem((3, 8, 8, 128), F32),
                vmem((2, 448, 128), BF16),
                vmem((10, 16, 16), F32),
                vmem((10, 16, 16), F32),
                vmem((10, 16, 16), F32),
                vmem((10, 24, 16), F32),
                vmem((3, 16, 16), F32),
                pltpu.SemaphoreType.DMA((33,)),
                vmem((2, 2, 2, 8, 128), F32),
                vmem((2, 2, 8, 2, 128), F32),
                vmem((2, 4, 2, 2, 128), F32),
                vmem((2, 2, 2, 8, 128), F32),
                vmem((2, 2, 8, 2, 128), F32),
                vmem((2, 4, 2, 2, 128), F32),
                pltpu.SemaphoreType.DMA((2, 8)),
                pltpu.SemaphoreType.DMA((2, 8)),
                vmem((2, 1, ROWS), F32),
                vmem((2, 1, ROWS), F32),
                vmem((16, 128), F32),
                vmem((16, 128), F32),
                pltpu.SemaphoreType.DMA((2, 2)),
                pltpu.SemaphoreType.DMA((2, 2)),
                pltpu.SemaphoreType.REGULAR,
                pltpu.SemaphoreType.REGULAR((8,)),
                vmem((1, ROWS), F32),
                pltpu.SemaphoreType.DMA,
                pltpu.SemaphoreType.DMA,
                vmem((8, 128), F32),
                vmem((8, 128), F32),
                vmem((8, 128), F32),
                vmem((2, 2, 128), F32),
                vmem((8, 2, 128), F32),
                vmem((3, 2, 128), F32),
                pltpu.SemaphoreType.DMA((9,)),
                pltpu.SemaphoreType.DMA((9,)),
                pltpu.SemaphoreType.DMA((4,)),
                pltpu.SemaphoreType.DMA((4,)),
                vmem((10, 16, 128), F32),
                vmem((16, 128), F32),
                vmem((10, 16, 128), F32),
                vmem((128, 128), F32),
                vmem((2, ROWS, 128), F32),
                vmem((2, 10, 10, 8, 128), F32),
                vmem((2, 10, 16, 128), F32),
                vmem((2, 160, 128), BF16),
                vmem((2, 160, 128), BF16),
                vmem((2, 10, 16, 128), F32),
            ],
            compiler_params=pltpu.CompilerParams(collective_id=0, has_side_effects=True),
        )(
            initial,
            source,
            metric,
            eigenvectors,
            eigenvalues,
            jnp.asarray(operator_tables()),
        )
        return initial + correction

    placed = (
        P("gx", "gy", "gz"),
        P("gx", "gy", "gz"),
        P(None, "gx", "gy", "gz"),
        P(None, None, None, "gx", "gy", "gz"),
        P(None, None, "gx", "gy", "gz"),
    )
    return jax.shard_map(
        body, mesh=mesh, in_specs=placed, out_specs=P("gx", "gy", "gz"), check_vma=False
    )
```

```python
import functools

import jax
import jax.numpy as jnp
import numpy as np
from jax import lax
from jax.experimental import pallas as pl
from jax.experimental.pallas import tpu as pltpu
from jax.sharding import PartitionSpec as P

MESH = pl.DeviceIdType.MESH
F32 = jnp.float32
BF16 = jnp.bfloat16

gll_points = np.array(
    [
        -1.0,
        -0.8717401485096066,
        -0.5917001814331423,
        -0.2092992179024789,
        0.2092992179024789,
        0.5917001814331423,
        0.8717401485096066,
        1.0,
    ]
)

DIRS = [(-1, 0), (1, 0), (0, -1), (0, 1), (-1, -1), (-1, 1), (1, -1), (1, 1)]
OPP = [1, 0, 3, 2, 7, 6, 5, 4]
PIECES = [4, 6, 2, 5, 7, 3, 0, 1, 8]
HELD = {0: 0, 2: 1, 4: 2, 8: 3}
OYF, OYB, OZ, OL, ROWS = 160, 320, 480, 720, 768


def derivative_table():
    number = gll_points.shape[0]
    products = np.array(
        [
            np.prod([gll_points[i] - gll_points[k] for k in range(number) if k != i])
            for i in range(number)
        ]
    )
    table = np.zeros((number, number))
    for i in range(number):
        for j in range(number):
            if i != j:
                table[i, j] = products[i] / products[j] / (gll_points[i] - gll_points[j])
        table[i, i] = -np.sum(table[i])
    return table


def operator_tables():
    table = derivative_table().astype(np.float32)
    eye = np.eye(8, dtype=np.float32)
    left = np.concatenate([np.kron(table, eye), np.kron(eye, table)], axis=0)
    left = np.concatenate([left, np.zeros((128, 64), np.float32)], axis=1)
    left_t = np.ascontiguousarray(left.T[:64])
    right = np.kron(np.eye(16, dtype=np.float32), table.T)
    full = np.concatenate([left, left_t, right, right.T], axis=0)
    high = full.astype(jnp.bfloat16)
    low = (full - high.astype(np.float32)).astype(jnp.bfloat16)
    return np.stack([high, low])


def dot(a, b, dims=((1,), (0,))):
    return lax.dot_general(a, b, (dims, ((), ())), preferred_element_type=F32)


def halves(value):
    high = value.astype(BF16)
    return high, (value - high.astype(F32)).astype(BF16)


def thirds(value):
    high = value.astype(BF16)
    rest = value - high.astype(F32)
    mid = rest.astype(BF16)
    return high, mid, (rest - mid.astype(F32)).astype(BF16)


def dot3(a, b, dims=((1,), (0,))):
    return dot(a[0], b[0], dims) + (dot(a[1], b[0], dims) + dot(a[0], b[1], dims))


def lanes(group):
    lane = lax.broadcasted_iota(jnp.int32, (1, 128), 1)
    block = (lane * 205) >> 11
    mode = lane - 10 * block
    if group == 0:
        return jnp.where(lane < 120, block + 1, 99), mode
    ends = jnp.where(block < 2, block - 1, block + 11)
    return jnp.where(lane < 60, ends, 99), mode


def kernel(
    nx, ny, nz,
    u_h, f_h, m_h, eig_h, lam_h, cst_h, out_ref,
    u_v, f_v, m_v, cst_v, ex, eyf, eyb, ez, el, in_sem,
    send_x, send_y, send_d, recv_x, recv_y, recv_d, near_send, near_recv,
    fe_send, fe_recv, fx_send, fx_recv, far_send, far_recv, ready, near_ready, pe, side_send, side_recv,
    slab_send, slab_recv, slab_held, part_send, part_recv, part_held, piece_send, piece_recv, held_send, held_recv, xf, fan,
    xs, xc, cm, cxb, inv, wh, wl, zs,
):
    ix, iy, iz = lax.axis_index("gx"), lax.axis_index("gy"), lax.axis_index("gz")

    first = [(u_h, u_v), (cst_h, cst_v), (m_h, m_v), (f_h, f_v)]
    second = [
        (eig_h.at[0, 1:9, :, 0, 0], ex.at[0:8, 0:10]),
        (eig_h.at[0, 0, :, 0, 0], ex.at[8, 0:10]),
        (eig_h.at[0, 9, :, 0, 0], ex.at[9, 0:10]),
        (eig_h.at[1, 1:9, :, 0, 0], eyf.at[0:8, 0:10]),
        (eig_h.at[1, 0, :, 0, 0], eyf.at[8, 0:10]),
        (eig_h.at[1, 9, :, 0, 0], eyf.at[9, 0:10]),
        (lam_h.at[:, :, 0, 0], el.at[:, 0:10]),
    ]
    for row, pos in enumerate([1, 2, 3, 4, 5, 6, 7, 8, 0, 9]):
        second.append((eig_h.at[1, pos, :, 0, 0], eyb.at[:, row]))
    for row, pos in enumerate([1, 2, 3, 4, 5, 6, 7, 8]):
        second.append((eig_h.at[2, pos, :, 0, 0], ez.at[:, row]))
    for row, pos in [(14, 0), (15, 1), (16, 8), (17, 9)]:
        second.append((eig_h.at[2, pos, :, 0, 0], ez.at[:, row]))
    loads = [
        pltpu.make_async_copy(src, dst, in_sem.at[i])
        for i, (src, dst) in enumerate(first + second)
    ]
    for load in loads:
        load.start()

    recv_x[...] = jnp.zeros_like(recv_x)
    recv_y[...] = jnp.zeros_like(recv_y)
    recv_d[...] = jnp.zeros_like(recv_d)
    fe_recv[...] = jnp.zeros_like(fe_recv)
    fx_recv[...] = jnp.zeros_like(fx_recv)
    slab_recv[...] = jnp.zeros_like(slab_recv)
    part_recv[...] = jnp.zeros_like(part_recv)

    has_next, has_prev = iz < nz - 1, iz > 0
    to_next, to_prev = (ix, iy, iz + 1), (ix, iy, iz - 1)
    detour = nx > 1 and nz > 1
    in_line = (ix == 0) & (iy == 0)
    origin = in_line & (iz == 0) & detour
    after_origin = in_line & (iz == 1) & detour
    helper = (ix == 1) & (iy == 0) & (iz == 0) & detour
    near, target = [], []
    for dx, dy in DIRS:
        ok = None
        for cond in (
            [ix > 0] * (dx < 0) + [ix < nx - 1] * (dx > 0)
            + [iy > 0] * (dy < 0) + [iy < ny - 1] * (dy > 0)
        ):
            ok = cond if ok is None else ok & cond
        near.append(ok)
        target.append((ix + dx, iy + dy, iz))
    barrier = pltpu.get_barrier_semaphore()
    count = jnp.int32(0)
    later = []
    for dx, dy in DIRS:
        if dy > 0 or (dy == 0 and dx < 0):
            later.append(~origin)
        else:
            later.append(detour & (iz == 0) & (ix + dx == 0) & (iy + dy == 0))
    beside = [near[k] & (iz > 0) & (iy < ny - 1) & (DIRS[k][1] == 0) for k in range(8)]
    before_me = [ok & ~after & ~x for ok, after, x in zip(near, later, beside)]
    after_me = [ok & after & ~x for ok, after, x in zip(near, later, beside)]
    first_row = (iy == 0) & (iz == 0) & (nx > 2)
    greeted = list(zip(after_me, target)) + [
        (has_next & ~origin, to_next), (after_origin, (0, 0, 0)),
        (first_row & (ix == nx - 2), (nx - 1, iy, iz)),
    ]
    spot, half = iz * ny + iy, max(ny // 2, 1)
    relayed = nz > 2
    last, second = relayed & (iz == nz - 1), relayed & (iz == nz - 2)
    middle = relayed & (spot >= (nz - 2) * ny + half) & (spot < (nz - 1) * ny + half)
    down_spot, up_spot = jnp.maximum(spot - half, 0), spot + half
    half_down = (ix, down_spot % ny, down_spot // ny)
    half_up = (ix, up_spot % ny, up_spot // ny)
    greeted += [(last, half_down), (second, half_up)]
    over, under, from_origin = [], [], []
    for k, (dx, dy) in enumerate(DIRS + [(0, 0)]):
        inside = near[k] if k < 8 else (ix >= 0)
        over.append(has_next & inside)
        under.append(has_prev & inside)
        from_origin.append(detour & (iz == 1) & (ix + dx == 0) & (iy + dy == 0))
        if k < 8:
            greeted.append((over[k] & ~origin, (ix + dx, iy + dy, iz + 1)))
    for ok, device in greeted:
        @pl.when(ok)
        def _(device=device):
            pl.semaphore_signal(barrier, 1, device_id=device, device_id_type=MESH)
    count = jnp.int32(0)
    below = [ok & ~start for ok, start in zip(under, from_origin)]
    for ok in before_me + below + [origin, first_row & (ix == nx - 1)]:
        count = count + ok.astype(jnp.int32)
    count = count + 2 * middle.astype(jnp.int32)

    xf[...] = jnp.zeros_like(xf)
    fan[...] = jnp.zeros_like(fan)
    ex[:, 10:16, :] = jnp.zeros((10, 6, 16), F32)
    eyf[:, 10:16, :] = jnp.zeros((10, 6, 16), F32)
    eyb[:, 10:16, :] = jnp.zeros((10, 6, 16), F32)
    ez[:, 8:14, :] = jnp.zeros((10, 6, 16), F32)
    ez[:, 18:24, :] = jnp.zeros((10, 6, 16), F32)
    el[:, 10:16, :] = jnp.zeros((3, 6, 16), F32)
    xs[:, 10:16, :] = jnp.zeros((10, 6, 128), F32)
    xc[96:128, :] = jnp.zeros((32, 128), F32)

    for load in loads[:4]:
        load.wait()
    field = halves(u_v[...].reshape(64, 128))
    left = cst_v[0, 0:128, 0:64], cst_v[1, 0:128, 0:64]
    left_t = cst_v[0, 128:192], cst_v[1, 128:192]
    right = cst_v[0, 192:320], cst_v[1, 192:320]
    right_t = cst_v[0, 320:448], cst_v[1, 320:448]
    flux = dot3(left, field) * m_v[0:2].reshape(128, 128)
    flux_z = dot3(field, right) * m_v[2].reshape(64, 128)
    applied = dot3(left_t, halves(flux)) + dot3(halves(flux_z), right_t)
    res = f_v[...] - applied.reshape(8, 8, 128)

    def recv_of(turn, k):
        if k < 2:
            return recv_x.at[turn, k]
        return recv_y.at[turn, k - 2] if k < 4 else recv_d.at[turn, k - 4]

    def send_of(turn, k):
        if k < 2:
            return send_x.at[turn, k]
        return send_y.at[turn, k - 2] if k < 4 else send_d.at[turn, k - 4]

    def outgoing(turn, k):
        return pltpu.make_async_remote_copy(
            src_ref=send_of(turn, k),
            dst_ref=recv_of(turn, OPP[k]),
            send_sem=near_send.at[turn, k],
            recv_sem=near_recv.at[turn, OPP[k]],
            device_id=target[k],
            device_id_type=MESH,
        )

    def incoming(turn, k):
        return pltpu.make_async_remote_copy(
            src_ref=send_of(turn, k),
            dst_ref=recv_of(turn, k),
            send_sem=near_send.at[turn, k],
            recv_sem=near_recv.at[turn, k],
            device_id=target[k],
            device_id_type=MESH,
        )

    ORDER = [4, 5, 6, 7, 0, 1, 2, 3]

    def send_near(turn, where):
        for k in ORDER:
            @pl.when(where[k])
            def _(k=k):
                if where is after_me:
                    pl.semaphore_wait(near_ready.at[k], 1)
                outgoing(turn, k).start()

    def wait_near(turn):
        for k in ORDER:
            @pl.when(near[k])
            def _(k=k):
                incoming(turn, k).wait_recv()

    def pack(turn, value, low, high):
        for side, rows in enumerate((low, high)):
            for j, row in enumerate(rows):
                send_x[turn, side, j] = value[row, 0:8]
                send_y[turn, side, :, j : j + 1, :] = value[0:8, row : row + 1]
        for k in range(4, 8):
            rows_x = low if DIRS[k][0] < 0 else high
            rows_y = low if DIRS[k][1] < 0 else high
            for i, row_x in enumerate(rows_x):
                for j, row_y in enumerate(rows_y):
                    send_d[turn, k - 4, i, j : j + 1, :] = value[row_x, row_y : row_y + 1]

    first16 = lax.broadcasted_iota(jnp.int32, (8, 128), 1) < 16
    low = [jnp.where(first16, res[x], 0.0) for x in range(8)]
    packed = low[0]
    for x in range(1, 8):
        packed = packed + pltpu.roll(low[x], 16 * x, 1)
    slab_send[...] = packed
    def piece(k, arriving, held=False):
        dx, dy = (DIRS + [(0, 0)])[k]
        if k == 8:
            src, slot, dst = slab_send, 8, slab_recv
        else:
            slot = k if arriving else OPP[k]
            src = part_send.at[k] if k < 2 else slab_send.at[pl.ds(6 if dy > 0 else 0, 2)]
            dst = part_recv.at[slot]
        if held:
            dst = slab_held if k == 8 else part_held.at[HELD[k]]
        return pltpu.make_async_remote_copy(
            src_ref=src,
            dst_ref=dst,
            send_sem=piece_send.at[k],
            recv_sem=held_recv.at[HELD[k]] if held else piece_recv.at[slot],
            device_id=(1, 0, 0) if held else (ix + dx, iy + dy, iz + 1 if arriving else iz - 1),
            device_id_type=MESH,
        )

    def pass_piece(k):
        slot = 8 if k == 8 else OPP[k]
        return pltpu.make_async_remote_copy(
            src_ref=slab_held if k == 8 else part_held.at[HELD[k]],
            dst_ref=slab_recv if k == 8 else part_recv.at[slot],
            send_sem=held_send.at[HELD[k]],
            recv_sem=piece_recv.at[slot],
            device_id=(0, 0, 0),
            device_id_type=MESH,
        )

    def send_pieces(pieces):
        for k in pieces:
            @pl.when(below[k])
            def _(k=k):
                piece(k, False).start()

            if k in HELD:
                @pl.when(under[k] & from_origin[k])
                def _(k=k):
                    piece(k, False, True).start()

    pl.semaphore_wait(barrier, count)
    send_pieces([k for k in PIECES if k > 1])
    for k in range(8):
        @pl.when(before_me[k])
        def _(k=k):
            pl.semaphore_signal(
                near_ready.at[OPP[k]], 1, device_id=target[k], device_id_type=MESH
            )

    @pl.when(has_prev & ~after_origin & ~last)
    def _():
        pl.semaphore_signal(ready, 1, device_id=to_prev, device_id_type=MESH)

    @pl.when(middle)
    def _():
        pl.semaphore_signal(ready, 1, device_id=half_down, device_id_type=MESH)

    row8 = lax.broadcasted_iota(jnp.int32, (8, 128), 0)
    for side, pair in enumerate(((0, 1), (6, 7))):
        for j, x in enumerate(pair):
            line = jnp.where(row8 == 0, low[x], 0.0)
            for y in range(1, 8):
                line = line + jnp.where(row8 == y, pltpu.roll(low[x], 16 * y, 1), 0.0)
            part_send[side, j : j + 1, :] = line.sum(axis=0, keepdims=True)

    send_pieces([k for k in PIECES if k < 2])
    pack(0, res, (0, 1), (6, 7))
    send_near(0, before_me)

    for load in loads[4:]:
        load.wait()
    eigen = jnp.concatenate(
        [
            ex[...].reshape(160, 16),
            eyf[...].reshape(160, 16),
            eyb[...].reshape(160, 16),
            ez[...].reshape(240, 16),
            el[...].reshape(48, 16),
        ],
        axis=0,
    )
    parts = thirds(eigen)
    wanted = lax.broadcasted_iota(jnp.int32, (8, 16), 0) * 15
    picks = jnp.where(lax.broadcasted_iota(jnp.int32, (8, 16), 1) == wanted, 1.0, 0.0).astype(BF16)
    ends = sum(dot(picks, part, ((1,), (1,))) for part in parts)
    fe_send[0] = ends[0:1]
    fe_send[1] = ends[1:2]

    def prepare(g):
        element, mode = lanes(g)
        spread = jnp.where(
            lax.broadcasted_iota(jnp.int32, (16, 128), 0) == element, 1.0, 0.0
        ).astype(BF16)
        table = sum(dot(part, spread) for part in parts)
        if g == 1:
            row = lax.broadcasted_iota(jnp.int32, (8, ROWS), 0)
            other = jnp.where(row == 0, fe_recv[0], jnp.where(row == 1, fe_recv[1], 0.0))
            far_row = lax.broadcasted_iota(jnp.int32, (8, 128), 0)
            spread_far = jnp.where(
                ((far_row == 0) & (element == -1)) | ((far_row == 1) & (element == 16)), 1.0, 0.0
            ).astype(BF16)
            far = sum(dot(part, spread_far, ((0,), (0,))) for part in thirds(other))
            table = table + far
        cm[g] = table
        for r in range(100):
            at = 16 * (r // 10) + r % 10
            cxb[g, r // 10, r % 10] = jnp.broadcast_to(cm[g, at : at + 1, :], (8, 128))
        tiles = jnp.zeros((24, 128), F32)
        for s in range(10):
            tiles = tiles + jnp.where(mode == s, cm[g, OZ + 24 * s : OZ + 24 * s + 24, :], 0.0)
        inner, lower, upper = tiles[0:8], tiles[8:16], tiles[16:24]
        columns = []
        for e in list(range(16)) + [-2, -1, 16, 17]:
            columns.append(
                jnp.where(
                    element == e,
                    inner,
                    jnp.where(element == e + 1, lower, jnp.where(element == e - 1, upper, 0.0)),
                )
            )
        wh[g], wl[g] = halves(jnp.concatenate(columns, axis=0))
        rate_z = jnp.where(
            lax.broadcasted_iota(jnp.int32, (16, 128), 0) == mode, cm[g, OL + 32 : OL + 48, :], 0.0
        ).sum(axis=0, keepdims=True)
        rate_yz = cm[g, OL + 16 : OL + 32, :] + rate_z
        for p in range(10):
            rate = rate_yz + cm[g, OL + p : OL + p + 1, :]
            some = rate > 0.0
            inv[g, p] = jnp.where(some, 1.0 / jnp.where(some, rate, 1.0), 0.0)

    def far_copy(kind, way, arriving):
        if kind == 0:
            src, dst = fe_send.at[1 - way], fe_recv.at[way]
        else:
            src, dst = fx_send.at[pl.ds(6, 10)], fx_recv.at[pl.ds(6, 10)]
        return pltpu.make_async_remote_copy(
            src_ref=src,
            dst_ref=dst,
            send_sem=far_send.at[kind, way],
            recv_sem=far_recv.at[kind, way],
            device_id=to_next if (way == 0) != arriving else to_prev,
            device_id_type=MESH,
        )

    def aside(passing):
        return pltpu.make_async_remote_copy(
            src_ref=pe if passing else fe_send.at[0],
            dst_ref=fe_recv.at[1] if passing else pe,
            send_sem=side_send if passing else far_send.at[0, 1],
            recv_sem=far_recv.at[0, 1] if passing else side_recv,
            device_id=(0, 0, 0) if passing else (1, 0, 0),
            device_id_type=MESH,
        )

    @pl.when(below[8])
    def _():
        far_copy(0, 1, False).start()

    @pl.when(after_origin)
    def _():
        aside(False).start()

    def send_up(kind):
        @pl.when(has_next)
        def _():
            far_copy(kind, 0, False).start()

    send_near(0, after_me)
    send_near(0, beside)
    prepare(0)

    wait_near(0)

    def join(own, prev, after):
        return jnp.concatenate(
            [own[0:1] + prev[1:2], own[1:7], own[7:8] + after[0:1], prev[0:1], after[1:2]], axis=0
        )

    xs[:, 0:8, :] = join(res, recv_x[0, 0], recv_x[0, 1])
    before = join(recv_y[0, 0], recv_d[0, 0], recv_d[0, 2])
    behind = join(recv_y[0, 1], recv_d[0, 1], recv_d[0, 3])
    xs[:, 0:1, :] = xs[:, 0:1, :] + before[:, 1:2]
    xs[:, 7:8, :] = xs[:, 7:8, :] + behind[:, 0:1]
    xs[:, 8:9, :] = before[:, 0:1]
    xs[:, 9:10, :] = behind[:, 1:2]
    xc[0:80, :] = xs[:, 0:8, :].reshape(80, 128)
    for a in range(10):
        xc[80 + 2 * a : 82 + 2 * a, :] = xs[a, 8:10, :]
    turned = xc[...].T
    fx_send[...] = turned[112:128]

    nodes = halves(xs[...].reshape(160, 128))

    def to_modes(g):
        zs[g] = dot3(nodes, (wh[g, 0:128], wl[g, 0:128])).reshape(10, 16, 128)

    def solve(g):
        value = zs[g].reshape(10, 2, 8, 128)
        total = None
        for a in range(10):
            term = cxb[g, a][:, None] * value[a][None]
            total = term if total is None else total + term
        value, total = total, None
        for b in range(10):
            row = value[:, b // 8, b % 8 : b % 8 + 1, :][:, None]
            pick = cm[g, OYF + 16 * b : OYF + 16 * b + 16, :].reshape(1, 2, 8, 128)
            term = pick * row
            total = term if total is None else total + term
        value, total = total * inv[g].reshape(10, 2, 8, 128), None
        for q in range(10):
            row = value[:, q // 8, q % 8 : q % 8 + 1, :][:, None]
            pick = cm[g, OYB + 16 * q : OYB + 16 * q + 16, :].reshape(1, 2, 8, 128)
            term = pick * row
            total = term if total is None else total + term
        value, total = total, None
        for p in range(10):
            term = cxb[g, :, p][:, None] * value[p][None]
            total = term if total is None else total + term
        return dot3(
            halves(total.reshape(160, 128)), (wh[g, 0:128], wl[g, 0:128]), ((1,), (1,))
        )

    to_modes(0)

    @pl.when(has_next & ~origin)
    def _():
        pl.semaphore_wait(ready, 1)

    send_up(0)
    send_up(1)
    found = solve(0)

    @pl.when(helper)
    def _():
        aside(False).wait_recv()
        aside(True).start()

    @pl.when(has_next)
    def _():
        far_copy(0, 1, True).wait_recv()

    @pl.when(has_prev)
    def _():
        far_copy(0, 0, True).wait_recv()

    prepare(1)
    to_modes(1)

    @pl.when(helper)
    def _():
        for k in HELD:
            piece(k, False, True).wait_recv()
            pass_piece(k).start()

    @pl.when(has_prev)
    def _():
        far_copy(1, 0, True).wait_recv()

    beyond = halves(fx_recv[...])

    more = dot3(beyond, (wh[1, 128:144], wl[1, 128:144]), ((0,), (0,)))
    zs[1, :, 0:8, :] = zs[1, :, 0:8, :] + more[0:80].reshape(10, 8, 128)
    for a in range(10):
        zs[1, a, 8:10, :] = zs[1, a, 8:10, :] + more[80 + 2 * a : 82 + 2 * a]

    for k in PIECES:
        @pl.when(over[k])
        def _(k=k):
            piece(k, True).wait_recv()

    def unpack(rows):
        return jnp.concatenate(
            [(pltpu.roll(rows, 128 - 16 * x, 1) if x else rows)[None] for x in range(8)], axis=0
        )

    own = unpack(slab_recv[...])
    sides = []
    for side in range(2):
        lines = []
        for j in range(2):
            line = jnp.broadcast_to(part_recv[side, j : j + 1, :], (8, 128))
            tile = jnp.where(row8 == 0, line, 0.0)
            for y in range(1, 8):
                tile = tile + jnp.where(row8 == y, pltpu.roll(line, 128 - 16 * y, 1), 0.0)
            lines.append(tile[None])
        sides.append(jnp.concatenate(lines, axis=0))
    for i in range(6):
        fan[2 * i : 2 * i + 2, :] = part_recv[2 + i]
    wide = unpack(fan[...])
    xf[:, 0:8, :] = join(own, sides[0], sides[1])
    before = join(wide[:, 0:2], wide[6:8, 4:6], wide[0:2, 8:10])
    behind = join(wide[:, 2:4], wide[6:8, 6:8], wide[0:2, 10:12])
    xf[:, 0:1, :] = xf[:, 0:1, :] + before[:, 1:2]
    xf[:, 7:8, :] = xf[:, 7:8, :] + behind[:, 0:1]
    xf[:, 8:9, :] = before[:, 0:1]
    xf[:, 9:10, :] = behind[:, 1:2]
    above = halves(xf[:, :, 0:16].reshape(160, 16))
    risen = dot3(above, (wh[1, 144:160], wl[1, 144:160])).reshape(10, 16, 128)

    zs[1] = zs[1] + risen
    found = (found + solve(1)).reshape(10, 16, 128)
    pack(1, found, (8, 0), (7, 9))
    send_near(1, near)

    for turn in range(2):
        for k in range(8):
            @pl.when(near[k])
            def _(turn=turn, k=k):
                outgoing(turn, k).wait_send()

    for kind in range(2):
        @pl.when(has_next)
        def _(kind=kind):
            far_copy(kind, 0, False).wait_send()

    @pl.when(below[8])
    def _():
        far_copy(0, 1, False).wait_send()

    @pl.when(after_origin)
    def _():
        aside(False).wait_send()

    @pl.when(helper)
    def _():
        aside(True).wait_send()
        for k in HELD:
            pass_piece(k).wait_send()

    for k in PIECES:
        @pl.when(under[k])
        def _(k=k):
            piece(k, False).wait_send()

    wait_near(1)

    def gather(own, prev, after):
        return jnp.concatenate([own[0:2] + prev, own[2:6], own[6:8] + after], axis=0)

    out_ref[...] = gather(found[0:8, 0:8], recv_x[1, 0], recv_x[1, 1])
    out_ref[:, 0:2, :] = out_ref[:, 0:2, :] + gather(recv_y[1, 0], recv_d[1, 0], recv_d[1, 2])
    out_ref[:, 6:8, :] = out_ref[:, 6:8, :] + gather(recv_y[1, 1], recv_d[1, 1], recv_d[1, 3])


def solution(mesh):
    nx, ny, nz = mesh.shape["gx"], mesh.shape["gy"], mesh.shape["gz"]

    def body(initial, source, metric, eigenvectors, eigenvalues):
        hbm = pl.BlockSpec(memory_space=pl.ANY)
        vmem = pltpu.VMEM
        correction = pl.pallas_call(
            functools.partial(kernel, nx, ny, nz),
            out_shape=vmem((8, 8, 128), F32),
            in_specs=[hbm] * 6,
            out_specs=pl.BlockSpec(memory_space=vmem),
            scratch_shapes=[
                vmem((8, 8, 128), F32),
                vmem((8, 8, 128), F32),
                vmem((3, 8, 8, 128), F32),
                vmem((2, 448, 128), BF16),
                vmem((10, 16, 16), F32),
                vmem((10, 16, 16), F32),
                vmem((10, 16, 16), F32),
                vmem((10, 24, 16), F32),
                vmem((3, 16, 16), F32),
                pltpu.SemaphoreType.DMA((33,)),
                vmem((2, 2, 2, 8, 128), F32),
                vmem((2, 2, 8, 2, 128), F32),
                vmem((2, 4, 2, 2, 128), F32),
                vmem((2, 2, 2, 8, 128), F32),
                vmem((2, 2, 8, 2, 128), F32),
                vmem((2, 4, 2, 2, 128), F32),
                pltpu.SemaphoreType.DMA((2, 8)),
                pltpu.SemaphoreType.DMA((2, 8)),
                vmem((2, 1, ROWS), F32),
                vmem((2, 1, ROWS), F32),
                vmem((16, 128), F32),
                vmem((16, 128), F32),
                pltpu.SemaphoreType.DMA((2, 2)),
                pltpu.SemaphoreType.DMA((2, 2)),
                pltpu.SemaphoreType.REGULAR,
                pltpu.SemaphoreType.REGULAR((8,)),
                vmem((1, ROWS), F32),
                pltpu.SemaphoreType.DMA,
                pltpu.SemaphoreType.DMA,
                vmem((8, 128), F32),
                vmem((8, 128), F32),
                vmem((8, 128), F32),
                vmem((2, 2, 128), F32),
                vmem((8, 2, 128), F32),
                vmem((3, 2, 128), F32),
                pltpu.SemaphoreType.DMA((9,)),
                pltpu.SemaphoreType.DMA((9,)),
                pltpu.SemaphoreType.DMA((4,)),
                pltpu.SemaphoreType.DMA((4,)),
                vmem((10, 16, 128), F32),
                vmem((16, 128), F32),
                vmem((10, 16, 128), F32),
                vmem((128, 128), F32),
                vmem((2, ROWS, 128), F32),
                vmem((2, 10, 10, 8, 128), F32),
                vmem((2, 10, 16, 128), F32),
                vmem((2, 160, 128), BF16),
                vmem((2, 160, 128), BF16),
                vmem((2, 10, 16, 128), F32),
            ],
            compiler_params=pltpu.CompilerParams(collective_id=0, has_side_effects=True),
        )(
            initial,
            source,
            metric,
            eigenvectors,
            eigenvalues,
            jnp.asarray(operator_tables()),
        )
        return initial + correction

    placed = (
        P("gx", "gy", "gz"),
        P("gx", "gy", "gz"),
        P(None, "gx", "gy", "gz"),
        P(None, None, None, "gx", "gy", "gz"),
        P(None, None, "gx", "gy", "gz"),
    )
    return jax.shard_map(
        body, mesh=mesh, in_specs=placed, out_specs=P("gx", "gy", "gz"), check_vma=False
    )
```
